512 devices in a mesh: row: 32 (over y, x), col: 16 (over z, core).
Axes of the slice: x: 4, y: 8, z: 8, core: 2. Of those that a mesh axis runs over, the one named last changes fastest.
Arguments:
- right_side: float32 [64, 16384], P(None, ('row', 'col')), may hold values from -6 to 6
- regular: float32 [16384], P(('row', 'col')), may hold values from 1 to 2
- curvature: bfloat16 [32, 32, 16, 128, 128], P('row', None, 'col'), as said below
- block_rows: int32 [32, 32, 16], P('row', None, 'col'), may hold values from 0 to 3, as said below
- block_cols: int32 [32, 32, 16], P('row', None, 'col'), may hold values from 0 to 3
- block_counts: int32 [32, 32, 16], P('row', None, 'col'), may hold values from 0 to 1, as said below
Outputs:
- solution: float32 [64, 16384], P(None, ('row', 'col'))
- residual: float32 [64, 16384], P(None, ('row', 'col'))
The draws below stay inside these ranges and needn't reach their ends.
Inputs may be any that keep to these rules, and one draw needn't show every extreme that they name: `block_rows`: the curvature is symmetric: a live term of owner r from source s with block row a and block column b is matched, in the same slot of owner s from source r, by block row b, block column a and the transposed block. `block_counts`: counts for the first index of col are always 1. A with this curvature and regular is symmetric positive definite.
All inputs are finite; a program needn't handle non-finite values.
Results may differ from the reference program's by a relative error of at most 0.0041.
Values may be sent and summed in bfloat16 or wider, within the bound.
No kernel may reach another device: no remote copies, remote signals or barrier semaphores. Data moves between devices by JAX's collectives and lax.ppermute only.
A program may use at most 64 MiB of HBM per device.

```python
import math
import jax
import jax.numpy as jnp
from jax import lax

RHS = 64
BLOCK = 128
NB_DEV = 4
M_DEV = 1
ITERS = 3
SOURCES = 32
COLS = 16
SLOTS = 16
NPIX = 16384


def pair_table():
    indices = jnp.arange(SOURCES, dtype=jnp.int32)
    low_end = jnp.minimum(indices[:, None], indices[None, :])
    high_end = jnp.maximum(indices[:, None], indices[None, :])
    return low_end * SOURCES + high_end


def order_masks():
    indices = jnp.arange(SOURCES, dtype=jnp.int32)
    is_before = indices[:, None] < indices[None, :]
    is_after = indices[:, None] > indices[None, :]
    return (is_before, is_after)


def pair_ints(key, salt_tag, out_shape, low_val, high_val):
    base_key = jax.random.fold_in(key, salt_tag)

    def draw_pair(pair_id):
        return jax.random.randint(jax.random.fold_in(base_key, pair_id), out_shape, low_val, high_val, dtype=jnp.int32)
    return jax.vmap(jax.vmap(draw_pair))(pair_table())


def pair_ids(key):
    first_ids = pair_ints(key, 11, (SLOTS,), 0, NB_DEV)
    offsets = pair_ints(key, 12, (SLOTS,), -2, 3)
    second_ids = (first_ids + offsets) % NB_DEV
    return (first_ids, second_ids)


def draw_block_rows(key, part):
    first_ids, second_ids = pair_ids(key)
    is_before, is_after = order_masks()
    return jnp.where(is_after[:, :, None], second_ids, first_ids)


def draw_block_cols(key, part):
    first_ids, second_ids = pair_ids(key)
    is_before, is_after = order_masks()
    return jnp.where(is_before[:, :, None], second_ids, first_ids)


def draw_block_counts(key, part):
    counted = pair_ints(key, 13, (COLS,), 0, M_DEV + 1)
    return counted.at[:, :, 0].set(M_DEV)


def draw_curvature(key, part):
    base_key = jax.random.fold_in(key, 14)
    pairs = pair_table()
    spread = 0.35 / math.sqrt(SOURCES * COLS * M_DEV * BLOCK / NB_DEV)

    def row_blocks(owner):

        def source_blocks(source):
            pair_key = jax.random.fold_in(base_key, pairs[owner, source])
            drawn_tile = jax.random.normal(pair_key, (SLOTS, BLOCK, BLOCK), jnp.float32)
            flipped = jnp.swapaxes(drawn_tile, 1, 2)
            symmetric = (drawn_tile + flipped) * 0.70710678
            chosen = jnp.where(owner < source, drawn_tile, jnp.where(owner > source, flipped, symmetric))
            return (chosen * spread).astype(jnp.bfloat16)
        return lax.map(source_blocks, jnp.arange(SOURCES, dtype=jnp.int32))
    return lax.map(row_blocks, jnp.arange(SOURCES, dtype=jnp.int32))


def block_scale(stream_key, extent, shards, least, high):
    def one(dim, parts):
        draws = jax.random.uniform(jax.random.fold_in(jax.random.fold_in(stream_key, 6), dim), (parts,), jnp.float32, least / len(shards), high / len(shards))
        return jnp.repeat(jnp.exp(draws), extent[dim] // parts).reshape((-1,) + (1,) * (len(extent) - dim - 1))

    loudness = one(*shards[0])
    for cut in shards[1:]:
        loudness = loudness * one(*cut)
    return loudness


def scatter_about(rng, shape, scale, reach, pieces=(), kind=jnp.bfloat16):
    values = jax.random.normal(rng, shape, jnp.float32) * scale
    if len(pieces) > 0:
        values = block_scale(rng, shape, pieces, -0.22, 0.18) * values
    return jnp.clip(values, min=-reach, max=reach).astype(kind)


def setup_inputs(seed: int = 0) -> dict:
    keys = jax.random.split(jax.random.key(seed), 7)
    right_side = scatter_about(keys[0], (RHS, NPIX), 1.0, 6.0, ((1, 512),), jnp.float32)
    regular = jnp.clip(1.0 + 1.0 * jax.random.uniform(keys[1], (NPIX,), jnp.float32) ** block_scale(keys[1], (NPIX,), ((0, 512),), -0.2, 0.2), 1.0, 2.0)
    curvature = draw_curvature(jax.random.fold_in(keys[6], 71), 0)
    block_rows = draw_block_rows(jax.random.fold_in(keys[6], 71), 0)
    block_cols = draw_block_cols(jax.random.fold_in(keys[6], 71), 0)
    block_counts = draw_block_counts(jax.random.fold_in(keys[6], 71), 0)
    return dict(right_side=right_side, regular=regular, curvature=curvature, block_rows=block_rows, block_cols=block_cols, block_counts=block_counts)


def chol_solve(matrix, rhs_mat):
    factor = jnp.linalg.cholesky(matrix)
    return jax.scipy.linalg.cho_solve((factor, True), rhs_mat)

def local_gram(left, right):
    return jnp.dot(left, right.T, precision=lax.Precision.HIGHEST)

def apply_operator(direction, regular, curvature, block_rows, block_cols, block_counts):
    dir_bf = direction.astype(jnp.bfloat16).reshape(RHS, SOURCES, NB_DEV, BLOCK)
    source_ids = jnp.arange(SOURCES, dtype=jnp.int32)
    slot_rank = jnp.arange(SLOTS, dtype=jnp.int32) % M_DEV
    block_ids = jnp.arange(NB_DEV, dtype=jnp.int32)

    def row_product(owner):
        curv_row = curvature[owner].astype(jnp.float32)
        rows_here = block_rows[owner]
        cols_here = block_cols[owner]
        counts_here = jnp.repeat(block_counts[owner], M_DEV, axis=1)
        chosen = dir_bf[:, source_ids[:, None], cols_here, :].astype(jnp.float32)
        products = jnp.einsum('xskq,skpq->xskp', chosen, curv_row, precision=lax.Precision.HIGHEST)
        live_slots = slot_rank[None, :] < counts_here
        row_table = ((rows_here[:, :, None] == block_ids[None, None, :]) & live_slots[:, :, None]).astype(jnp.float32)
        return jnp.einsum('xskp,skb->xbp', products, row_table, precision=lax.Precision.HIGHEST)
    coupled = lax.map(row_product, source_ids)
    coupled = jnp.transpose(coupled, (1, 0, 2, 3)).reshape(RHS, NPIX)
    return regular[None, :] * direction + coupled

def reference(right_side, regular, curvature, block_rows, block_cols, block_counts):
    solution = jnp.zeros_like(right_side)
    residual = right_side
    direction = right_side
    res_gram = local_gram(residual, residual)
    for iteration in range(ITERS):
        image = apply_operator(direction, regular, curvature, block_rows, block_cols, block_counts)
        curv_gram = local_gram(direction, image)
        curv_gram = 0.5 * (curv_gram + curv_gram.T)
        alpha_mat = chol_solve(curv_gram, res_gram)
        solution = solution + jnp.dot(alpha_mat.T, direction, precision=lax.Precision.HIGHEST)
        residual = residual - jnp.dot(alpha_mat.T, image, precision=lax.Precision.HIGHEST)
        if iteration + 1 < ITERS:
            new_gram = local_gram(residual, residual)
            beta_mat = chol_solve(res_gram, new_gram)
            direction = residual + jnp.dot(beta_mat.T, direction, precision=lax.Precision.HIGHEST)
            res_gram = new_gram
    return (solution, residual)
```

```python
import functools

import jax
import jax.numpy as jnp
from jax import lax
from jax.experimental import pallas as pl
from jax.experimental.pallas import tpu as pltpu
from jax.sharding import Mesh
from jax.sharding import PartitionSpec as P

ITERS = 3
COL = ("col_0", "col_1")
ROW = ("row_0", "row_1")
ROW_COL = ROW + COL
F32 = jnp.float32
BF16 = jnp.bfloat16
SMP = 64
LANE = 128
BLKS = 4
COLS = 16
PIECE = 32
NT = (((1,), (1,)), ((), ()))
NN = (((1,), (0,)), ((), ()))
VMEM = pl.BlockSpec(memory_space=pltpu.VMEM)
SMEM = pl.BlockSpec(memory_space=pltpu.SMEM)


def exact_dot(left, right, dims):
    return lax.dot_general(
        left, right, dims, precision=lax.Precision.HIGHEST, preferred_element_type=F32
    )


def swap(msg, axes):
    return lax.all_to_all(msg, axes, 0, 0, tiled=True)


def call(kernel, in_specs, outs, scratch, name):
    return pl.pallas_call(
        kernel,
        in_specs=in_specs,
        out_specs=[VMEM] * len(outs),
        out_shape=[jax.ShapeDtypeStruct(s, d) for s, d in outs],
        scratch_shapes=scratch,
        name=name,
    )


def pack_kernel(right_ref, reg_ref, out_ref):
    packed = jnp.concatenate([right_ref[16 * j : 16 * j + 16, :] for j in range(4)], axis=1)
    reg_row = jnp.concatenate([reg_ref[...], jnp.zeros((1, LANE - PIECE), F32)], axis=1)
    reg_tile = jnp.broadcast_to(reg_row, (8, LANE))
    for k in range(COLS):
        out_ref[k, 0:16, :] = packed
        out_ref[k, 16:24, :] = reg_tile


def emit_blocks(rows_ref, half_ref, sel_ref):
    for s in range(sel_ref.shape[0]):
        sel_ref[s] = half_ref[rows_ref[s]]


def unpack_kernel(rows_ref, got_ref, res_ref, reg_ref, sel_ref, half_ref):
    group = lax.broadcasted_iota(jnp.int32, (16, LANE), 1) // PIECE
    for b in range(BLKS):
        for j in range(4):
            piece = jnp.zeros((16, LANE), F32)
            for m in range(4):
                shift = (PIECE * (m - j)) % LANE
                part = got_ref[4 * b + m, 0:16, :]
                part = pltpu.roll(part, shift, 1) if shift else part
                piece = jnp.where(group == m, part, piece)
            res_ref[b, 16 * j : 16 * j + 16, :] = piece
            half_ref[b, 16 * j : 16 * j + 16, :] = piece.astype(BF16)
        reg = jnp.zeros((8, LANE), F32)
        for m in range(4):
            part = got_ref[4 * b + m, 16:24, :]
            part = pltpu.roll(part, PIECE * m, 1) if m else part
            reg = jnp.where(group[0:8] == m, part, reg)
        reg_ref[b] = reg
    emit_blocks(rows_ref, half_ref, sel_ref)


def product_kernel(first, *refs):
    rows_ref, counts_ref, chosen_ref, curv_ref, res_ref, reg_ref = refs[:6]
    if first:
        out_ref, acc_ref = refs[6:]
    else:
        img_ref, dir_ref, out_ref, acc_ref = refs[6:]
    acc_ref[...] = jnp.zeros_like(acc_ref)
    for s in range(chosen_ref.shape[0]):
        prod = lax.dot_general(chosen_ref[s], curv_ref[s], NT, preferred_element_type=F32)
        row = rows_ref[s]
        acc_ref[row] = acc_ref[row] + jnp.where(counts_ref[s] > 0, prod, 0.0)
    share = 1.0 / COLS
    pair = jnp.zeros((SMP, LANE), F32)
    mixed = jnp.zeros((SMP, SMP), F32)
    for b in range(BLKS):
        res = res_ref[b]
        part = acc_ref[b] + reg_ref[b, 0:1, :] * res * share
        pair += exact_dot(res, jnp.concatenate([part, res * share], axis=0), NT)
        if not first:
            mixed += exact_dot(res, img_ref[b] * share, NT) + exact_dot(part, dir_ref[b], NT)
    other = jnp.concatenate([mixed, jnp.zeros((SMP, LANE - SMP), F32)], axis=1)
    for k in range(COLS):
        m = k % 4
        out_ref[k, 0:16, :] = acc_ref[k // 4, 16 * m : 16 * m + 16, :]
        source = pair if k < 8 else other
        n = k % 8
        out_ref[k, 16:24, :] = source[8 * n : 8 * n + 8, :]


def col_sum_kernel(got_ref, gram_ref, piece_ref):
    total = got_ref[0]
    for k in range(1, COLS):
        total = total + got_ref[k]
    piece_ref[...] = total[0:16, :]
    gram = total[16:24, :]
    for r in range(gram_ref.shape[0]):
        gram_ref[r] = gram


def row_sum_kernel(got_ref, piece_ref, out_ref):
    total = got_ref[0]
    for r in range(1, got_ref.shape[0]):
        total = total + got_ref[r]
    piece = piece_ref[...]
    for k in range(COLS):
        out_ref[k, 0:16, :] = piece
        out_ref[k, 16:24, :] = total


def factor(matrices):
    row_id = lax.broadcasted_iota(jnp.int32, (8, LANE), 0)
    lane_id = lax.broadcasted_iota(jnp.int32, (SMP, SMP), 1)
    eye = (lax.broadcasted_iota(jnp.int32, (SMP, SMP), 0) == lane_id).astype(F32)
    work = []
    for matrix in matrices:
        wide = jnp.concatenate([matrix, eye], axis=1)
        work.append([wide[8 * t : 8 * t + 8, :] for t in range(8)])
    for j in range(SMP):
        top, low = divmod(j, 8)
        for tiles in work:
            pivot = tiles[top][low : low + 1, :]
            scaled = pivot / pivot[:, j : j + 1]
            for t in range(top, 8):
                column = tiles[t][:, j : j + 1]
                change = column * scaled
                if t == top:
                    if low == 7:
                        continue
                    change = jnp.where(row_id > low, change, 0.0)
                tiles[t] = tiles[t] - change
    done = []
    for tiles in work:
        wide = jnp.concatenate(tiles, axis=0)
        upper = wide[:, 0:SMP]
        inverse = pltpu.roll(wide, SMP, 1)[:, 0:SMP]
        diag = jnp.sum(upper * eye, axis=1, keepdims=True)
        done.append((inverse, inverse / diag))
    return done


def solve_kernel(first, last, *refs):
    refs = list(refs)
    rows_ref = refs.pop(0)
    got_ref, res_ref, reg_ref = refs[:3]
    refs = refs[3:]
    if not first:
        dir_ref, img_ref, sol_ref, inv_ref, scaled_ref, curv_ref = refs[:6]
        refs = refs[6:]
    if last:
        out_sol_ref, out_res_ref, keep_ref = refs
    else:
        new_res_ref, new_dir_ref, new_img_ref, new_sol_ref = refs[:4]
        new_inv_ref, new_scaled_ref, new_curv_ref, sel_ref, half_ref = refs[4:]
    pair = jnp.concatenate([got_ref[k, 16:24, :] for k in range(8)], axis=0)
    gram = pltpu.roll(pair, SMP, 1)[:, 0:SMP]
    curv = pair[:, 0:SMP]
    if not first:
        mixed = jnp.concatenate([got_ref[k, 16:24, :] for k in range(8, 16)], axis=0)[:, 0:SMP]
        beta_t = exact_dot(exact_dot(gram, inv_ref[...], NT), scaled_ref[...], NN)
        curv = curv + exact_dot(mixed + exact_dot(beta_t, curv_ref[...], NN), beta_t, NT)
    curv = 0.5 * (curv + curv.T)
    if last:
        ((inv_c, scaled_c),) = factor([curv])
    else:
        (inv_c, scaled_c), (inv_g, scaled_g) = factor([curv, gram])
        new_inv_ref[...] = inv_g
        new_scaled_ref[...] = scaled_g
        new_curv_ref[...] = curv
    alpha_t = exact_dot(exact_dot(gram, inv_c, NT), scaled_c, NN)
    for b in range(BLKS):
        res = res_ref[b]
        coupled = jnp.concatenate([got_ref[4 * b + m, 0:16, :] for m in range(4)], axis=0)
        image = coupled + reg_ref[b, 0:1, :] * res
        direction = res
        if not first:
            image = image + exact_dot(beta_t, img_ref[b], NN)
            direction = direction + exact_dot(beta_t, dir_ref[b], NN)
        new_res = res - exact_dot(alpha_t, image, NN)
        new_sol = exact_dot(alpha_t, direction, NN)
        if not first:
            new_sol = sol_ref[b] + new_sol
        if last:
            keep_ref[0, b] = new_sol
            keep_ref[1, b] = new_res
        else:
            new_res_ref[b] = new_res
            half_ref[b] = new_res.astype(BF16)
            new_dir_ref[b] = direction
            new_img_ref[b] = image
            new_sol_ref[b] = new_sol
    if last:
        mine = rows_ref[0]
        shift = (LANE - PIECE * (mine % 4)) % LANE
        out_sol_ref[...] = pltpu.roll(keep_ref[0, mine // 4], shift, 1)[:, 0:PIECE]
        out_res_ref[...] = pltpu.roll(keep_ref[1, mine // 4], shift, 1)[:, 0:PIECE]
    else:
        emit_blocks(rows_ref, half_ref, sel_ref)


def body(right_side, regular, curvature, block_rows, block_cols, block_counts):
    sources = block_rows.shape[1]
    curv = curvature.reshape(sources, LANE, LANE)
    rows = block_rows.reshape(sources)
    counts = block_counts.reshape(sources)
    field = ((BLKS, SMP, LANE), F32)
    small = ((SMP, SMP), F32)
    sel = ((sources, SMP, LANE), BF16)
    msg = ((COLS, 24, LANE), F32)
    half = pltpu.VMEM((BLKS, SMP, LANE), BF16)

    (packed,) = call(pack_kernel, [VMEM] * 2, [msg], [], "pack")(
        right_side, regular.reshape(1, PIECE)
    )
    res, reg, out = call(
        unpack_kernel, [SMEM, VMEM], [field, ((BLKS, 8, LANE), F32), sel], [half], "unpack"
    )(rows, swap(packed, COL))
    state = []
    for step in range(ITERS):
        first, last = step == 0, step == ITERS - 1
        chosen = swap(out, ROW)
        before = [] if first else [state[1], state[0]]
        (part,) = call(
            functools.partial(product_kernel, first),
            [SMEM, SMEM] + [VMEM] * (4 + len(before)),
            [msg],
            [pltpu.VMEM((BLKS, SMP, LANE), F32)],
            f"product_{step}",
        )(rows, counts, chosen, curv, res, reg, *before)
        gram, piece = call(
            col_sum_kernel,
            [VMEM],
            [((sources, 8, LANE), F32), ((16, LANE), F32)],
            [],
            f"col_sum_{step}",
        )(swap(part, COL))
        (whole,) = call(row_sum_kernel, [VMEM] * 2, [msg], [], f"row_sum_{step}")(
            swap(gram, ROW), piece
        )
        got = swap(whole, COL)
        specs = [SMEM] + [VMEM] * (3 + len(state))
        solve = functools.partial(solve_kernel, first, last)
        if last:
            mine = lax.axis_index(COL).astype(jnp.int32).reshape(1)
            share = ((SMP, PIECE), F32)
            keep = pltpu.VMEM((2, BLKS, SMP, LANE), F32)
            return tuple(
                call(solve, specs, [share, share], [keep], f"solve_{step}")(
                    mine, got, res, reg, *state
                )
            )
        outs = [field] * 4 + [small] * 3 + [sel]
        res, *state, out = call(solve, specs, outs, [half], f"solve_{step}")(
            rows, got, res, reg, *state
        )


def solution(mesh):
    finer = Mesh(mesh.devices.reshape(8, 4, 8, 2), ROW_COL)
    placed = (
        P(None, ROW_COL),
        P(ROW_COL),
        P(ROW, None, COL, None, None),
        P(ROW, None, COL),
        P(ROW, None, COL),
        P(ROW, None, COL),
    )
    return jax.shard_map(
        body,
        mesh=finer,
        in_specs=placed,
        out_specs=(P(None, ROW_COL), P(None, ROW_COL)),
        check_vma=False,
    )
```

```python
import functools

import jax
import jax.numpy as jnp
from jax import lax
from jax.experimental import pallas as pl
from jax.experimental.pallas import tpu as pltpu
from jax.sharding import Mesh
from jax.sharding import PartitionSpec as P

ITERS = 3
COL = ("col_0", "col_1")
ROW = ("row_0", "row_1")
ROW_COL = ROW + COL
F32 = jnp.float32
BF16 = jnp.bfloat16
SMP = 64
LANE = 128
BLKS = 4
COLS = 16
PIECE = 32
NT = (((1,), (1,)), ((), ()))
NN = (((1,), (0,)), ((), ()))
VMEM = pl.BlockSpec(memory_space=pltpu.VMEM)
SMEM = pl.BlockSpec(memory_space=pltpu.SMEM)


def exact_dot(left, right, dims):
    return lax.dot_general(
        left, right, dims, precision=lax.Precision.HIGHEST, preferred_element_type=F32
    )


def swap(msg, axes):
    return lax.all_to_all(msg, axes, 0, 0, tiled=True)


def call(kernel, in_specs, outs, scratch, name, make=pltpu.VMEM):
    run = pl.pallas_call(
        kernel,
        in_specs=in_specs,
        out_specs=[VMEM] * len(outs),
        out_shape=[make(s, d) for s, d in outs],
        scratch_shapes=scratch,
        name=name,
    )

    def placed(*args):
        near = [
            pltpu.with_memory_space_constraint(arg, pltpu.VMEM) if spec is VMEM else arg
            for spec, arg in zip(in_specs, args, strict=True)
        ]
        return run(*near)

    return placed


def pack_kernel(right_ref, reg_ref, out_ref):
    right = right_ref[...].T
    packed = jnp.concatenate([right[16 * j : 16 * j + 16, :] for j in range(4)], axis=1)
    reg_row = jnp.concatenate([reg_ref[...], jnp.zeros((1, LANE - PIECE), F32)], axis=1)
    reg_tile = jnp.broadcast_to(reg_row, (8, LANE))
    for k in range(COLS):
        out_ref[k, 0:16, :] = packed
        out_ref[k, 16:24, :] = reg_tile


def emit_blocks(rows_ref, half_ref, sel_ref):
    for s in range(sel_ref.shape[0]):
        sel_ref[s] = half_ref[rows_ref[s]]


def unpack_kernel(rows_ref, got_ref, res_ref, reg_ref, sel_ref, half_ref):
    group = lax.broadcasted_iota(jnp.int32, (16, LANE), 1) // PIECE
    for b in range(BLKS):
        for j in range(4):
            piece = jnp.zeros((16, LANE), F32)
            for m in range(4):
                shift = (PIECE * (m - j)) % LANE
                part = got_ref[4 * b + m, 0:16, :]
                part = pltpu.roll(part, shift, 1) if shift else part
                piece = jnp.where(group == m, part, piece)
            res_ref[b, 16 * j : 16 * j + 16, :] = piece
            half_ref[b, 16 * j : 16 * j + 16, :] = piece.astype(BF16)
        reg = jnp.zeros((8, LANE), F32)
        for m in range(4):
            part = got_ref[4 * b + m, 16:24, :]
            part = pltpu.roll(part, PIECE * m, 1) if m else part
            reg = jnp.where(group[0:8] == m, part, reg)
        reg_ref[b] = reg
    emit_blocks(rows_ref, half_ref, sel_ref)


def product_kernel(first, *refs):
    rows_ref, counts_ref, chosen_ref, curv_ref, res_ref, reg_ref = refs[:6]
    if first:
        out_ref, acc_ref = refs[6:]
    else:
        img_ref, dir_ref, out_ref, acc_ref = refs[6:]
    acc_ref[...] = jnp.zeros_like(acc_ref)
    for s in range(chosen_ref.shape[0]):
        prod = lax.dot_general(chosen_ref[s], curv_ref[s], NT, preferred_element_type=F32)
        row = rows_ref[s]
        acc_ref[row] = acc_ref[row] + jnp.where(counts_ref[s] > 0, prod, 0.0)
    share = 1.0 / COLS
    pair = jnp.zeros((SMP, LANE), F32)
    mixed = jnp.zeros((SMP, SMP), F32)
    for b in range(BLKS):
        res = res_ref[b]
        part = acc_ref[b] + reg_ref[b, 0:1, :] * res * share
        pair += exact_dot(res, jnp.concatenate([part, res * share], axis=0), NT)
        if not first:
            mixed += exact_dot(res, img_ref[b] * share, NT) + exact_dot(part, dir_ref[b], NT)
    other = jnp.concatenate([mixed, jnp.zeros((SMP, LANE - SMP), F32)], axis=1)
    for k in range(COLS):
        m = k % 4
        out_ref[k, 0:16, :] = acc_ref[k // 4, 16 * m : 16 * m + 16, :]
        source = pair if k < 8 else other
        n = k % 8
        out_ref[k, 16:24, :] = source[8 * n : 8 * n + 8, :]


def col_sum_kernel(got_ref, gram_ref, piece_ref):
    total = got_ref[0]
    for k in range(1, COLS):
        total = total + got_ref[k]
    piece_ref[...] = total[0:16, :]
    gram = total[16:24, :]
    for r in range(gram_ref.shape[0]):
        gram_ref[r] = gram


def row_sum_kernel(got_ref, piece_ref, out_ref):
    total = got_ref[0]
    for r in range(1, got_ref.shape[0]):
        total = total + got_ref[r]
    piece = piece_ref[...]
    for k in range(COLS):
        out_ref[k, 0:16, :] = piece
        out_ref[k, 16:24, :] = total


def factor(matrices):
    row_id = lax.broadcasted_iota(jnp.int32, (8, LANE), 0)
    lane_id = lax.broadcasted_iota(jnp.int32, (SMP, SMP), 1)
    eye = (lax.broadcasted_iota(jnp.int32, (SMP, SMP), 0) == lane_id).astype(F32)
    work = []
    for matrix in matrices:
        wide = jnp.concatenate([matrix, eye], axis=1)
        work.append([wide[8 * t : 8 * t + 8, :] for t in range(8)])
    for j in range(SMP):
        top, low = divmod(j, 8)
        for tiles in work:
            pivot = tiles[top][low : low + 1, :]
            scaled = pivot / pivot[:, j : j + 1]
            for t in range(top, 8):
                column = tiles[t][:, j : j + 1]
                change = column * scaled
                if t == top:
                    if low == 7:
                        continue
                    change = jnp.where(row_id > low, change, 0.0)
                tiles[t] = tiles[t] - change
    done = []
    for tiles in work:
        wide = jnp.concatenate(tiles, axis=0)
        upper = wide[:, 0:SMP]
        inverse = pltpu.roll(wide, SMP, 1)[:, 0:SMP]
        diag = jnp.sum(upper * eye, axis=1, keepdims=True)
        done.append((inverse, inverse / diag))
    return done


def solve_kernel(first, last, *refs):
    refs = list(refs)
    rows_ref = refs.pop(0)
    got_ref, res_ref, reg_ref = refs[:3]
    refs = refs[3:]
    if not first:
        dir_ref, img_ref, sol_ref, inv_ref, scaled_ref, curv_ref = refs[:6]
        refs = refs[6:]
    if last:
        out_sol_ref, out_res_ref, keep_ref = refs
    else:
        new_res_ref, new_dir_ref, new_img_ref, new_sol_ref = refs[:4]
        new_inv_ref, new_scaled_ref, new_curv_ref, sel_ref, half_ref = refs[4:]
    pair = jnp.concatenate([got_ref[k, 16:24, :] for k in range(8)], axis=0)
    gram = pltpu.roll(pair, SMP, 1)[:, 0:SMP]
    curv = pair[:, 0:SMP]
    if not first:
        mixed = jnp.concatenate([got_ref[k, 16:24, :] for k in range(8, 16)], axis=0)[:, 0:SMP]
        beta_t = exact_dot(exact_dot(gram, inv_ref[...], NT), scaled_ref[...], NN)
        curv = curv + exact_dot(mixed + exact_dot(beta_t, curv_ref[...], NN), beta_t, NT)
    curv = 0.5 * (curv + curv.T)
    if last:
        ((inv_c, scaled_c),) = factor([curv])
    else:
        (inv_c, scaled_c), (inv_g, scaled_g) = factor([curv, gram])
        new_inv_ref[...] = inv_g
        new_scaled_ref[...] = scaled_g
        new_curv_ref[...] = curv
    alpha_t = exact_dot(exact_dot(gram, inv_c, NT), scaled_c, NN)
    for b in range(BLKS):
        res = res_ref[b]
        coupled = jnp.concatenate([got_ref[4 * b + m, 0:16, :] for m in range(4)], axis=0)
        image = coupled + reg_ref[b, 0:1, :] * res
        direction = res
        if not first:
            image = image + exact_dot(beta_t, img_ref[b], NN)
            direction = direction + exact_dot(beta_t, dir_ref[b], NN)
        new_res = res - exact_dot(alpha_t, image, NN)
        new_sol = exact_dot(alpha_t, direction, NN)
        if not first:
            new_sol = sol_ref[b] + new_sol
        if last:
            keep_ref[0, b] = new_sol
            keep_ref[1, b] = new_res
        else:
            new_res_ref[b] = new_res
            half_ref[b] = new_res.astype(BF16)
            new_dir_ref[b] = direction
            new_img_ref[b] = image
            new_sol_ref[b] = new_sol
    if last:
        mine = rows_ref[0]
        shift = (LANE - PIECE * (mine % 4)) % LANE
        out_sol_ref[...] = pltpu.roll(keep_ref[0, mine // 4], shift, 1)[:, 0:PIECE].T
        out_res_ref[...] = pltpu.roll(keep_ref[1, mine // 4], shift, 1)[:, 0:PIECE].T
    else:
        emit_blocks(rows_ref, half_ref, sel_ref)


def body(right_side, regular, curvature, block_rows, block_cols, block_counts):
    sources = block_rows.shape[1]
    curv = curvature.reshape(sources, LANE, LANE)
    rows = block_rows.reshape(sources)
    counts = block_counts.reshape(sources)
    field = ((BLKS, SMP, LANE), F32)
    small = ((SMP, SMP), F32)
    sel = ((sources, SMP, LANE), BF16)
    msg = ((COLS, 24, LANE), F32)
    half = pltpu.VMEM((BLKS, SMP, LANE), BF16)

    (packed,) = call(pack_kernel, [VMEM] * 2, [msg], [], "pack")(
        right_side.T, regular.reshape(1, PIECE)
    )
    res, reg, out = call(
        unpack_kernel, [SMEM, VMEM], [field, ((BLKS, 8, LANE), F32), sel], [half], "unpack"
    )(rows, swap(packed, COL))
    state = []
    for step in range(ITERS):
        first, last = step == 0, step == ITERS - 1
        chosen = swap(out, ROW)
        before = [] if first else [state[1], state[0]]
        (part,) = call(
            functools.partial(product_kernel, first),
            [SMEM, SMEM] + [VMEM] * (4 + len(before)),
            [msg],
            [pltpu.VMEM((BLKS, SMP, LANE), F32)],
            f"product_{step}",
        )(rows, counts, chosen, curv, res, reg, *before)
        gram, piece = call(
            col_sum_kernel,
            [VMEM],
            [((sources, 8, LANE), F32), ((16, LANE), F32)],
            [],
            f"col_sum_{step}",
        )(swap(part, COL))
        (whole,) = call(row_sum_kernel, [VMEM] * 2, [msg], [], f"row_sum_{step}")(
            swap(gram, ROW), piece
        )
        got = swap(whole, COL)
        specs = [SMEM] + [VMEM] * (3 + len(state))
        solve = functools.partial(solve_kernel, first, last)
        if last:
            mine = lax.axis_index(COL).astype(jnp.int32).reshape(1)
            share = ((PIECE, SMP), F32)
            keep = pltpu.VMEM((2, BLKS, SMP, LANE), F32)
            shares = call(
                solve, specs, [share, share], [keep], f"solve_{step}", jax.ShapeDtypeStruct
            )(mine, got, res, reg, *state)
            return tuple(part.T for part in shares)
        outs = [field] * 4 + [small] * 3 + [sel]
        res, *state, out = call(solve, specs, outs, [half], f"solve_{step}")(
            rows, got, res, reg, *state
        )


def solution(mesh):
    finer = Mesh(mesh.devices.reshape(8, 4, 8, 2), ROW_COL)
    placed = (
        P(None, ROW_COL),
        P(ROW_COL),
        P(ROW, None, COL, None, None),
        P(ROW, None, COL),
        P(ROW, None, COL),
        P(ROW, None, COL),
    )
    return jax.shard_map(
        body,
        mesh=finer,
        in_specs=placed,
        out_specs=(P(None, ROW_COL), P(None, ROW_COL)),
        check_vma=False,
    )
```

```python
import functools

import jax
import jax.numpy as jnp
from jax import lax
from jax.experimental import pallas as pl
from jax.experimental.pallas import tpu as pltpu
from jax.sharding import Mesh
from jax.sharding import PartitionSpec as P

ITERS = 3
COL = ("col_0", "col_1")
ROW = ("row_0", "row_1")
ROW_COL = ROW + COL
F32 = jnp.float32
BF16 = jnp.bfloat16
SMP = 64
LANE = 128
BLKS = 4
COLS = 16
PIECE = 32
NT = (((1,), (1,)), ((), ()))
NN = (((1,), (0,)), ((), ()))
VMEM = pl.BlockSpec(memory_space=pltpu.VMEM)
SMEM = pl.BlockSpec(memory_space=pltpu.SMEM)


def exact_dot(left, right, dims):
    return lax.dot_general(
        left, right, dims, precision=lax.Precision.HIGHEST, preferred_element_type=F32
    )


def swap(msg, axes):
    return lax.all_to_all(msg, axes, 0, 0, tiled=True)


def call(kernel, in_specs, outs, scratch, name, make=pltpu.VMEM, near=True):
    run = pl.pallas_call(
        kernel,
        in_specs=in_specs,
        out_specs=[VMEM] * len(outs),
        out_shape=[make(s, d) for s, d in outs],
        scratch_shapes=scratch,
        name=name,
    )

    def placed(*args):
        if near:
            args = [
                pltpu.with_memory_space_constraint(arg, pltpu.VMEM) if spec is VMEM else arg
                for spec, arg in zip(in_specs, args, strict=True)
            ]
        return run(*args)

    return placed


def pack_kernel(right_ref, reg_ref, out_ref):
    right = right_ref[...].T
    packed = jnp.concatenate([right[16 * j : 16 * j + 16, :] for j in range(4)], axis=1)
    reg_row = jnp.concatenate([reg_ref[...], jnp.zeros((1, LANE - PIECE), F32)], axis=1)
    reg_tile = jnp.broadcast_to(reg_row, (8, LANE))
    for k in range(COLS):
        out_ref[k, 0:16, :] = packed
        out_ref[k, 16:24, :] = reg_tile


def emit_blocks(rows_ref, half_ref, sel_ref):
    for s in range(sel_ref.shape[0]):
        sel_ref[s] = half_ref[rows_ref[s]]


def unpack_kernel(rows_ref, got_ref, res_ref, reg_ref, sel_ref, half_ref):
    group = lax.broadcasted_iota(jnp.int32, (16, LANE), 1) // PIECE
    for b in range(BLKS):
        for j in range(4):
            piece = jnp.zeros((16, LANE), F32)
            for m in range(4):
                shift = (PIECE * (m - j)) % LANE
                part = got_ref[4 * b + m, 0:16, :]
                part = pltpu.roll(part, shift, 1) if shift else part
                piece = jnp.where(group == m, part, piece)
            res_ref[b, 16 * j : 16 * j + 16, :] = piece
            half_ref[b, 16 * j : 16 * j + 16, :] = piece.astype(BF16)
        reg = jnp.zeros((8, LANE), F32)
        for m in range(4):
            part = got_ref[4 * b + m, 16:24, :]
            part = pltpu.roll(part, PIECE * m, 1) if m else part
            reg = jnp.where(group[0:8] == m, part, reg)
        reg_ref[b] = reg
    emit_blocks(rows_ref, half_ref, sel_ref)


def product_kernel(first, *refs):
    rows_ref, counts_ref, chosen_ref, curv_ref, res_ref, reg_ref = refs[:6]
    if first:
        out_ref, acc_ref = refs[6:]
    else:
        img_ref, dir_ref, out_ref, acc_ref = refs[6:]
    acc_ref[...] = jnp.zeros_like(acc_ref)
    for s in range(chosen_ref.shape[0]):
        prod = lax.dot_general(chosen_ref[s], curv_ref[s], NT, preferred_element_type=F32)
        row = rows_ref[s]
        acc_ref[row] = acc_ref[row] + jnp.where(counts_ref[s] > 0, prod, 0.0)
    share = 1.0 / COLS
    pair = jnp.zeros((SMP, LANE), F32)
    mixed = jnp.zeros((SMP, SMP), F32)
    for b in range(BLKS):
        res = res_ref[b]
        part = acc_ref[b] + reg_ref[b, 0:1, :] * res * share
        pair += exact_dot(res, jnp.concatenate([part, res * share], axis=0), NT)
        if not first:
            mixed += exact_dot(res, img_ref[b] * share, NT) + exact_dot(part, dir_ref[b], NT)
    other = jnp.concatenate([mixed, jnp.zeros((SMP, LANE - SMP), F32)], axis=1)
    for k in range(COLS):
        m = k % 4
        out_ref[k, 0:16, :] = acc_ref[k // 4, 16 * m : 16 * m + 16, :]
        source = pair if k < 8 else other
        n = k % 8
        out_ref[k, 16:24, :] = source[8 * n : 8 * n + 8, :]


def col_sum_kernel(got_ref, gram_ref, piece_ref):
    total = got_ref[0]
    for k in range(1, COLS):
        total = total + got_ref[k]
    piece_ref[...] = total[0:16, :]
    gram = total[16:24, :]
    for r in range(gram_ref.shape[0]):
        gram_ref[r] = gram


def row_sum_kernel(got_ref, piece_ref, out_ref):
    total = got_ref[0]
    for r in range(1, got_ref.shape[0]):
        total = total + got_ref[r]
    piece = piece_ref[...]
    for k in range(COLS):
        out_ref[k, 0:16, :] = piece
        out_ref[k, 16:24, :] = total


def solve_systems(systems, width):
    row_id = lax.broadcasted_iota(jnp.int32, (8, LANE), 0)
    work = []
    for matrix, rhs in systems:
        wide = jnp.concatenate([matrix, rhs], axis=1)
        work.append([wide[8 * t : 8 * t + 8, :] for t in range(8)])
    for j in range(0, SMP, width):
        top, low = divmod(j, 8)
        for tiles in work:
            columns = [
                [
                    jnp.broadcast_to(tile[:, j + i : j + i + 1], (8, LANE))
                    for i in range(width)
                ]
                for tile in tiles
            ]
            rows = [tiles[top][low + i : low + i + 1, :] for i in range(width)]
            block = [
                [columns[top][c][low + r : low + r + 1, :] for c in range(width)]
                for r in range(width)
            ]
            recip, lower = [], {}
            for a in range(width):
                recip.append(1.0 / block[a][a])
                for r in range(a + 1, width):
                    lower[r, a] = block[r][a] * recip[a]
                    rows[r] = rows[r] - lower[r, a] * rows[a]
                    for c in range(a + 1, width):
                        block[r][c] = block[r][c] - lower[r, a] * block[a][c]
            for a in reversed(range(width)):
                rows[a] = rows[a] * recip[a]
                for r in range(a + 1, width):
                    rows[a] = rows[a] - lower[r, a] * rows[r]
            for t in range(8):
                tile = tiles[t]
                for i in range(width):
                    tile = tile - columns[t][i] * rows[i]
                if t == top:
                    for i in range(width):
                        tile = jnp.where(row_id == low + i, rows[i], tile)
                tiles[t] = tile
    return [pltpu.roll(jnp.concatenate(tiles, axis=0), SMP, 1)[:, 0:SMP] for tiles in work]


def solve_kernel(first, last, *refs):
    refs = list(refs)
    rows_ref = refs.pop(0)
    got_ref, res_ref, reg_ref = refs[:3]
    refs = refs[3:]
    if not first:
        dir_ref, img_ref, sol_ref, inv_ref, curv_ref = refs[:5]
        refs = refs[5:]
    if last:
        out_sol_ref, out_res_ref, keep_ref = refs
    else:
        new_res_ref, new_dir_ref, new_img_ref, new_sol_ref = refs[:4]
        new_inv_ref, new_curv_ref, sel_ref, half_ref = refs[4:]
    pair = jnp.concatenate([got_ref[k, 16:24, :] for k in range(8)], axis=0)
    gram = pltpu.roll(pair, SMP, 1)[:, 0:SMP]
    curv = pair[:, 0:SMP]
    if not first:
        mixed = jnp.concatenate([got_ref[k, 16:24, :] for k in range(8, 16)], axis=0)[:, 0:SMP]
        beta_t = exact_dot(gram, inv_ref[...], NN)
        curv = curv + exact_dot(mixed + exact_dot(beta_t, curv_ref[...], NN), beta_t, NT)
    curv = 0.5 * (curv + curv.T)
    if last:
        (alpha,) = solve_systems([(curv, gram)], 8)
    else:
        square = (SMP, SMP)
        same = lax.broadcasted_iota(jnp.int32, square, 0) == lax.broadcasted_iota(
            jnp.int32, square, 1
        )
        alpha, inverse = solve_systems([(curv, gram), (gram, same.astype(F32))], 4)
        new_inv_ref[...] = inverse
        new_curv_ref[...] = curv
    alpha_t = alpha.T
    for b in range(BLKS):
        res = res_ref[b]
        coupled = jnp.concatenate([got_ref[4 * b + m, 0:16, :] for m in range(4)], axis=0)
        image = coupled + reg_ref[b, 0:1, :] * res
        direction = res
        if not first:
            image = image + exact_dot(beta_t, img_ref[b], NN)
            direction = direction + exact_dot(beta_t, dir_ref[b], NN)
        new_res = res - exact_dot(alpha_t, image, NN)
        new_sol = exact_dot(alpha_t, direction, NN)
        if not first:
            new_sol = sol_ref[b] + new_sol
        if last:
            keep_ref[0, b] = new_sol
            keep_ref[1, b] = new_res
        else:
            new_res_ref[b] = new_res
            half_ref[b] = new_res.astype(BF16)
            new_dir_ref[b] = direction
            new_img_ref[b] = image
            new_sol_ref[b] = new_sol
    if last:
        mine = rows_ref[0]
        shift = (LANE - PIECE * (mine % 4)) % LANE
        out_sol_ref[...] = pltpu.roll(keep_ref[0, mine // 4], shift, 1)[:, 0:PIECE].T
        out_res_ref[...] = pltpu.roll(keep_ref[1, mine // 4], shift, 1)[:, 0:PIECE].T
    else:
        emit_blocks(rows_ref, half_ref, sel_ref)


def body(right_side, regular, curvature, block_rows, block_cols, block_counts):
    sources = block_rows.shape[1]
    curv = curvature.reshape(sources, LANE, LANE)
    rows = block_rows.reshape(sources)
    counts = block_counts.reshape(sources)
    field = ((BLKS, SMP, LANE), F32)
    small = ((SMP, SMP), F32)
    sel = ((sources, SMP, LANE), BF16)
    msg = ((COLS, 24, LANE), F32)
    half = pltpu.VMEM((BLKS, SMP, LANE), BF16)

    (packed,) = call(pack_kernel, [VMEM] * 2, [msg], [], "pack", near=False)(
        right_side.T, regular.reshape(1, PIECE)
    )
    mine = lax.axis_index(COL).astype(jnp.int32).reshape(1)
    packed, mine = lax.optimization_barrier((packed, mine))
    res, reg, out = call(
        unpack_kernel, [SMEM, VMEM], [field, ((BLKS, 8, LANE), F32), sel], [half], "unpack"
    )(rows, swap(packed, COL))
    state = []
    for step in range(ITERS):
        first, last = step == 0, step == ITERS - 1
        chosen = swap(out, ROW)
        before = [] if first else [state[1], state[0]]
        (part,) = call(
            functools.partial(product_kernel, first),
            [SMEM, SMEM] + [VMEM] * (4 + len(before)),
            [msg],
            [pltpu.VMEM((BLKS, SMP, LANE), F32)],
            f"product_{step}",
        )(rows, counts, chosen, curv, res, reg, *before)
        gram, piece = call(
            col_sum_kernel,
            [VMEM],
            [((sources, 8, LANE), F32), ((16, LANE), F32)],
            [],
            f"col_sum_{step}",
        )(swap(part, COL))
        (whole,) = call(row_sum_kernel, [VMEM] * 2, [msg], [], f"row_sum_{step}")(
            swap(gram, ROW), piece
        )
        got = swap(whole, COL)
        specs = [SMEM] + [VMEM] * (3 + len(state))
        solve = functools.partial(solve_kernel, first, last)
        if last:
            share = ((PIECE, SMP), F32)
            keep = pltpu.VMEM((2, BLKS, SMP, LANE), F32)
            shares = call(
                solve, specs, [share, share], [keep], f"solve_{step}", jax.ShapeDtypeStruct
            )(mine, got, res, reg, *state)
            return tuple(part.T for part in shares)
        outs = [field] * 4 + [small] * 2 + [sel]
        res, *state, out = call(solve, specs, outs, [half], f"solve_{step}")(
            rows, got, res, reg, *state
        )


def solution(mesh):
    finer = Mesh(mesh.devices.reshape(8, 4, 8, 2), ROW_COL)
    placed = (
        P(None, ROW_COL),
        P(ROW_COL),
        P(ROW, None, COL, None, None),
        P(ROW, None, COL),
        P(ROW, None, COL),
        P(ROW, None, COL),
    )
    return jax.shard_map(
        body,
        mesh=finer,
        in_specs=placed,
        out_specs=(P(None, ROW_COL), P(None, ROW_COL)),
        check_vma=False,
    )
```

```python
import functools

import jax
import jax.numpy as jnp
from jax import lax
from jax.experimental import pallas as pl
from jax.experimental.pallas import tpu as pltpu
from jax.sharding import Mesh
from jax.sharding import PartitionSpec as P

ITERS = 3
COL = ("col_0", "col_1")
ROW = ("row_0", "row_1")
ROW_COL = ROW + COL
F32 = jnp.float32
BF16 = jnp.bfloat16
SMP = 64
LANE = 128
BLKS = 4
COLS = 16
PIECE = 32
STRIP = 8
OWN = 2 * STRIP
NT = (((1,), (1,)), ((), ()))
NN = (((1,), (0,)), ((), ()))
VMEM = pl.BlockSpec(memory_space=pltpu.VMEM)
SMEM = pl.BlockSpec(memory_space=pltpu.SMEM)


def exact_dot(left, right, dims):
    return lax.dot_general(
        left, right, dims, precision=lax.Precision.HIGHEST, preferred_element_type=F32
    )


def swap(msg, axes):
    return lax.all_to_all(msg, axes, 0, 0, tiled=True)


def call(kernel, in_specs, outs, scratch, name, make=pltpu.VMEM, near=True):
    run = pl.pallas_call(
        kernel,
        in_specs=in_specs,
        out_specs=[VMEM] * len(outs),
        out_shape=[make(s, d) for s, d in outs],
        scratch_shapes=scratch,
        name=name,
    )

    def placed(*args):
        if near:
            args = [
                pltpu.with_memory_space_constraint(arg, pltpu.VMEM) if spec is VMEM else arg
                for spec, arg in zip(in_specs, args, strict=True)
            ]
        return run(*args)

    return placed


def thirds(value):
    high = value.astype(BF16).astype(F32)
    middle = (value - high).astype(BF16).astype(F32)
    return high, middle, value - high - middle


def pack_kernel(right_ref, reg_ref, rows_ref, cols_ref, counts_ref, curv_ref, out_ref):
    sources = curv_ref.shape[0]
    base = STRIP * sources
    for s in range(sources):
        flipped = curv_ref[s].astype(F32).T
        for k in range(COLS):
            strip = flipped[STRIP * k : STRIP * k + STRIP, :].astype(BF16)
            out_ref[k, STRIP * s : STRIP * s + STRIP, :] = strip
    right = right_ref[...].T
    packed = jnp.concatenate([right[16 * j : 16 * j + 16, :] for j in range(4)], axis=1)
    cols = cols_ref[...]
    place = ((cols // 2) * BLKS + rows_ref[...]) * 2 + cols % 2
    place = jnp.where(counts_ref[...] > 0, place, -1).astype(F32)
    lines = [*thirds(reg_ref[...]), place]
    lines.append(jnp.zeros((16 - len(lines), PIECE), F32))
    notes = jnp.concatenate(lines, axis=0)
    notes = jnp.concatenate([notes, jnp.zeros((16, LANE - PIECE), F32)], axis=1)
    tiles = [tile.astype(BF16) for tile in (*thirds(packed), notes)]
    for k in range(COLS):
        for i, tile in enumerate(tiles):
            out_ref[k, base + 16 * i : base + 16 * i + 16, :] = tile


def pixel_rows(fields):
    return [jnp.concatenate([fields[b].T, fields[2 + b].T], axis=1) for b in range(2)]


def unpack_kernel(place_ref, got_ref, res_ref, reg_ref, own_ref, own_reg_ref, out_ref, tall_ref):
    base = got_ref.shape[1] - 4 * 16
    packed, notes = [], []
    for k in range(COLS):
        parts = [got_ref[k, base + 16 * i : base + 16 * i + 16, :].astype(F32) for i in range(4)]
        packed.append(parts[0] + parts[1] + parts[2])
        note = parts[3]
        notes.append(note[0:1] + note[1:2] + note[2:3])
    group = lax.broadcasted_iota(jnp.int32, (16, LANE), 1) // PIECE
    fields, regs = [], []
    for b in range(BLKS):
        pieces = []
        for j in range(4):
            piece = jnp.zeros((16, LANE), F32)
            for m in range(4):
                shift = (PIECE * (m - j)) % LANE
                part = packed[4 * b + m]
                part = pltpu.roll(part, shift, 1) if shift else part
                piece = jnp.where(group == m, part, piece)
            pieces.append(piece)
        fields.append(jnp.concatenate(pieces, axis=0))
        reg = jnp.zeros((8, LANE), F32)
        for m in range(4):
            part = jnp.broadcast_to(notes[4 * b + m], (8, LANE))
            part = pltpu.roll(part, PIECE * m, 1) if m else part
            reg = jnp.where(group[0:8] == m, part, reg)
        regs.append(jnp.broadcast_to(reg[0:1], (SMP, LANE)))
        res_ref[b] = fields[b]
        reg_ref[b] = reg
    start = pl.multiple_of(place_ref[0] * STRIP, STRIP)
    for target, values in ((own_ref, fields), (own_reg_ref, regs)):
        for b, tall in enumerate(pixel_rows(values)):
            tall_ref[b] = tall
            target[STRIP * b : STRIP * b + STRIP, :] = tall_ref[b, pl.ds(start, STRIP), :]
    own = own_ref[...]
    for r in range(out_ref.shape[0]):
        out_ref[r] = own


def dense_kernel(place_ref, got_ref, high_ref, low_ref, sum_ref):
    sources = place_ref.shape[1]
    sum_ref[...] = jnp.zeros_like(sum_ref)
    for s in range(sources):
        for k in range(COLS):
            place = place_ref[k, s]
            strip = got_ref[k, STRIP * s : STRIP * s + STRIP, :].astype(F32)
            strip = jnp.where(place >= 0, strip, 0.0)
            spot = jnp.maximum(place, 0)
            plane = spot // 2
            rows = pl.ds(pl.multiple_of(OWN * s + STRIP * (spot % 2), STRIP), STRIP)
            sum_ref[plane, rows, :] = sum_ref[plane, rows, :] + strip
    for plane in range(2 * BLKS):
        total = sum_ref[plane]
        high = total.astype(BF16)
        high_ref[plane] = high
        low_ref[plane] = (total - high.astype(F32)).astype(BF16)


def product_kernel(first, *refs):
    spread_ref, high_ref, low_ref, res_ref, reg_ref = refs[:5]
    if first:
        (out_ref,) = refs[5:]
    else:
        img_ref, dir_ref, out_ref = refs[5:]
    pixels = OWN * spread_ref.shape[0]
    spread = spread_ref[...].reshape(pixels, LANE)
    inputs = jnp.concatenate(
        [spread[LANE * i : LANE * i + LANE, :].T for i in range(pixels // LANE)], axis=1
    ).astype(BF16)
    share = 1.0 / COLS
    pair = jnp.zeros((SMP, LANE), F32)
    mixed = jnp.zeros((SMP, SMP), F32)
    coupled = []
    for b in range(BLKS):
        acc = jnp.zeros((SMP, LANE), F32)
        for half in range(2):
            left = inputs[SMP * half : SMP * half + SMP, :]
            for weights in (high_ref, low_ref):
                acc += lax.dot_general(
                    left, weights[BLKS * half + b], NN, preferred_element_type=F32
                )
        coupled.append(acc)
        res = res_ref[b]
        part = acc + reg_ref[b, 0:1, :] * res * share
        pair += exact_dot(res, jnp.concatenate([part, res * share], axis=0), NT)
        if not first:
            mixed += exact_dot(res, img_ref[b] * share, NT) + exact_dot(part, dir_ref[b], NT)
    other = jnp.concatenate([mixed, jnp.zeros((SMP, LANE - SMP), F32)], axis=1)
    tall = pixel_rows(coupled)
    for k in range(COLS):
        for b in range(2):
            out_ref[k, STRIP * b : STRIP * b + STRIP, :] = tall[b][STRIP * k : STRIP * k + STRIP]
        source = pair if k < 8 else other
        n = k % 8
        out_ref[k, OWN : OWN + 8, :] = source[8 * n : 8 * n + 8, :]


def col_sum_kernel(last, got_ref, own_ref, own_reg_ref, out_ref, piece_ref):
    total = got_ref[0]
    for k in range(1, COLS):
        total = total + got_ref[k]
    coupled = total[0:OWN, :]
    piece_ref[...] = coupled
    gram = total[OWN : OWN + 8, :]
    full = coupled + own_reg_ref[...] * own_ref[...]
    for r in range(out_ref.shape[0]):
        if last:
            out_ref[r] = gram
        else:
            out_ref[r, 0:OWN, :] = full
            out_ref[r, OWN : OWN + 8, :] = gram


def row_sum_kernel(got_ref, piece_ref, out_ref):
    top = got_ref.shape[1] - 8
    total = got_ref[0, top:, :]
    for r in range(1, got_ref.shape[0]):
        total = total + got_ref[r, top:, :]
    piece = piece_ref[...]
    for k in range(COLS):
        out_ref[k, 0:OWN, :] = piece
        out_ref[k, OWN : OWN + 8, :] = total


def solve_systems(systems, width):
    row_id = lax.broadcasted_iota(jnp.int32, (8, LANE), 0)
    work = []
    for matrix, rhs in systems:
        wide = jnp.concatenate([matrix, rhs], axis=1)
        work.append([wide[8 * t : 8 * t + 8, :] for t in range(8)])
    for j in range(0, SMP, width):
        top, low = divmod(j, 8)
        for tiles in work:
            columns = [
                [
                    jnp.broadcast_to(tile[:, j + i : j + i + 1], (8, LANE))
                    for i in range(width)
                ]
                for tile in tiles
            ]
            rows = [tiles[top][low + i : low + i + 1, :] for i in range(width)]
            block = [
                [columns[top][c][low + r : low + r + 1, :] for c in range(width)]
                for r in range(width)
            ]
            recip, lower = [], {}
            for a in range(width):
                recip.append(1.0 / block[a][a])
                for r in range(a + 1, width):
                    lower[r, a] = block[r][a] * recip[a]
                    rows[r] = rows[r] - lower[r, a] * rows[a]
                    for c in range(a + 1, width):
                        block[r][c] = block[r][c] - lower[r, a] * block[a][c]
            for a in reversed(range(width)):
                rows[a] = rows[a] * recip[a]
                for r in range(a + 1, width):
                    rows[a] = rows[a] - lower[r, a] * rows[r]
            for t in range(8):
                tile = tiles[t]
                for i in range(width):
                    tile = tile - columns[t][i] * rows[i]
                if t == top:
                    for i in range(width):
                        tile = jnp.where(row_id == low + i, rows[i], tile)
                tiles[t] = tile
    return [pltpu.roll(jnp.concatenate(tiles, axis=0), SMP, 1)[:, 0:SMP] for tiles in work]


def both_halves(matrix):
    zero = jnp.zeros((SMP, SMP), F32)
    upper = jnp.concatenate([matrix, zero], axis=1)
    lower = jnp.concatenate([zero, matrix], axis=1)
    return jnp.concatenate([upper, lower], axis=0)


def solve_kernel(first, last, *refs):
    refs = list(refs)
    place_ref, got_ref, res_ref, reg_ref = refs[:4]
    refs = refs[4:]
    if not first:
        dir_ref, img_ref, sol_ref, inv_ref, curv_ref = refs[:5]
        refs = refs[5:]
    if last:
        out_sol_ref, out_res_ref, keep_ref = refs
    else:
        spread_ref, fresh_ref = refs[:2]
        refs = refs[2:]
        if not first:
            spread_img_ref = refs.pop(0)
        new_res_ref, new_dir_ref, new_img_ref, new_sol_ref = refs[:4]
        new_inv_ref, new_curv_ref, new_spread_ref, new_spread_img_ref, own_ref = refs[4:]
    pair = jnp.concatenate([got_ref[k, OWN : OWN + 8, :] for k in range(8)], axis=0)
    gram = pltpu.roll(pair, SMP, 1)[:, 0:SMP]
    curv = pair[:, 0:SMP]
    if not first:
        mixed = jnp.concatenate([got_ref[k, OWN : OWN + 8, :] for k in range(8, 16)], axis=0)
        mixed = mixed[:, 0:SMP]
        beta_t = exact_dot(gram, inv_ref[...], NN)
        curv = curv + exact_dot(mixed + exact_dot(beta_t, curv_ref[...], NN), beta_t, NT)
    curv = 0.5 * (curv + curv.T)
    if last:
        (alpha,) = solve_systems([(curv, gram)], 8)
    else:
        square = (SMP, SMP)
        same = lax.broadcasted_iota(jnp.int32, square, 0) == lax.broadcasted_iota(
            jnp.int32, square, 1
        )
        alpha, inverse = solve_systems([(curv, gram), (gram, same.astype(F32))], 4)
        new_inv_ref[...] = inverse
        new_curv_ref[...] = curv
        sources = spread_ref.shape[0]
        pixels = OWN * sources
        spread_img = fresh_ref[:, 0:OWN, :].reshape(pixels, LANE)
        if not first:
            old = spread_img_ref[...].reshape(pixels, LANE)
            spread_img = spread_img + exact_dot(old, both_halves(beta_t.T), NN)
        spread = spread_ref[...].reshape(pixels, LANE)
        spread = spread - exact_dot(spread_img, both_halves(alpha), NN)
        new_spread_ref[...] = spread.reshape(sources, OWN, LANE)
        new_spread_img_ref[...] = spread_img.reshape(sources, OWN, LANE)
        own_ref[...] = new_spread_ref[place_ref[1]]
    alpha_t = alpha.T
    wide = [
        jnp.concatenate(
            [got_ref[k, STRIP * b : STRIP * b + STRIP, :] for k in range(COLS)], axis=0
        ).T
        for b in range(2)
    ]
    for b in range(BLKS):
        res = res_ref[b]
        half = SMP * (b // 2)
        image = wide[b % 2][half : half + SMP, :] + reg_ref[b, 0:1, :] * res
        direction = res
        if not first:
            image = image + exact_dot(beta_t, img_ref[b], NN)
            direction = direction + exact_dot(beta_t, dir_ref[b], NN)
        new_res = res - exact_dot(alpha_t, image, NN)
        new_sol = exact_dot(alpha_t, direction, NN)
        if not first:
            new_sol = sol_ref[b] + new_sol
        if last:
            keep_ref[0, b] = new_sol
            keep_ref[1, b] = new_res
        else:
            new_res_ref[b] = new_res
            new_dir_ref[b] = direction
            new_img_ref[b] = image
            new_sol_ref[b] = new_sol
    if last:
        mine = place_ref[0]
        shift = (LANE - PIECE * (mine % 4)) % LANE
        out_sol_ref[...] = pltpu.roll(keep_ref[0, mine // 4], shift, 1)[:, 0:PIECE].T
        out_res_ref[...] = pltpu.roll(keep_ref[1, mine // 4], shift, 1)[:, 0:PIECE].T


def body(right_side, regular, curvature, block_rows, block_cols, block_counts):
    sources = block_rows.shape[1]
    pixels = OWN * sources
    curv = curvature.reshape(sources, LANE, LANE)
    tables = [table.reshape(1, sources) for table in (block_rows, block_cols, block_counts)]
    field = ((BLKS, SMP, LANE), F32)
    small = ((SMP, SMP), F32)
    own_share = ((OWN, LANE), F32)
    spread_share = ((sources, OWN, LANE), F32)
    msg = ((COLS, OWN + 8, LANE), F32)
    start = ((COLS, STRIP * sources + 64, LANE), BF16)
    dense = ((2 * BLKS, pixels, LANE), BF16)

    (packed,) = call(pack_kernel, [VMEM] * 6, [start], [], "pack", near=False)(
        right_side.T, regular.reshape(1, PIECE), *tables, curv
    )
    here = jnp.stack([lax.axis_index(COL), lax.axis_index(ROW)]).astype(jnp.int32)
    packed, here = lax.optimization_barrier((packed, here))
    packed = swap(packed, COL)
    res, reg, own, own_reg, out = call(
        unpack_kernel,
        [SMEM, VMEM],
        [field, ((BLKS, 8, LANE), F32), own_share, own_share, spread_share],
        [pltpu.VMEM((2, LANE, LANE), F32)],
        "unpack",
    )(here, packed)
    spread = swap(out, ROW)
    places = packed[:, STRIP * sources + 51, 0:sources].astype(jnp.int32)
    high, low = call(
        dense_kernel,
        [SMEM, VMEM],
        [dense, dense],
        [pltpu.VMEM(dense[0], F32)],
        "dense",
    )(places, packed)
    state, spread_img = [], []
    for step in range(ITERS):
        first, last = step == 0, step == ITERS - 1
        before = [] if first else [state[1], state[0]]
        (part,) = call(
            functools.partial(product_kernel, first),
            [VMEM] * (5 + len(before)),
            [msg],
            [],
            f"product_{step}",
        )(spread, high, low, res, reg, *before)
        out, piece = call(
            functools.partial(col_sum_kernel, last),
            [VMEM] * 3,
            [((sources, 8 if last else OWN + 8, LANE), F32), own_share],
            [],
            f"col_sum_{step}",
        )(swap(part, COL), own, own_reg)
        fresh = swap(out, ROW)
        (whole,) = call(row_sum_kernel, [VMEM] * 2, [msg], [], f"row_sum_{step}")(fresh, piece)
        got = swap(whole, COL)
        solve = functools.partial(solve_kernel, first, last)
        if last:
            share = ((PIECE, SMP), F32)
            keep = pltpu.VMEM((2, BLKS, SMP, LANE), F32)
            shares = call(
                solve,
                [SMEM] + [VMEM] * (3 + len(state)),
                [share, share],
                [keep],
                f"solve_{step}",
                jax.ShapeDtypeStruct,
            )(here, got, res, reg, *state)
            return tuple(part.T for part in shares)
        inputs = [got, res, reg, *state, spread, fresh, *spread_img]
        outs = [field] * 4 + [small] * 2 + [spread_share] * 2 + [own_share]
        res, *state, spread, img, own = call(
            solve, [SMEM] + [VMEM] * len(inputs), outs, [], f"solve_{step}"
        )(here, *inputs)
        spread_img = [img]


def solution(mesh):
    finer = Mesh(mesh.devices.reshape(8, 4, 8, 2), ROW_COL)
    placed = (
        P(None, ROW_COL),
        P(ROW_COL),
        P(ROW, None, COL, None, None),
        P(ROW, None, COL),
        P(ROW, None, COL),
        P(ROW, None, COL),
    )
    return jax.shard_map(
        body,
        mesh=finer,
        in_specs=placed,
        out_specs=(P(None, ROW_COL), P(None, ROW_COL)),
        check_vma=False,
    )
```

```python
import functools

import jax
import jax.numpy as jnp
from jax import lax
from jax.experimental import pallas as pl
from jax.experimental.pallas import tpu as pltpu
from jax.sharding import Mesh
from jax.sharding import PartitionSpec as P

ITERS = 3
COL = ("col_0", "col_1")
ROW = ("row_0", "row_1")
ROW_COL = ROW + COL
F32 = jnp.float32
BF16 = jnp.bfloat16
SMP = 64
LANE = 128
BLKS = 4
COLS = 16
PIECE = 32
STRIP = 8
OWN = 2 * STRIP
GRANT = 16 * 2**20
NOTES = 56
NT = (((1,), (1,)), ((), ()))
NN = (((1,), (0,)), ((), ()))
VMEM = pl.BlockSpec(memory_space=pltpu.VMEM)
SMEM = pl.BlockSpec(memory_space=pltpu.SMEM)


def exact_dot(left, right, dims):
    return lax.dot_general(
        left, right, dims, precision=lax.Precision.HIGHEST, preferred_element_type=F32
    )


def swap(msg, axes):
    return lax.all_to_all(msg, axes, 0, 0, tiled=True)


def call(kernel, in_specs, outs, scratch, name, make=pltpu.VMEM, near=True):
    run = pl.pallas_call(
        kernel,
        in_specs=in_specs,
        out_specs=[VMEM] * len(outs),
        out_shape=[make(s, d) for s, d in outs],
        scratch_shapes=scratch,
        compiler_params=pltpu.CompilerParams(vmem_limit_bytes=GRANT if near else None),
        name=name,
    )

    def placed(*args):
        if near:
            args = [
                pltpu.with_memory_space_constraint(arg, pltpu.VMEM) if spec is VMEM else arg
                for spec, arg in zip(in_specs, args, strict=True)
            ]
        return run(*args)

    return placed


def thirds(value):
    high = value.astype(BF16).astype(F32)
    middle = (value - high).astype(BF16).astype(F32)
    return high, middle, value - high - middle


def pack_kernel(right_ref, reg_ref, rows_ref, cols_ref, counts_ref, curv_ref, out_ref):
    sources = curv_ref.shape[0]
    base = STRIP * sources
    for s in range(sources):
        flipped = curv_ref[s].astype(F32).T
        for k in range(COLS):
            strip = flipped[STRIP * k : STRIP * k + STRIP, :].astype(BF16)
            out_ref[k, STRIP * s : STRIP * s + STRIP, :] = strip
    right = right_ref[...].T
    packed = jnp.concatenate([right[16 * j : 16 * j + 16, :] for j in range(4)], axis=1)
    cols = cols_ref[...]
    place = ((cols // 2) * BLKS + rows_ref[...]) * 2 + cols % 2
    place = jnp.where(counts_ref[...] > 0, place, -1).astype(F32)
    lines = [*thirds(reg_ref[...]), place]
    lines.append(jnp.zeros((8 - len(lines), PIECE), F32))
    notes = jnp.concatenate(lines, axis=0)
    notes = jnp.concatenate([notes, jnp.zeros((8, LANE - PIECE), F32)], axis=1)
    tiles = [tile.astype(BF16) for tile in (*thirds(packed), notes)]
    for k in range(COLS):
        for i, tile in enumerate(tiles):
            out_ref[k, base + 16 * i : base + 16 * i + tile.shape[0], :] = tile


def pixel_rows(fields):
    return [jnp.concatenate([fields[b].T, fields[2 + b].T], axis=1) for b in range(2)]


def unpack_kernel(place_ref, got_ref, res_ref, reg_ref, own_ref, own_reg_ref, out_ref, tall_ref):
    base = got_ref.shape[1] - NOTES
    packed, notes = [], []
    for k in range(COLS):
        parts = [got_ref[k, base + 16 * i : base + 16 * i + 16, :].astype(F32) for i in range(3)]
        packed.append(parts[0] + parts[1] + parts[2])
        note = got_ref[k, base + 48 : base + NOTES, :].astype(F32)
        notes.append(note[0:1] + note[1:2] + note[2:3])
    group = lax.broadcasted_iota(jnp.int32, (16, LANE), 1) // PIECE
    fields, regs = [], []
    for b in range(BLKS):
        pieces = []
        for j in range(4):
            piece = jnp.zeros((16, LANE), F32)
            for m in range(4):
                shift = (PIECE * (m - j)) % LANE
                part = packed[4 * b + m]
                part = pltpu.roll(part, shift, 1) if shift else part
                piece = jnp.where(group == m, part, piece)
            pieces.append(piece)
        fields.append(jnp.concatenate(pieces, axis=0))
        reg = jnp.zeros((8, LANE), F32)
        for m in range(4):
            part = jnp.broadcast_to(notes[4 * b + m], (8, LANE))
            part = pltpu.roll(part, PIECE * m, 1) if m else part
            reg = jnp.where(group[0:8] == m, part, reg)
        regs.append(jnp.broadcast_to(reg[0:1], (SMP, LANE)))
        res_ref[b] = fields[b]
        reg_ref[b] = reg
    start = pl.multiple_of(place_ref[0] * STRIP, STRIP)
    for target, values in ((own_ref, fields), (own_reg_ref, regs)):
        for b, tall in enumerate(pixel_rows(values)):
            tall_ref[b] = tall
            target[STRIP * b : STRIP * b + STRIP, :] = tall_ref[b, pl.ds(start, STRIP), :]
    own = own_ref[...]
    for r in range(out_ref.shape[0]):
        out_ref[r] = own


def dense_kernel(place_ref, got_ref, high_ref, low_ref, sum_ref):
    sources = place_ref.shape[1]
    sum_ref[...] = jnp.zeros_like(sum_ref)
    for s in range(sources):
        for k in range(COLS):
            place = place_ref[k, s]
            strip = got_ref[k, STRIP * s : STRIP * s + STRIP, :].astype(F32)
            strip = jnp.where(place >= 0, strip, 0.0)
            spot = jnp.maximum(place, 0)
            plane = spot // 2
            rows = pl.ds(pl.multiple_of(OWN * s + STRIP * (spot % 2), STRIP), STRIP)
            sum_ref[plane, rows, :] = sum_ref[plane, rows, :] + strip
    for plane in range(2 * BLKS):
        total = sum_ref[plane]
        high = total.astype(BF16)
        high_ref[plane] = high
        low_ref[plane] = (total - high.astype(F32)).astype(BF16)


def product_kernel(first, *refs):
    spread_ref, high_ref, low_ref, res_ref, reg_ref = refs[:5]
    if first:
        (out_ref,) = refs[5:]
    else:
        img_ref, dir_ref, out_ref = refs[5:]
    pixels = OWN * spread_ref.shape[0]
    spread = spread_ref[...].reshape(pixels, LANE)
    inputs = jnp.concatenate(
        [spread[LANE * i : LANE * i + LANE, :].T for i in range(pixels // LANE)], axis=1
    ).astype(BF16)
    share = 1.0 / COLS
    pair = jnp.zeros((SMP, LANE), F32)
    mixed = jnp.zeros((SMP, SMP), F32)
    coupled = []
    for b in range(BLKS):
        acc = jnp.zeros((SMP, LANE), F32)
        for half in range(2):
            left = inputs[SMP * half : SMP * half + SMP, :]
            for weights in (high_ref, low_ref):
                acc += lax.dot_general(
                    left, weights[BLKS * half + b], NN, preferred_element_type=F32
                )
        coupled.append(acc)
        res = res_ref[b]
        part = acc + reg_ref[b, 0:1, :] * res * share
        pair += exact_dot(res, jnp.concatenate([part, res * share], axis=0), NT)
        if not first:
            mixed += exact_dot(res, img_ref[b] * share, NT) + exact_dot(part, dir_ref[b], NT)
    other = jnp.concatenate([mixed, jnp.zeros((SMP, LANE - SMP), F32)], axis=1)
    tall = pixel_rows(coupled)
    for k in range(COLS):
        for b in range(2):
            out_ref[k, STRIP * b : STRIP * b + STRIP, :] = tall[b][STRIP * k : STRIP * k + STRIP]
        source = pair if k < 8 else other
        n = k % 8
        out_ref[k, OWN : OWN + 8, :] = source[8 * n : 8 * n + 8, :]


def col_sum_kernel(last, got_ref, own_ref, own_reg_ref, out_ref, piece_ref):
    total = got_ref[0]
    for k in range(1, COLS):
        total = total + got_ref[k]
    coupled = total[0:OWN, :]
    piece_ref[...] = coupled
    gram = total[OWN : OWN + 8, :]
    full = coupled + own_reg_ref[...] * own_ref[...]
    for r in range(out_ref.shape[0]):
        if last:
            out_ref[r] = gram
        else:
            out_ref[r, 0:OWN, :] = full
            out_ref[r, OWN : OWN + 8, :] = gram


def row_sum_kernel(got_ref, piece_ref, out_ref):
    top = got_ref.shape[1] - 8
    total = got_ref[0, top:, :]
    for r in range(1, got_ref.shape[0]):
        total = total + got_ref[r, top:, :]
    piece = piece_ref[...]
    for k in range(COLS):
        out_ref[k, 0:OWN, :] = piece
        out_ref[k, OWN : OWN + 8, :] = total


def solve_systems(systems, width):
    row_id = lax.broadcasted_iota(jnp.int32, (8, LANE), 0)
    work = []
    for matrix, rhs in systems:
        wide = jnp.concatenate([matrix, rhs], axis=1)
        work.append([wide[8 * t : 8 * t + 8, :] for t in range(8)])
    for j in range(0, SMP, width):
        top, low = divmod(j, 8)
        for tiles in work:
            columns = [
                [
                    jnp.broadcast_to(tile[:, j + i : j + i + 1], (8, LANE))
                    for i in range(width)
                ]
                for tile in tiles
            ]
            rows = [tiles[top][low + i : low + i + 1, :] for i in range(width)]
            block = [
                [columns[top][c][low + r : low + r + 1, :] for c in range(width)]
                for r in range(width)
            ]
            recip, lower = [], {}
            for a in range(width):
                recip.append(1.0 / block[a][a])
                for r in range(a + 1, width):
                    lower[r, a] = block[r][a] * recip[a]
                    rows[r] = rows[r] - lower[r, a] * rows[a]
                    for c in range(a + 1, width):
                        block[r][c] = block[r][c] - lower[r, a] * block[a][c]
            for a in reversed(range(width)):
                rows[a] = rows[a] * recip[a]
                for r in range(a + 1, width):
                    rows[a] = rows[a] - lower[r, a] * rows[r]
            for t in range(8):
                tile = tiles[t]
                for i in range(width):
                    tile = tile - columns[t][i] * rows[i]
                if t == top:
                    for i in range(width):
                        tile = jnp.where(row_id == low + i, rows[i], tile)
                tiles[t] = tile
    return [pltpu.roll(jnp.concatenate(tiles, axis=0), SMP, 1)[:, 0:SMP] for tiles in work]


def both_halves(matrix):
    zero = jnp.zeros((SMP, SMP), F32)
    upper = jnp.concatenate([matrix, zero], axis=1)
    lower = jnp.concatenate([zero, matrix], axis=1)
    return jnp.concatenate([upper, lower], axis=0)


def solve_kernel(first, last, *refs):
    refs = list(refs)
    place_ref, got_ref, res_ref, reg_ref = refs[:4]
    refs = refs[4:]
    if not first:
        dir_ref, img_ref, sol_ref, inv_ref, curv_ref = refs[:5]
        refs = refs[5:]
    if last:
        out_sol_ref, out_res_ref, keep_ref = refs
    else:
        spread_ref, fresh_ref = refs[:2]
        refs = refs[2:]
        if not first:
            spread_img_ref = refs.pop(0)
        new_res_ref, new_dir_ref, new_img_ref, new_sol_ref = refs[:4]
        new_inv_ref, new_curv_ref, new_spread_ref, new_spread_img_ref, own_ref = refs[4:]
    pair = jnp.concatenate([got_ref[k, OWN : OWN + 8, :] for k in range(8)], axis=0)
    gram = pltpu.roll(pair, SMP, 1)[:, 0:SMP]
    curv = pair[:, 0:SMP]
    if not first:
        mixed = jnp.concatenate([got_ref[k, OWN : OWN + 8, :] for k in range(8, 16)], axis=0)
        mixed = mixed[:, 0:SMP]
        beta_t = exact_dot(gram, inv_ref[...], NN)
        curv = curv + exact_dot(mixed + exact_dot(beta_t, curv_ref[...], NN), beta_t, NT)
    curv = 0.5 * (curv + curv.T)
    if last:
        (alpha,) = solve_systems([(curv, gram)], 8)
    else:
        square = (SMP, SMP)
        same = lax.broadcasted_iota(jnp.int32, square, 0) == lax.broadcasted_iota(
            jnp.int32, square, 1
        )
        alpha, inverse = solve_systems([(curv, gram), (gram, same.astype(F32))], 4)
        new_inv_ref[...] = inverse
        new_curv_ref[...] = curv
        sources = spread_ref.shape[0]
        pixels = OWN * sources
        spread_img = fresh_ref[:, 0:OWN, :].reshape(pixels, LANE)
        if not first:
            old = spread_img_ref[...].reshape(pixels, LANE)
            spread_img = spread_img + exact_dot(old, both_halves(beta_t.T), NN)
        spread = spread_ref[...].reshape(pixels, LANE)
        spread = spread - exact_dot(spread_img, both_halves(alpha), NN)
        new_spread_ref[...] = spread.reshape(sources, OWN, LANE)
        new_spread_img_ref[...] = spread_img.reshape(sources, OWN, LANE)
        own_ref[...] = new_spread_ref[place_ref[0]]
    alpha_t = alpha.T
    wide = [
        jnp.concatenate(
            [got_ref[k, STRIP * b : STRIP * b + STRIP, :] for k in range(COLS)], axis=0
        ).T
        for b in range(2)
    ]
    for b in range(BLKS):
        res = res_ref[b]
        half = SMP * (b // 2)
        image = wide[b % 2][half : half + SMP, :] + reg_ref[b, 0:1, :] * res
        direction = res
        if not first:
            image = image + exact_dot(beta_t, img_ref[b], NN)
            direction = direction + exact_dot(beta_t, dir_ref[b], NN)
        new_res = res - exact_dot(alpha_t, image, NN)
        new_sol = exact_dot(alpha_t, direction, NN)
        if not first:
            new_sol = sol_ref[b] + new_sol
        if last:
            keep_ref[0, b] = new_sol
            keep_ref[1, b] = new_res
        else:
            new_res_ref[b] = new_res
            new_dir_ref[b] = direction
            new_img_ref[b] = image
            new_sol_ref[b] = new_sol
    if last:
        mine = place_ref[0]
        shift = (LANE - PIECE * (mine % 4)) % LANE
        out_sol_ref[...] = pltpu.roll(keep_ref[0, mine // 4], shift, 1)[:, 0:PIECE].T
        out_res_ref[...] = pltpu.roll(keep_ref[1, mine // 4], shift, 1)[:, 0:PIECE].T


def body(right_side, regular, curvature, block_rows, block_cols, block_counts):
    sources = block_rows.shape[1]
    pixels = OWN * sources
    curv = curvature.reshape(sources, LANE, LANE)
    tables = [table.reshape(1, sources) for table in (block_rows, block_cols, block_counts)]
    field = ((BLKS, SMP, LANE), F32)
    small = ((SMP, SMP), F32)
    own_share = ((OWN, LANE), F32)
    spread_share = ((sources, OWN, LANE), F32)
    msg = ((COLS, OWN + 8, LANE), F32)
    start = ((COLS, STRIP * sources + NOTES, LANE), BF16)
    dense = ((2 * BLKS, pixels, LANE), BF16)

    (packed,) = call(pack_kernel, [VMEM] * 6, [start], [], "pack", near=False)(
        right_side.T, regular.reshape(1, PIECE), *tables, curv
    )
    col_here = lax.axis_index(COL).astype(jnp.int32).reshape(1)
    row_here = lax.axis_index(ROW).astype(jnp.int32).reshape(1)
    packed, col_here, row_here = lax.optimization_barrier((packed, col_here, row_here))
    packed = swap(packed, COL)
    res, reg, own, own_reg, out = call(
        unpack_kernel,
        [SMEM, VMEM],
        [field, ((BLKS, 8, LANE), F32), own_share, own_share, spread_share],
        [pltpu.VMEM((2, LANE, LANE), F32)],
        "unpack",
    )(col_here, packed)
    spread = swap(out, ROW)
    places = packed[:, STRIP * sources + 51, 0:sources].astype(jnp.int32)
    high, low = call(
        dense_kernel,
        [SMEM, VMEM],
        [dense, dense],
        [pltpu.VMEM(dense[0], F32)],
        "dense",
    )(places, packed)
    state, spread_img = [], []
    for step in range(ITERS):
        first, last = step == 0, step == ITERS - 1
        before = [] if first else [state[1], state[0]]
        (part,) = call(
            functools.partial(product_kernel, first),
            [VMEM] * (5 + len(before)),
            [msg],
            [],
            f"product_{step}",
        )(spread, high, low, res, reg, *before)
        out, piece = call(
            functools.partial(col_sum_kernel, last),
            [VMEM] * 3,
            [((sources, 8 if last else OWN + 8, LANE), F32), own_share],
            [],
            f"col_sum_{step}",
        )(swap(part, COL), own, own_reg)
        fresh = swap(out, ROW)
        (whole,) = call(row_sum_kernel, [VMEM] * 2, [msg], [], f"row_sum_{step}")(fresh, piece)
        got = swap(whole, COL)
        solve = functools.partial(solve_kernel, first, last)
        if last:
            share = ((PIECE, SMP), F32)
            keep = pltpu.VMEM((2, BLKS, SMP, LANE), F32)
            shares = call(
                solve,
                [SMEM] + [VMEM] * (3 + len(state)),
                [share, share],
                [keep],
                f"solve_{step}",
                jax.ShapeDtypeStruct,
            )(col_here, got, res, reg, *state)
            return tuple(part.T for part in shares)
        inputs = [got, res, reg, *state, spread, fresh, *spread_img]
        outs = [field] * 4 + [small] * 2 + [spread_share] * 2 + [own_share]
        res, *state, spread, img, own = call(
            solve, [SMEM] + [VMEM] * len(inputs), outs, [], f"solve_{step}"
        )(row_here, *inputs)
        spread_img = [img]


def solution(mesh):
    finer = Mesh(mesh.devices.reshape(8, 4, 8, 2), ROW_COL)
    placed = (
        P(None, ROW_COL),
        P(ROW_COL),
        P(ROW, None, COL, None, None),
        P(ROW, None, COL),
        P(ROW, None, COL),
        P(ROW, None, COL),
    )
    return jax.shard_map(
        body,
        mesh=finer,
        in_specs=placed,
        out_specs=(P(None, ROW_COL), P(None, ROW_COL)),
        check_vma=False,
    )
```

```python
import functools

import jax
import jax.numpy as jnp
from jax import lax
from jax.experimental import pallas as pl
from jax.experimental.pallas import tpu as pltpu
from jax.sharding import Mesh
from jax.sharding import PartitionSpec as P

ITERS = 3
COL = ("col_0", "col_1")
ROW = ("row_0", "row_1")
ROW_COL = ROW + COL
F32 = jnp.float32
BF16 = jnp.bfloat16
SMP = 64
LANE = 128
BLKS = 4
COLS = 16
PIECE = 32
STRIP = 8
OWN = 2 * STRIP
GRANT = 16 * 2**20
NOTES = 56
NT = (((1,), (1,)), ((), ()))
NN = (((1,), (0,)), ((), ()))
VMEM = pl.BlockSpec(memory_space=pltpu.VMEM)
SMEM = pl.BlockSpec(memory_space=pltpu.SMEM)


def exact_dot(left, right, dims):
    return lax.dot_general(
        left, right, dims, precision=lax.Precision.HIGHEST, preferred_element_type=F32
    )


def swap(msg, axes):
    return lax.all_to_all(msg, axes, 0, 0, tiled=True)


def call(kernel, in_specs, outs, scratch, name, make=pltpu.VMEM, near=True):
    run = pl.pallas_call(
        kernel,
        in_specs=in_specs,
        out_specs=[VMEM] * len(outs),
        out_shape=[make(s, d) for s, d in outs],
        scratch_shapes=scratch,
        compiler_params=pltpu.CompilerParams(vmem_limit_bytes=GRANT if near else None),
        name=name,
    )

    def placed(*args):
        if near:
            args = [
                pltpu.with_memory_space_constraint(arg, pltpu.VMEM) if spec is VMEM else arg
                for spec, arg in zip(in_specs, args, strict=True)
            ]
        return run(*args)

    return placed


def thirds(value):
    high = value.astype(BF16).astype(F32)
    middle = (value - high).astype(BF16).astype(F32)
    return high, middle, value - high - middle


def pack_kernel(right_ref, reg_ref, rows_ref, cols_ref, counts_ref, curv_ref, out_ref):
    sources = curv_ref.shape[0]
    base = STRIP * sources
    for s in range(sources):
        flipped = curv_ref[s].astype(F32).T
        for k in range(COLS):
            strip = flipped[STRIP * k : STRIP * k + STRIP, :].astype(BF16)
            out_ref[k, STRIP * s : STRIP * s + STRIP, :] = strip
    right = right_ref[...].T
    packed = jnp.concatenate([right[16 * j : 16 * j + 16, :] for j in range(4)], axis=1)
    cols = cols_ref[...]
    place = ((cols // 2) * BLKS + rows_ref[...]) * 2 + cols % 2
    place = jnp.where(counts_ref[...] > 0, place, -1).astype(F32)
    lines = [*thirds(reg_ref[...]), place]
    lines.append(jnp.zeros((8 - len(lines), PIECE), F32))
    notes = jnp.concatenate(lines, axis=0)
    notes = jnp.concatenate([notes, jnp.zeros((8, LANE - PIECE), F32)], axis=1)
    tiles = [tile.astype(BF16) for tile in (*thirds(packed), notes)]
    for k in range(COLS):
        for i, tile in enumerate(tiles):
            out_ref[k, base + 16 * i : base + 16 * i + tile.shape[0], :] = tile


def pixel_rows(fields):
    return [jnp.concatenate([fields[b].T, fields[2 + b].T], axis=1) for b in range(2)]


def unpack_kernel(place_ref, got_ref, res_ref, reg_ref, own_ref, own_reg_ref, out_ref, tall_ref):
    base = got_ref.shape[1] - NOTES
    packed, notes = [], []
    for k in range(COLS):
        parts = [got_ref[k, base + 16 * i : base + 16 * i + 16, :].astype(F32) for i in range(3)]
        packed.append(parts[0] + parts[1] + parts[2])
        note = got_ref[k, base + 48 : base + NOTES, :].astype(F32)
        notes.append(note[0:1] + note[1:2] + note[2:3])
    group = lax.broadcasted_iota(jnp.int32, (16, LANE), 1) // PIECE
    fields, regs = [], []
    for b in range(BLKS):
        pieces = []
        for j in range(4):
            piece = jnp.zeros((16, LANE), F32)
            for m in range(4):
                shift = (PIECE * (m - j)) % LANE
                part = packed[4 * b + m]
                part = pltpu.roll(part, shift, 1) if shift else part
                piece = jnp.where(group == m, part, piece)
            pieces.append(piece)
        fields.append(jnp.concatenate(pieces, axis=0))
        reg = jnp.zeros((8, LANE), F32)
        for m in range(4):
            part = jnp.broadcast_to(notes[4 * b + m], (8, LANE))
            part = pltpu.roll(part, PIECE * m, 1) if m else part
            reg = jnp.where(group[0:8] == m, part, reg)
        regs.append(jnp.broadcast_to(reg[0:1], (SMP, LANE)))
        res_ref[b] = fields[b]
        reg_ref[b] = reg
    start = pl.multiple_of(place_ref[0] * STRIP, STRIP)
    for target, values in ((own_ref, fields), (own_reg_ref, regs)):
        for b, tall in enumerate(pixel_rows(values)):
            tall_ref[b] = tall
            target[STRIP * b : STRIP * b + STRIP, :] = tall_ref[b, pl.ds(start, STRIP), :]
    own = own_ref[...]
    for r in range(out_ref.shape[0]):
        out_ref[r] = own


def dense_kernel(place_ref, got_ref, high_ref, low_ref, sum_ref):
    sources = place_ref.shape[1]
    sum_ref[...] = jnp.zeros_like(sum_ref)
    for s in range(sources):
        for k in range(COLS):
            place = place_ref[k, s]
            strip = got_ref[k, STRIP * s : STRIP * s + STRIP, :].astype(F32)
            strip = jnp.where(place >= 0, strip, 0.0)
            spot = jnp.maximum(place, 0)
            plane = spot // 2
            rows = pl.ds(pl.multiple_of(OWN * s + STRIP * (spot % 2), STRIP), STRIP)
            sum_ref[plane, rows, :] = sum_ref[plane, rows, :] + strip
    for plane in range(2 * BLKS):
        total = sum_ref[plane]
        high = total.astype(BF16)
        high_ref[plane] = high
        low_ref[plane] = (total - high.astype(F32)).astype(BF16)


def product_kernel(first, *refs):
    spread_ref, high_ref, low_ref, res_ref, reg_ref = refs[:5]
    if first:
        (out_ref,) = refs[5:]
    else:
        img_ref, dir_ref, out_ref = refs[5:]
    pixels = OWN * spread_ref.shape[0]
    spread = spread_ref[...].reshape(pixels, LANE)
    inputs = jnp.concatenate(
        [spread[LANE * i : LANE * i + LANE, :].T for i in range(pixels // LANE)], axis=1
    )
    parts = [inputs.astype(BF16)]
    if not first:
        parts.append((inputs - parts[0].astype(F32)).astype(BF16))
    share = 1.0 / COLS
    pair = jnp.zeros((SMP, LANE), F32)
    mixed = jnp.zeros((SMP, SMP), F32)
    coupled = []
    for b in range(BLKS):
        acc = jnp.zeros((SMP, LANE), F32)
        for half in range(2):
            for i, weights in enumerate((high_ref, low_ref)):
                for part in parts[: 2 - i]:
                    acc += lax.dot_general(
                        part[SMP * half : SMP * half + SMP, :],
                        weights[BLKS * half + b],
                        NN,
                        preferred_element_type=F32,
                    )
        coupled.append(acc)
        res = res_ref[b]
        part = acc + reg_ref[b, 0:1, :] * res * share
        pair += exact_dot(res, jnp.concatenate([part, res * share], axis=0), NT)
        if not first:
            mixed += exact_dot(res, img_ref[b] * share, NT) + exact_dot(part, dir_ref[b], NT)
    other = jnp.concatenate([mixed, jnp.zeros((SMP, LANE - SMP), F32)], axis=1)
    tall = pixel_rows(coupled)
    for k in range(COLS):
        for b in range(2):
            out_ref[k, STRIP * b : STRIP * b + STRIP, :] = tall[b][STRIP * k : STRIP * k + STRIP]
        source = pair if k < 8 else other
        n = k % 8
        out_ref[k, OWN : OWN + 8, :] = source[8 * n : 8 * n + 8, :]


def col_sum_kernel(last, got_ref, own_ref, own_reg_ref, out_ref, piece_ref):
    total = got_ref[0]
    for k in range(1, COLS):
        total = total + got_ref[k]
    coupled = total[0:OWN, :]
    piece_ref[...] = coupled
    gram = total[OWN : OWN + 8, :]
    full = coupled + own_reg_ref[...] * own_ref[...]
    for r in range(out_ref.shape[0]):
        if last:
            out_ref[r] = gram
        else:
            out_ref[r, 0:OWN, :] = full
            out_ref[r, OWN : OWN + 8, :] = gram


def row_sum_kernel(got_ref, piece_ref, out_ref):
    top = got_ref.shape[1] - 8
    total = got_ref[0, top:, :]
    for r in range(1, got_ref.shape[0]):
        total = total + got_ref[r, top:, :]
    piece = piece_ref[...]
    for k in range(COLS):
        out_ref[k, 0:OWN, :] = piece
        out_ref[k, OWN : OWN + 8, :] = total


def solve_systems(systems, width):
    row_id = lax.broadcasted_iota(jnp.int32, (8, LANE), 0)
    work = []
    for matrix, rhs in systems:
        wide = jnp.concatenate([matrix, rhs], axis=1)
        work.append([wide[8 * t : 8 * t + 8, :] for t in range(8)])
    for j in range(0, SMP, width):
        top, low = divmod(j, 8)
        for tiles in work:
            columns = [
                [
                    jnp.broadcast_to(tile[:, j + i : j + i + 1], (8, LANE))
                    for i in range(width)
                ]
                for tile in tiles
            ]
            rows = [tiles[top][low + i : low + i + 1, :] for i in range(width)]
            block = [
                [columns[top][c][low + r : low + r + 1, :] for c in range(width)]
                for r in range(width)
            ]
            recip, lower = [], {}
            for a in range(width):
                recip.append(1.0 / block[a][a])
                for r in range(a + 1, width):
                    lower[r, a] = block[r][a] * recip[a]
                    rows[r] = rows[r] - lower[r, a] * rows[a]
                    for c in range(a + 1, width):
                        block[r][c] = block[r][c] - lower[r, a] * block[a][c]
            for a in reversed(range(width)):
                rows[a] = rows[a] * recip[a]
                for r in range(a + 1, width):
                    rows[a] = rows[a] - lower[r, a] * rows[r]
            for t in range(8):
                tile = tiles[t]
                for i in range(width):
                    tile = tile - columns[t][i] * rows[i]
                if t == top:
                    for i in range(width):
                        tile = jnp.where(row_id == low + i, rows[i], tile)
                tiles[t] = tile
    return [pltpu.roll(jnp.concatenate(tiles, axis=0), SMP, 1)[:, 0:SMP] for tiles in work]


def both_halves(matrix):
    zero = jnp.zeros((SMP, SMP), F32)
    upper = jnp.concatenate([matrix, zero], axis=1)
    lower = jnp.concatenate([zero, matrix], axis=1)
    return jnp.concatenate([upper, lower], axis=0)


def solve_kernel(first, last, *refs):
    refs = list(refs)
    col_ref, row_ref, got_ref, res_ref, reg_ref = refs[:5]
    refs = refs[5:]
    mine = col_ref[0] // 4
    if not first:
        dir_ref, img_ref, sol_ref, inv_ref, curv_ref = refs[:5]
        refs = refs[5:]
    if last:
        out_sol_ref, out_res_ref, keep_ref = refs
    else:
        spread_ref, fresh_ref = refs[:2]
        refs = refs[2:]
        if not first:
            spread_img_ref = refs.pop(0)
        new_res_ref, new_dir_ref, new_img_ref, new_sol_ref = refs[:4]
        new_inv_ref, new_curv_ref, new_spread_ref, new_spread_img_ref, own_ref = refs[4:]
    pair = jnp.concatenate([got_ref[k, OWN : OWN + 8, :] for k in range(8)], axis=0)
    gram = pltpu.roll(pair, SMP, 1)[:, 0:SMP]
    curv = pair[:, 0:SMP]
    if not first:
        mixed = jnp.concatenate([got_ref[k, OWN : OWN + 8, :] for k in range(8, 16)], axis=0)
        mixed = mixed[:, 0:SMP]
        beta_t = exact_dot(gram, inv_ref[...], NN)
        curv = curv + exact_dot(mixed + exact_dot(beta_t, curv_ref[...], NN), beta_t, NT)
    curv = 0.5 * (curv + curv.T)
    if last:
        (alpha,) = solve_systems([(curv, gram)], 8)
    else:
        square = (SMP, SMP)
        same = lax.broadcasted_iota(jnp.int32, square, 0) == lax.broadcasted_iota(
            jnp.int32, square, 1
        )
        alpha, inverse = solve_systems([(curv, gram), (gram, same.astype(F32))], 4)
        new_inv_ref[...] = inverse
        new_curv_ref[...] = curv
        sources = spread_ref.shape[0]
        pixels = OWN * sources
        spread_img = fresh_ref[:, 0:OWN, :].reshape(pixels, LANE)
        if not first:
            old = spread_img_ref[...].reshape(pixels, LANE)
            spread_img = spread_img + exact_dot(old, both_halves(beta_t.T), NN)
        spread = spread_ref[...].reshape(pixels, LANE)
        spread = spread - exact_dot(spread_img, both_halves(alpha), NN)
        new_spread_ref[...] = spread.reshape(sources, OWN, LANE)
        new_spread_img_ref[...] = spread_img.reshape(sources, OWN, LANE)
        own_ref[...] = new_spread_ref[row_ref[0]]
    alpha_t = alpha.T
    wide = [
        jnp.concatenate(
            [got_ref[k, STRIP * b : STRIP * b + STRIP, :] for k in range(COLS)], axis=0
        ).T
        for b in range(2)
    ]

    def advance(coupled, b):
        res = res_ref[b]
        image = coupled + reg_ref[b][0:1, :] * res
        direction = res
        if not first:
            image = image + exact_dot(beta_t, img_ref[b], NN)
            direction = direction + exact_dot(beta_t, dir_ref[b], NN)
        return res - exact_dot(alpha_t, image, NN), image, direction

    if last:
        for b in range(2):
            keep_ref[b] = wide[b]
        start = pl.multiple_of(SMP * (mine // 2), SMP)
        new_res, _, direction = advance(keep_ref[mine % 2, pl.ds(start, SMP), :], mine)
    else:
        for b in range(BLKS):
            half = SMP * (b // 2)
            coupled = wide[b % 2][half : half + SMP, :]
            new_res_ref[b], new_img_ref[b], new_dir_ref[b] = advance(coupled, b)
        direction = new_dir_ref[mine]
    new_sol = exact_dot(alpha_t, direction, NN)
    if not first:
        new_sol = sol_ref[...] + new_sol
    if last:
        shift = (LANE - PIECE * (col_ref[0] % 4)) % LANE
        out_sol_ref[...] = pltpu.roll(new_sol, shift, 1)[:, 0:PIECE].T
        out_res_ref[...] = pltpu.roll(new_res, shift, 1)[:, 0:PIECE].T
    else:
        new_sol_ref[...] = new_sol


def body(right_side, regular, curvature, block_rows, block_cols, block_counts):
    sources = block_rows.shape[1]
    pixels = OWN * sources
    curv = curvature.reshape(sources, LANE, LANE)
    tables = [table.reshape(1, sources) for table in (block_rows, block_cols, block_counts)]
    field = ((BLKS, SMP, LANE), F32)
    small = ((SMP, SMP), F32)
    own_share = ((OWN, LANE), F32)
    spread_share = ((sources, OWN, LANE), F32)
    msg = ((COLS, OWN + 8, LANE), F32)
    start = ((COLS, STRIP * sources + NOTES, LANE), BF16)
    dense = ((2 * BLKS, pixels, LANE), BF16)

    (packed,) = call(pack_kernel, [VMEM] * 6, [start], [], "pack", near=False)(
        right_side.T, regular.reshape(1, PIECE), *tables, curv
    )
    col_here = lax.axis_index(COL).astype(jnp.int32).reshape(1)
    row_here = lax.axis_index(ROW).astype(jnp.int32).reshape(1)
    packed, col_here, row_here = lax.optimization_barrier((packed, col_here, row_here))
    packed = swap(packed, COL)
    res, reg, own, own_reg, out = call(
        unpack_kernel,
        [SMEM, VMEM],
        [field, ((BLKS, 8, LANE), F32), own_share, own_share, spread_share],
        [pltpu.VMEM((2, LANE, LANE), F32)],
        "unpack",
    )(col_here, packed)
    spread = swap(out, ROW)
    places = packed[:, STRIP * sources + 51, 0:sources].astype(jnp.int32)
    high, low = call(
        dense_kernel,
        [SMEM, VMEM],
        [dense, dense],
        [pltpu.VMEM(dense[0], F32)],
        "dense",
    )(places, packed)
    state, spread_img = [], []
    for step in range(ITERS):
        first, last = step == 0, step == ITERS - 1
        before = [] if first else [state[1], state[0]]
        (part,) = call(
            functools.partial(product_kernel, first),
            [VMEM] * (5 + len(before)),
            [msg],
            [],
            f"product_{step}",
        )(spread, high, low, res, reg, *before)
        out, piece = call(
            functools.partial(col_sum_kernel, last),
            [VMEM] * 3,
            [((sources, 8 if last else OWN + 8, LANE), F32), own_share],
            [],
            f"col_sum_{step}",
        )(swap(part, COL), own, own_reg)
        fresh = swap(out, ROW)
        (whole,) = call(row_sum_kernel, [VMEM] * 2, [msg], [], f"row_sum_{step}")(fresh, piece)
        got = swap(whole, COL)
        solve = functools.partial(solve_kernel, first, last)
        if last:
            share = ((PIECE, SMP), F32)
            keep = pltpu.VMEM((2, LANE, LANE), F32)
            shares = call(
                solve,
                [SMEM] * 2 + [VMEM] * (3 + len(state)),
                [share, share],
                [keep],
                f"solve_{step}",
                jax.ShapeDtypeStruct,
            )(col_here, row_here, got, res, reg, *state)
            return tuple(part.T for part in shares)
        inputs = [got, res, reg, *state, spread, fresh, *spread_img]
        outs = [field] * 3 + [((SMP, LANE), F32)] + [small] * 2 + [spread_share] * 2 + [own_share]
        res, *state, spread, img, own = call(
            solve, [SMEM] * 2 + [VMEM] * len(inputs), outs, [], f"solve_{step}"
        )(col_here, row_here, *inputs)
        spread_img = [img]


def solution(mesh):
    finer = Mesh(mesh.devices.reshape(8, 4, 8, 2), ROW_COL)
    placed = (
        P(None, ROW_COL),
        P(ROW_COL),
        P(ROW, None, COL, None, None),
        P(ROW, None, COL),
        P(ROW, None, COL),
        P(ROW, None, COL),
    )
    return jax.shard_map(
        body,
        mesh=finer,
        in_specs=placed,
        out_specs=(P(None, ROW_COL), P(None, ROW_COL)),
        check_vma=False,
    )
```

```python
import functools

import jax
import jax.numpy as jnp
from jax import lax
from jax.experimental import pallas as pl
from jax.experimental.pallas import tpu as pltpu
from jax.sharding import Mesh
from jax.sharding import PartitionSpec as P

ITERS = 3
COL = ("col_0", "col_1")
ROW = ("row_0", "row_1")
ROW_COL = ROW + COL
F32 = jnp.float32
BF16 = jnp.bfloat16
SMP = 64
LANE = 128
BLKS = 4
COLS = 16
PIECE = 32
STRIP = 8
OWN = 2 * STRIP
GRANT = 16 * 2**20
NOTES = 56
NT = (((1,), (1,)), ((), ()))
NN = (((1,), (0,)), ((), ()))
VMEM = pl.BlockSpec(memory_space=pltpu.VMEM)
SMEM = pl.BlockSpec(memory_space=pltpu.SMEM)


def exact_dot(left, right, dims):
    return lax.dot_general(
        left, right, dims, precision=lax.Precision.HIGHEST, preferred_element_type=F32
    )


def swap(msg, axes):
    return lax.all_to_all(msg, axes, 0, 0, tiled=True)


def call(kernel, in_specs, outs, scratch, name, make=pltpu.VMEM, near=True):
    run = pl.pallas_call(
        kernel,
        in_specs=in_specs,
        out_specs=[VMEM] * len(outs),
        out_shape=[make(s, d) for s, d in outs],
        scratch_shapes=scratch,
        compiler_params=pltpu.CompilerParams(vmem_limit_bytes=GRANT if near else None),
        name=name,
    )

    def placed(*args):
        if near:
            args = [
                pltpu.with_memory_space_constraint(arg, pltpu.VMEM) if spec is VMEM else arg
                for spec, arg in zip(in_specs, args, strict=True)
            ]
        return run(*args)

    return placed


def thirds(value):
    high = value.astype(BF16).astype(F32)
    middle = (value - high).astype(BF16).astype(F32)
    return high, middle, value - high - middle


def pack_kernel(right_ref, reg_ref, rows_ref, cols_ref, counts_ref, curv_ref, out_ref):
    sources = curv_ref.shape[0]
    base = STRIP * sources
    for s in range(sources):
        flipped = curv_ref[s].astype(F32).T
        for k in range(COLS):
            strip = flipped[STRIP * k : STRIP * k + STRIP, :].astype(BF16)
            out_ref[k, STRIP * s : STRIP * s + STRIP, :] = strip
    right = right_ref[...].T
    packed = jnp.concatenate([right[16 * j : 16 * j + 16, :] for j in range(4)], axis=1)
    cols = cols_ref[...]
    place = ((cols // 2) * BLKS + rows_ref[...]) * 2 + cols % 2
    place = jnp.where(counts_ref[...] > 0, place, -1).astype(F32)
    lines = [*thirds(reg_ref[...]), place]
    lines.append(jnp.zeros((8 - len(lines), PIECE), F32))
    notes = jnp.concatenate(lines, axis=0)
    notes = jnp.concatenate([notes, jnp.zeros((8, LANE - PIECE), F32)], axis=1)
    tiles = [tile.astype(BF16) for tile in (*thirds(packed), notes)]
    for k in range(COLS):
        for i, tile in enumerate(tiles):
            out_ref[k, base + 16 * i : base + 16 * i + tile.shape[0], :] = tile


def pixel_rows(fields):
    return [jnp.concatenate([fields[b].T, fields[2 + b].T], axis=1) for b in range(2)]


def unpack_kernel(place_ref, got_ref, res_ref, reg_ref, own_ref, own_reg_ref, out_ref, tall_ref):
    base = got_ref.shape[1] - NOTES
    packed, notes = [], []
    for k in range(COLS):
        parts = [got_ref[k, base + 16 * i : base + 16 * i + 16, :].astype(F32) for i in range(3)]
        packed.append(parts[0] + parts[1] + parts[2])
        note = got_ref[k, base + 48 : base + NOTES, :].astype(F32)
        notes.append(note[0:1] + note[1:2] + note[2:3])
    group = lax.broadcasted_iota(jnp.int32, (16, LANE), 1) // PIECE
    fields, regs = [], []
    for b in range(BLKS):
        pieces = []
        for j in range(4):
            piece = jnp.zeros((16, LANE), F32)
            for m in range(4):
                shift = (PIECE * (m - j)) % LANE
                part = packed[4 * b + m]
                part = pltpu.roll(part, shift, 1) if shift else part
                piece = jnp.where(group == m, part, piece)
            pieces.append(piece)
        fields.append(jnp.concatenate(pieces, axis=0))
        reg = jnp.zeros((8, LANE), F32)
        for m in range(4):
            part = jnp.broadcast_to(notes[4 * b + m], (8, LANE))
            part = pltpu.roll(part, PIECE * m, 1) if m else part
            reg = jnp.where(group[0:8] == m, part, reg)
        regs.append(jnp.broadcast_to(reg[0:1], (SMP, LANE)))
        res_ref[b] = fields[b]
        reg_ref[b] = reg
    start = pl.multiple_of(place_ref[0] * STRIP, STRIP)
    for target, values in ((own_ref, fields), (own_reg_ref, regs)):
        for b, tall in enumerate(pixel_rows(values)):
            tall_ref[b] = tall
            target[STRIP * b : STRIP * b + STRIP, :] = tall_ref[b, pl.ds(start, STRIP), :]
    own = own_ref[...]
    for r in range(out_ref.shape[0]):
        out_ref[r] = own


def dense_kernel(place_ref, got_ref, high_ref, low_ref, sum_ref):
    sources = place_ref.shape[1]
    sum_ref[...] = jnp.zeros_like(sum_ref)
    for s in range(sources):
        for k in range(COLS):
            place = place_ref[k, s]
            strip = got_ref[k, STRIP * s : STRIP * s + STRIP, :].astype(F32)
            strip = jnp.where(place >= 0, strip, 0.0)
            spot = jnp.maximum(place, 0)
            plane = spot // 2
            rows = pl.ds(pl.multiple_of(OWN * s + STRIP * (spot % 2), STRIP), STRIP)
            sum_ref[plane, rows, :] = sum_ref[plane, rows, :] + strip
    for plane in range(2 * BLKS):
        total = sum_ref[plane]
        high = total.astype(BF16)
        high_ref[plane] = high
        low_ref[plane] = (total - high.astype(F32)).astype(BF16)


def flat(field_ref):
    return jnp.concatenate([field_ref[b] for b in range(BLKS)], axis=1)


def product_kernel(first, *refs):
    spread_ref, high_ref, low_ref, res_ref, reg_ref = refs[:5]
    if first:
        (out_ref,) = refs[5:]
    else:
        img_ref, dir_ref, out_ref = refs[5:]
    pixels = OWN * spread_ref.shape[0]
    spread = spread_ref[...].reshape(pixels, LANE)
    inputs = jnp.concatenate(
        [spread[LANE * i : LANE * i + LANE, :].T for i in range(pixels // LANE)], axis=1
    )
    top = inputs.astype(BF16)
    low = (inputs - top.astype(F32)).astype(BF16)
    coupled = []
    for b in range(BLKS):
        acc = jnp.zeros((SMP, LANE), F32)
        for half in range(2):
            cut = slice(SMP * half, SMP * half + SMP)
            plane = BLKS * half + b
            left = top[cut] if first else jnp.concatenate([top[cut], low[cut]], axis=0)
            main = lax.dot_general(left, high_ref[plane], NN, preferred_element_type=F32)
            acc += main if first else main[0:SMP] + main[SMP:]
            acc += lax.dot_general(top[cut], low_ref[plane], NN, preferred_element_type=F32)
        coupled.append(acc)
    share = 1.0 / COLS
    res = flat(res_ref)
    part = jnp.concatenate(
        [coupled[b] + reg_ref[b, 0:1, :] * res_ref[b] * share for b in range(BLKS)], axis=1
    )
    pair = exact_dot(res, jnp.concatenate([part, res * share], axis=0), NT)
    if first:
        mixed = jnp.zeros((SMP, SMP), F32)
    else:
        left = jnp.concatenate([res, part], axis=1)
        right = jnp.concatenate([flat(img_ref) * share, flat(dir_ref)], axis=1)
        mixed = exact_dot(left, right, NT)
    other = jnp.concatenate([mixed, jnp.zeros((SMP, LANE - SMP), F32)], axis=1)
    tall = pixel_rows(coupled)
    for k in range(COLS):
        for b in range(2):
            out_ref[k, STRIP * b : STRIP * b + STRIP, :] = tall[b][STRIP * k : STRIP * k + STRIP]
        source = pair if k < 8 else other
        n = k % 8
        out_ref[k, OWN : OWN + 8, :] = source[8 * n : 8 * n + 8, :]


def col_sum_kernel(last, got_ref, own_ref, own_reg_ref, out_ref, piece_ref):
    total = got_ref[0]
    for k in range(1, COLS):
        total = total + got_ref[k]
    coupled = total[0:OWN, :]
    piece_ref[...] = coupled
    gram = total[OWN : OWN + 8, :]
    full = coupled + own_reg_ref[...] * own_ref[...]
    for r in range(out_ref.shape[0]):
        if last:
            out_ref[r] = gram
        else:
            out_ref[r, 0:OWN, :] = full
            out_ref[r, OWN : OWN + 8, :] = gram


def row_sum_kernel(got_ref, piece_ref, out_ref):
    top = got_ref.shape[1] - 8
    total = got_ref[0, top:, :]
    for r in range(1, got_ref.shape[0]):
        total = total + got_ref[r, top:, :]
    piece = piece_ref[...]
    for k in range(COLS):
        out_ref[k, 0:OWN, :] = piece
        out_ref[k, OWN : OWN + 8, :] = total


def solve_systems(systems, width):
    row_id = lax.broadcasted_iota(jnp.int32, (8, LANE), 0)
    work = []
    for matrix, rhs in systems:
        wide = jnp.concatenate([matrix, rhs], axis=1)
        work.append([wide[8 * t : 8 * t + 8, :] for t in range(8)])
    for j in range(0, SMP, width):
        top, low = divmod(j, 8)
        for tiles in work:
            columns = [
                [
                    jnp.broadcast_to(tile[:, j + i : j + i + 1], (8, LANE))
                    for i in range(width)
                ]
                for tile in tiles
            ]
            rows = [tiles[top][low + i : low + i + 1, :] for i in range(width)]
            block = [
                [columns[top][c][low + r : low + r + 1, :] for c in range(width)]
                for r in range(width)
            ]
            recip, lower = [], {}
            for a in range(width):
                recip.append(1.0 / block[a][a])
                for r in range(a + 1, width):
                    lower[r, a] = block[r][a] * recip[a]
                    rows[r] = rows[r] - lower[r, a] * rows[a]
                    for c in range(a + 1, width):
                        block[r][c] = block[r][c] - lower[r, a] * block[a][c]
            for a in reversed(range(width)):
                rows[a] = rows[a] * recip[a]
                for r in range(a + 1, width):
                    rows[a] = rows[a] - lower[r, a] * rows[r]
            for t in range(8):
                tile = tiles[t]
                for i in range(width):
                    tile = tile - columns[t][i] * rows[i]
                if t == top:
                    for i in range(width):
                        tile = jnp.where(row_id == low + i, rows[i], tile)
                tiles[t] = tile
    return [pltpu.roll(jnp.concatenate(tiles, axis=0), SMP, 1)[:, 0:SMP] for tiles in work]


def both_halves(matrix):
    zero = jnp.zeros((SMP, SMP), F32)
    upper = jnp.concatenate([matrix, zero], axis=1)
    lower = jnp.concatenate([zero, matrix], axis=1)
    return jnp.concatenate([upper, lower], axis=0)


def solve_kernel(first, last, *refs):
    refs = list(refs)
    col_ref, row_ref, got_ref, res_ref, reg_ref = refs[:5]
    refs = refs[5:]
    mine = col_ref[0] // 4
    if not first:
        dir_ref, img_ref, sol_ref, inv_ref, curv_ref = refs[:5]
        refs = refs[5:]
    if last:
        out_sol_ref, out_res_ref, keep_ref = refs
    else:
        spread_ref, fresh_ref = refs[:2]
        refs = refs[2:]
        if not first:
            spread_img_ref = refs.pop(0)
        new_res_ref, new_dir_ref, new_img_ref, new_sol_ref = refs[:4]
        new_inv_ref, new_curv_ref, new_spread_ref, new_spread_img_ref, own_ref = refs[4:]
    pair = jnp.concatenate([got_ref[k, OWN : OWN + 8, :] for k in range(8)], axis=0)
    gram = pltpu.roll(pair, SMP, 1)[:, 0:SMP]
    curv = pair[:, 0:SMP]
    if not first:
        mixed = jnp.concatenate([got_ref[k, OWN : OWN + 8, :] for k in range(8, 16)], axis=0)
        mixed = mixed[:, 0:SMP]
        beta_t = exact_dot(gram, inv_ref[...], NN)
        curv = curv + exact_dot(mixed + exact_dot(beta_t, curv_ref[...], NN), beta_t, NT)
    curv = 0.5 * (curv + curv.T)
    if last:
        (alpha,) = solve_systems([(curv, gram)], 8)
    else:
        square = (SMP, SMP)
        same = lax.broadcasted_iota(jnp.int32, square, 0) == lax.broadcasted_iota(
            jnp.int32, square, 1
        )
        alpha, inverse = solve_systems([(curv, gram), (gram, same.astype(F32))], 8)
        new_inv_ref[...] = inverse
        new_curv_ref[...] = curv
        sources = spread_ref.shape[0]
        pixels = OWN * sources
        spread_img = fresh_ref[:, 0:OWN, :].reshape(pixels, LANE)
        if not first:
            old = spread_img_ref[...].reshape(pixels, LANE)
            spread_img = spread_img + exact_dot(old, both_halves(beta_t.T), NN)
        spread = spread_ref[...].reshape(pixels, LANE)
        spread = spread - exact_dot(spread_img, both_halves(alpha), NN)
        new_spread_ref[...] = spread.reshape(sources, OWN, LANE)
        new_spread_img_ref[...] = spread_img.reshape(sources, OWN, LANE)
        own_ref[...] = new_spread_ref[row_ref[0]]
    alpha_t = alpha.T
    wide = [
        jnp.concatenate(
            [got_ref[k, STRIP * b : STRIP * b + STRIP, :] for k in range(COLS)], axis=0
        ).T
        for b in range(2)
    ]

    def advance(image, res, pick):
        direction = res
        if not first:
            image = image + exact_dot(beta_t, pick(img_ref), NN)
            direction = direction + exact_dot(beta_t, pick(dir_ref), NN)
        return res - exact_dot(alpha_t, image, NN), image, direction

    if last:
        for b in range(2):
            keep_ref[b] = wide[b]
        start = pl.multiple_of(SMP * (mine // 2), SMP)
        res = res_ref[mine]
        image = keep_ref[mine % 2, pl.ds(start, SMP), :] + reg_ref[mine][0:1, :] * res
        new_res, _, direction = advance(image, res, lambda ref: ref[mine])
    else:
        image = jnp.concatenate(
            [
                wide[b % 2][SMP * (b // 2) : SMP * (b // 2) + SMP, :]
                + reg_ref[b, 0:1, :] * res_ref[b]
                for b in range(BLKS)
            ],
            axis=1,
        )
        new_res, image, direction = advance(image, flat(res_ref), flat)
        for b in range(BLKS):
            cut = slice(LANE * b, LANE * b + LANE)
            new_res_ref[b] = new_res[:, cut]
            new_img_ref[b] = image[:, cut]
            new_dir_ref[b] = direction[:, cut]
        direction = new_dir_ref[mine]
    new_sol = exact_dot(alpha_t, direction, NN)
    if not first:
        new_sol = sol_ref[...] + new_sol
    if last:
        shift = (LANE - PIECE * (col_ref[0] % 4)) % LANE
        out_sol_ref[...] = pltpu.roll(new_sol, shift, 1)[:, 0:PIECE].T
        out_res_ref[...] = pltpu.roll(new_res, shift, 1)[:, 0:PIECE].T
    else:
        new_sol_ref[...] = new_sol


def body(right_side, regular, curvature, block_rows, block_cols, block_counts):
    sources = block_rows.shape[1]
    pixels = OWN * sources
    curv = curvature.reshape(sources, LANE, LANE)
    tables = [table.reshape(1, sources) for table in (block_rows, block_cols, block_counts)]
    field = ((BLKS, SMP, LANE), F32)
    small = ((SMP, SMP), F32)
    own_share = ((OWN, LANE), F32)
    spread_share = ((sources, OWN, LANE), F32)
    msg = ((COLS, OWN + 8, LANE), F32)
    start = ((COLS, STRIP * sources + NOTES, LANE), BF16)
    dense = ((2 * BLKS, pixels, LANE), BF16)

    (packed,) = call(pack_kernel, [VMEM] * 6, [start], [], "pack", near=False)(
        right_side.T, regular.reshape(1, PIECE), *tables, curv
    )
    col_here = lax.axis_index(COL).astype(jnp.int32).reshape(1)
    row_here = lax.axis_index(ROW).astype(jnp.int32).reshape(1)
    packed, col_here, row_here = lax.optimization_barrier((packed, col_here, row_here))
    packed = swap(packed, COL)
    res, reg, own, own_reg, out = call(
        unpack_kernel,
        [SMEM, VMEM],
        [field, ((BLKS, 8, LANE), F32), own_share, own_share, spread_share],
        [pltpu.VMEM((2, LANE, LANE), F32)],
        "unpack",
    )(col_here, packed)
    spread = swap(out, ROW)
    places = packed[:, STRIP * sources + 51, 0:sources].astype(jnp.int32)
    high, low = call(
        dense_kernel,
        [SMEM, VMEM],
        [dense, dense],
        [pltpu.VMEM(dense[0], F32)],
        "dense",
    )(places, packed)
    state, spread_img = [], []
    for step in range(ITERS):
        first, last = step == 0, step == ITERS - 1
        before = [] if first else [state[1], state[0]]
        (part,) = call(
            functools.partial(product_kernel, first),
            [VMEM] * (5 + len(before)),
            [msg],
            [],
            f"product_{step}",
        )(spread, high, low, res, reg, *before)
        out, piece = call(
            functools.partial(col_sum_kernel, last),
            [VMEM] * 3,
            [((sources, 8 if last else OWN + 8, LANE), F32), own_share],
            [],
            f"col_sum_{step}",
        )(swap(part, COL), own, own_reg)
        fresh = swap(out, ROW)
        (whole,) = call(row_sum_kernel, [VMEM] * 2, [msg], [], f"row_sum_{step}")(fresh, piece)
        got = swap(whole, COL)
        solve = functools.partial(solve_kernel, first, last)
        if last:
            share = ((PIECE, SMP), F32)
            keep = pltpu.VMEM((2, LANE, LANE), F32)
            shares = call(
                solve,
                [SMEM] * 2 + [VMEM] * (3 + len(state)),
                [share, share],
                [keep],
                f"solve_{step}",
                jax.ShapeDtypeStruct,
            )(col_here, row_here, got, res, reg, *state)
            return tuple(part.T for part in shares)
        inputs = [got, res, reg, *state, spread, fresh, *spread_img]
        outs = [field] * 3 + [((SMP, LANE), F32)] + [small] * 2 + [spread_share] * 2 + [own_share]
        res, *state, spread, img, own = call(
            solve, [SMEM] * 2 + [VMEM] * len(inputs), outs, [], f"solve_{step}"
        )(col_here, row_here, *inputs)
        spread_img = [img]


def solution(mesh):
    finer = Mesh(mesh.devices.reshape(8, 4, 8, 2), ROW_COL)
    placed = (
        P(None, ROW_COL),
        P(ROW_COL),
        P(ROW, None, COL, None, None),
        P(ROW, None, COL),
        P(ROW, None, COL),
        P(ROW, None, COL),
    )
    return jax.shard_map(
        body,
        mesh=finer,
        in_specs=placed,
        out_specs=(P(None, ROW_COL), P(None, ROW_COL)),
        check_vma=False,
    )
```

```python
import functools

import jax
import jax.numpy as jnp
from jax import lax
from jax.experimental import pallas as pl
from jax.experimental.pallas import tpu as pltpu
from jax.sharding import Mesh
from jax.sharding import PartitionSpec as P

ITERS = 3
COL = ("col_0", "col_1")
ROW = ("row_0", "row_1")
ROW_COL = ROW + COL
F32 = jnp.float32
BF16 = jnp.bfloat16
SMP = 64
LANE = 128
BLKS = 4
COLS = 16
PIECE = 32
STRIP = 8
OWN = 2 * STRIP
GRANT = 16 * 2**20
NOTES = 56
NT = (((1,), (1,)), ((), ()))
NN = (((1,), (0,)), ((), ()))
VMEM = pl.BlockSpec(memory_space=pltpu.VMEM)
SMEM = pl.BlockSpec(memory_space=pltpu.SMEM)


def exact_dot(left, right, dims):
    return lax.dot_general(
        left, right, dims, precision=lax.Precision.HIGHEST, preferred_element_type=F32
    )


def swap(msg, axes):
    return lax.all_to_all(msg, axes, 0, 0, tiled=True)


def call(kernel, in_specs, outs, scratch, name, make=pltpu.VMEM, near=True):
    run = pl.pallas_call(
        kernel,
        in_specs=in_specs,
        out_specs=[VMEM] * len(outs),
        out_shape=[make(s, d) for s, d in outs],
        scratch_shapes=scratch,
        compiler_params=pltpu.CompilerParams(vmem_limit_bytes=GRANT if near else None),
        name=name,
    )

    def placed(*args):
        if near:
            args = [
                pltpu.with_memory_space_constraint(arg, pltpu.VMEM) if spec is VMEM else arg
                for spec, arg in zip(in_specs, args, strict=True)
            ]
        return run(*args)

    return placed


def thirds(value):
    high = value.astype(BF16).astype(F32)
    middle = (value - high).astype(BF16).astype(F32)
    return high, middle, value - high - middle


def pack_kernel(right_ref, reg_ref, rows_ref, cols_ref, counts_ref, curv_ref, out_ref):
    sources = curv_ref.shape[0]
    base = STRIP * sources
    for s in range(sources):
        flipped = curv_ref[s].astype(F32).T
        for k in range(COLS):
            strip = flipped[STRIP * k : STRIP * k + STRIP, :].astype(BF16)
            out_ref[k, STRIP * s : STRIP * s + STRIP, :] = strip
    right = right_ref[...].T
    packed = jnp.concatenate([right[16 * j : 16 * j + 16, :] for j in range(4)], axis=1)
    cols = cols_ref[...]
    place = ((cols // 2) * BLKS + rows_ref[...]) * 2 + cols % 2
    place = jnp.where(counts_ref[...] > 0, place, -1).astype(F32)
    lines = [*thirds(reg_ref[...]), place]
    lines.append(jnp.zeros((8 - len(lines), PIECE), F32))
    notes = jnp.concatenate(lines, axis=0)
    notes = jnp.concatenate([notes, jnp.zeros((8, LANE - PIECE), F32)], axis=1)
    tiles = [tile.astype(BF16) for tile in (*thirds(packed), notes)]
    for k in range(COLS):
        for i, tile in enumerate(tiles):
            out_ref[k, base + 16 * i : base + 16 * i + tile.shape[0], :] = tile


def pixel_rows(fields):
    return [jnp.concatenate([fields[b].T, fields[2 + b].T], axis=1) for b in range(2)]


def unpack_kernel(place_ref, got_ref, res_ref, reg_ref, own_ref, own_reg_ref, out_ref, tall_ref):
    base = got_ref.shape[1] - NOTES
    packed, notes = [], []
    for k in range(COLS):
        parts = [got_ref[k, base + 16 * i : base + 16 * i + 16, :].astype(F32) for i in range(3)]
        packed.append(parts[0] + parts[1] + parts[2])
        note = got_ref[k, base + 48 : base + NOTES, :].astype(F32)
        notes.append(note[0:1] + note[1:2] + note[2:3])
    group = lax.broadcasted_iota(jnp.int32, (16, LANE), 1) // PIECE
    fields, regs = [], []
    for b in range(BLKS):
        pieces = []
        for j in range(4):
            piece = jnp.zeros((16, LANE), F32)
            for m in range(4):
                shift = (PIECE * (m - j)) % LANE
                part = packed[4 * b + m]
                part = pltpu.roll(part, shift, 1) if shift else part
                piece = jnp.where(group == m, part, piece)
            pieces.append(piece)
        fields.append(jnp.concatenate(pieces, axis=0))
        reg = jnp.zeros((8, LANE), F32)
        for m in range(4):
            part = jnp.broadcast_to(notes[4 * b + m], (8, LANE))
            part = pltpu.roll(part, PIECE * m, 1) if m else part
            reg = jnp.where(group[0:8] == m, part, reg)
        regs.append(jnp.broadcast_to(reg[0:1], (SMP, LANE)))
        res_ref[b] = fields[b]
        reg_ref[b] = reg
    start = pl.multiple_of(place_ref[0] * STRIP, STRIP)
    for target, values in ((own_ref, fields), (own_reg_ref, regs)):
        for b, tall in enumerate(pixel_rows(values)):
            tall_ref[b] = tall
            target[STRIP * b : STRIP * b + STRIP, :] = tall_ref[b, pl.ds(start, STRIP), :]
    own = own_ref[...]
    for r in range(out_ref.shape[0]):
        out_ref[r] = own


def dense_kernel(place_ref, got_ref, high_ref, low_ref, sum_ref):
    sources = place_ref.shape[1]
    sum_ref[...] = jnp.zeros_like(sum_ref)
    for s in range(sources):
        for k in range(COLS):
            place = place_ref[k, s]
            strip = got_ref[k, STRIP * s : STRIP * s + STRIP, :].astype(F32)
            strip = jnp.where(place >= 0, strip, 0.0)
            spot = jnp.maximum(place, 0)
            plane = spot // 2
            rows = pl.ds(pl.multiple_of(OWN * s + STRIP * (spot % 2), STRIP), STRIP)
            sum_ref[plane, rows, :] = sum_ref[plane, rows, :] + strip
    for plane in range(2 * BLKS):
        total = sum_ref[plane]
        high = total.astype(BF16)
        high_ref[plane] = high
        low_ref[plane] = (total - high.astype(F32)).astype(BF16)


def flat(field_ref):
    return jnp.concatenate([field_ref[b] for b in range(BLKS)], axis=1)


def product_kernel(first, last, *refs):
    spread_ref, high_ref, low_ref, res_ref, reg_ref = refs[:5]
    if first:
        (out_ref,) = refs[5:]
    else:
        img_ref, dir_ref, out_ref = refs[5:]
    pixels = OWN * spread_ref.shape[0]
    spread = spread_ref[...].reshape(pixels, LANE)
    inputs = jnp.concatenate(
        [spread[LANE * i : LANE * i + LANE, :].T for i in range(pixels // LANE)], axis=1
    )
    top = inputs.astype(BF16)
    low = (inputs - top.astype(F32)).astype(BF16)
    coupled = []
    for b in range(BLKS):
        acc = jnp.zeros((SMP, LANE), F32)
        for half in range(2):
            cut = slice(SMP * half, SMP * half + SMP)
            plane = BLKS * half + b
            left = top[cut] if first else jnp.concatenate([top[cut], low[cut]], axis=0)
            main = lax.dot_general(left, high_ref[plane], NN, preferred_element_type=F32)
            acc += main if first else main[0:SMP] + main[SMP:]
            acc += lax.dot_general(top[cut], low_ref[plane], NN, preferred_element_type=F32)
        coupled.append(acc)
    share = 1.0 / COLS
    res = flat(res_ref)
    part = jnp.concatenate(
        [coupled[b] + reg_ref[b, 0:1, :] * res_ref[b] * share for b in range(BLKS)], axis=1
    )
    pair = exact_dot(res, jnp.concatenate([part, res * share], axis=0), NT)
    if first:
        mixed = jnp.zeros((SMP, SMP), F32)
    else:
        left = jnp.concatenate([res, part], axis=1)
        right = jnp.concatenate([flat(img_ref) * share, flat(dir_ref)], axis=1)
        mixed = exact_dot(left, right, NT)
    other = jnp.concatenate([mixed, jnp.zeros((SMP, LANE - SMP), F32)], axis=1)
    tall = [field.T for field in coupled] if last else pixel_rows(coupled)
    for k in range(COLS):
        if last:
            m = PIECE * (k % 4)
            near, far = tall[k // 4][m : m + 16], tall[k // 4][m + 16 : m + 32]
            out_ref[k, 0:OWN, :] = jnp.concatenate([near, far], axis=1)
        else:
            for b in range(2):
                strip = tall[b][STRIP * k : STRIP * k + STRIP]
                out_ref[k, STRIP * b : STRIP * b + STRIP, :] = strip
        source = pair if k < 8 else other
        n = k % 8
        out_ref[k, OWN : OWN + 8, :] = source[8 * n : 8 * n + 8, :]


def col_sum_kernel(last, got_ref, own_ref, own_reg_ref, out_ref, piece_ref):
    total = got_ref[0]
    for k in range(1, COLS):
        total = total + got_ref[k]
    coupled = total[0:OWN, :]
    piece_ref[...] = coupled
    gram = total[OWN : OWN + 8, :]
    full = coupled + own_reg_ref[...] * own_ref[...]
    for r in range(out_ref.shape[0]):
        if last:
            out_ref[r] = gram
        else:
            out_ref[r, 0:OWN, :] = full
            out_ref[r, OWN : OWN + 8, :] = gram


def row_sum_kernel(last, got_ref, *refs):
    top = got_ref.shape[1] - 8
    total = got_ref[0, top:, :]
    for r in range(1, got_ref.shape[0]):
        total = total + got_ref[r, top:, :]
    if last:
        (out_ref,) = refs
    else:
        piece_ref, out_ref = refs
        piece = piece_ref[...]
    for k in range(COLS):
        if last:
            out_ref[k] = total
        else:
            out_ref[k, 0:OWN, :] = piece
            out_ref[k, OWN : OWN + 8, :] = total


def solve_systems(systems, width):
    row_id = lax.broadcasted_iota(jnp.int32, (8, LANE), 0)
    work = []
    for matrix, rhs in systems:
        wide = jnp.concatenate([matrix, rhs], axis=1)
        work.append([wide[8 * t : 8 * t + 8, :] for t in range(8)])
    for j in range(0, SMP, width):
        top, low = divmod(j, 8)
        for tiles in work:
            columns = [
                [
                    jnp.broadcast_to(tile[:, j + i : j + i + 1], (8, LANE))
                    for i in range(width)
                ]
                for tile in tiles
            ]
            rows = [tiles[top][low + i : low + i + 1, :] for i in range(width)]
            block = [
                [columns[top][c][low + r : low + r + 1, :] for c in range(width)]
                for r in range(width)
            ]
            recip, lower = [], {}
            for a in range(width):
                recip.append(1.0 / block[a][a])
                for r in range(a + 1, width):
                    lower[r, a] = block[r][a] * recip[a]
                    rows[r] = rows[r] - lower[r, a] * rows[a]
                    for c in range(a + 1, width):
                        block[r][c] = block[r][c] - lower[r, a] * block[a][c]
            for a in reversed(range(width)):
                rows[a] = rows[a] * recip[a]
                for r in range(a + 1, width):
                    rows[a] = rows[a] - lower[r, a] * rows[r]
            for t in range(8):
                tile = tiles[t]
                for i in range(width):
                    tile = tile - columns[t][i] * rows[i]
                if t == top:
                    for i in range(width):
                        tile = jnp.where(row_id == low + i, rows[i], tile)
                tiles[t] = tile
    return [pltpu.roll(jnp.concatenate(tiles, axis=0), SMP, 1)[:, 0:SMP] for tiles in work]


def both_halves(matrix):
    zero = jnp.zeros((SMP, SMP), F32)
    upper = jnp.concatenate([matrix, zero], axis=1)
    lower = jnp.concatenate([zero, matrix], axis=1)
    return jnp.concatenate([upper, lower], axis=0)


def solve_kernel(first, last, *refs):
    refs = list(refs)
    col_ref, row_ref, got_ref, res_ref, reg_ref = refs[:5]
    refs = refs[5:]
    mine = col_ref[0] // 4
    if not first:
        dir_ref, img_ref, sol_ref, inv_ref, curv_ref = refs[:5]
        refs = refs[5:]
    if last:
        piece_ref, out_sol_ref, out_res_ref = refs
    else:
        spread_ref, fresh_ref = refs[:2]
        refs = refs[2:]
        if not first:
            spread_img_ref = refs.pop(0)
        new_res_ref, new_dir_ref, new_img_ref, new_sol_ref = refs[:4]
        new_inv_ref, new_curv_ref, new_spread_ref, new_spread_img_ref, own_ref = refs[4:]
    base = got_ref.shape[1] - 8
    pair = jnp.concatenate([got_ref[k, base:, :] for k in range(8)], axis=0)
    gram = pltpu.roll(pair, SMP, 1)[:, 0:SMP]
    curv = pair[:, 0:SMP]
    if not first:
        mixed = jnp.concatenate([got_ref[k, base:, :] for k in range(8, 16)], axis=0)
        mixed = mixed[:, 0:SMP]
        beta_t = exact_dot(gram, inv_ref[...], NN)
        curv = curv + exact_dot(mixed + exact_dot(beta_t, curv_ref[...], NN), beta_t, NT)
    curv = 0.5 * (curv + curv.T)
    if last:
        (alpha,) = solve_systems([(curv, gram)], 8)
    else:
        square = (SMP, SMP)
        same = lax.broadcasted_iota(jnp.int32, square, 0) == lax.broadcasted_iota(
            jnp.int32, square, 1
        )
        alpha, inverse = solve_systems([(curv, gram), (gram, same.astype(F32))], 8)
        new_inv_ref[...] = inverse
        new_curv_ref[...] = curv
        sources = spread_ref.shape[0]
        pixels = OWN * sources
        spread_img = fresh_ref[:, 0:OWN, :].reshape(pixels, LANE)
        if not first:
            old = spread_img_ref[...].reshape(pixels, LANE)
            spread_img = spread_img + exact_dot(old, both_halves(beta_t.T), NN)
        spread = spread_ref[...].reshape(pixels, LANE)
        spread = spread - exact_dot(spread_img, both_halves(alpha), NN)
        new_spread_ref[...] = spread.reshape(sources, OWN, LANE)
        new_spread_img_ref[...] = spread_img.reshape(sources, OWN, LANE)
        own_ref[...] = new_spread_ref[row_ref[0]]
    if last:
        shift = (LANE - PIECE * (col_ref[0] % 4)) % LANE

        def cut(rows):
            return pltpu.roll(rows, shift, 1)[:, 0:PIECE].T

        res = cut(res_ref[mine])
        reg = cut(jnp.broadcast_to(reg_ref[mine][0:1, :], (SMP, LANE)))
        piece = piece_ref[...]
        halves = [piece[:, 0:SMP], pltpu.roll(piece, SMP, 1)[:, 0:SMP]]
        image = jnp.concatenate(halves, axis=0) + reg * res
        image = image + exact_dot(cut(img_ref[mine]), beta_t, NT)
        direction = res + exact_dot(cut(dir_ref[mine]), beta_t, NT)
        out_sol_ref[...] = cut(sol_ref[...]) + exact_dot(direction, alpha, NN)
        out_res_ref[...] = res - exact_dot(image, alpha, NN)
        return
    alpha_t = alpha.T
    wide = [
        jnp.concatenate(
            [got_ref[k, STRIP * b : STRIP * b + STRIP, :] for k in range(COLS)], axis=0
        ).T
        for b in range(2)
    ]
    res = flat(res_ref)
    direction = res
    image = jnp.concatenate(
        [
            wide[b % 2][SMP * (b // 2) : SMP * (b // 2) + SMP, :] + reg_ref[b, 0:1, :] * res_ref[b]
            for b in range(BLKS)
        ],
        axis=1,
    )
    if not first:
        image = image + exact_dot(beta_t, flat(img_ref), NN)
        direction = direction + exact_dot(beta_t, flat(dir_ref), NN)
    new_res = res - exact_dot(alpha_t, image, NN)
    for b in range(BLKS):
        part = slice(LANE * b, LANE * b + LANE)
        new_res_ref[b] = new_res[:, part]
        new_img_ref[b] = image[:, part]
        new_dir_ref[b] = direction[:, part]
    new_sol = exact_dot(alpha_t, new_dir_ref[mine], NN)
    new_sol_ref[...] = new_sol if first else sol_ref[...] + new_sol


def body(right_side, regular, curvature, block_rows, block_cols, block_counts):
    sources = block_rows.shape[1]
    pixels = OWN * sources
    curv = curvature.reshape(sources, LANE, LANE)
    tables = [table.reshape(1, sources) for table in (block_rows, block_cols, block_counts)]
    field = ((BLKS, SMP, LANE), F32)
    small = ((SMP, SMP), F32)
    own_share = ((OWN, LANE), F32)
    spread_share = ((sources, OWN, LANE), F32)
    msg = ((COLS, OWN + 8, LANE), F32)
    start = ((COLS, STRIP * sources + NOTES, LANE), BF16)
    dense = ((2 * BLKS, pixels, LANE), BF16)

    (packed,) = call(pack_kernel, [VMEM] * 6, [start], [], "pack", near=False)(
        right_side.T, regular.reshape(1, PIECE), *tables, curv
    )
    col_here = lax.axis_index(COL).astype(jnp.int32).reshape(1)
    row_here = lax.axis_index(ROW).astype(jnp.int32).reshape(1)
    packed, col_here, row_here = lax.optimization_barrier((packed, col_here, row_here))
    packed = swap(packed, COL)
    res, reg, own, own_reg, out = call(
        unpack_kernel,
        [SMEM, VMEM],
        [field, ((BLKS, 8, LANE), F32), own_share, own_share, spread_share],
        [pltpu.VMEM((2, LANE, LANE), F32)],
        "unpack",
    )(col_here, packed)
    spread = swap(out, ROW)
    places = packed[:, STRIP * sources + 51, 0:sources].astype(jnp.int32)
    high, low = call(
        dense_kernel,
        [SMEM, VMEM],
        [dense, dense],
        [pltpu.VMEM(dense[0], F32)],
        "dense",
    )(places, packed)
    state, spread_img = [], []
    for step in range(ITERS):
        first, last = step == 0, step == ITERS - 1
        before = [] if first else [state[1], state[0]]
        (part,) = call(
            functools.partial(product_kernel, first, last),
            [VMEM] * (5 + len(before)),
            [msg],
            [],
            f"product_{step}",
        )(spread, high, low, res, reg, *before)
        out, piece = call(
            functools.partial(col_sum_kernel, last),
            [VMEM] * 3,
            [((sources, 8 if last else OWN + 8, LANE), F32), own_share],
            [],
            f"col_sum_{step}",
        )(swap(part, COL), own, own_reg)
        fresh = swap(out, ROW)
        pieces = [] if last else [piece]
        (whole,) = call(
            functools.partial(row_sum_kernel, last),
            [VMEM] * (1 + len(pieces)),
            [((COLS, 8, LANE), F32) if last else msg],
            [],
            f"row_sum_{step}",
        )(fresh, *pieces)
        got = swap(whole, COL)
        solve = functools.partial(solve_kernel, first, last)
        if last:
            share = ((PIECE, SMP), F32)
            shares = call(
                solve,
                [SMEM] * 2 + [VMEM] * (4 + len(state)),
                [share, share],
                [],
                f"solve_{step}",
                jax.ShapeDtypeStruct,
            )(col_here, row_here, got, res, reg, *state, piece)
            return tuple(part.T for part in shares)
        inputs = [got, res, reg, *state, spread, fresh, *spread_img]
        outs = [field] * 3 + [((SMP, LANE), F32)] + [small] * 2 + [spread_share] * 2 + [own_share]
        res, *state, spread, img, own = call(
            solve, [SMEM] * 2 + [VMEM] * len(inputs), outs, [], f"solve_{step}"
        )(col_here, row_here, *inputs)
        spread_img = [img]


def solution(mesh):
    finer = Mesh(mesh.devices.reshape(8, 4, 8, 2), ROW_COL)
    placed = (
        P(None, ROW_COL),
        P(ROW_COL),
        P(ROW, None, COL, None, None),
        P(ROW, None, COL),
        P(ROW, None, COL),
        P(ROW, None, COL),
    )
    return jax.shard_map(
        body,
        mesh=finer,
        in_specs=placed,
        out_specs=(P(None, ROW_COL), P(None, ROW_COL)),
        check_vma=False,
    )
```

```python
import functools

import jax
import jax.numpy as jnp
from jax import lax
from jax.experimental import pallas as pl
from jax.experimental.pallas import tpu as pltpu
from jax.sharding import Mesh
from jax.sharding import PartitionSpec as P

ITERS = 3
COL = ("col_0", "col_1")
ROW = ("row_0", "row_1")
ROW_COL = ROW + COL
F32 = jnp.float32
BF16 = jnp.bfloat16
SMP = 64
LANE = 128
BLKS = 4
COLS = 16
PIECE = 32
STRIP = 8
OWN = 2 * STRIP
GRANT = 16 * 2**20
NOTES = 56
NT = (((1,), (1,)), ((), ()))
NN = (((1,), (0,)), ((), ()))
VMEM = pl.BlockSpec(memory_space=pltpu.VMEM)
SMEM = pl.BlockSpec(memory_space=pltpu.SMEM)


def exact_dot(left, right, dims):
    return lax.dot_general(
        left, right, dims, precision=lax.Precision.HIGHEST, preferred_element_type=F32
    )


def close_dot(left, right):
    heads = [side.astype(BF16) for side in (left, right)]
    tails = [
        (side - head.astype(F32)).astype(BF16)
        for side, head in zip((left, right), heads, strict=True)
    ]

    def dot(a, b):
        return lax.dot_general(a, b, NN, preferred_element_type=F32)

    return dot(heads[0], heads[1]) + (dot(tails[0], heads[1]) + dot(heads[0], tails[1]))


def swap(msg, axes):
    return lax.all_to_all(msg, axes, 0, 0, tiled=True)


def call(kernel, in_specs, outs, scratch, name, make=pltpu.VMEM, near=True):
    run = pl.pallas_call(
        kernel,
        in_specs=in_specs,
        out_specs=[VMEM] * len(outs),
        out_shape=[make(s, d) for s, d in outs],
        scratch_shapes=scratch,
        compiler_params=pltpu.CompilerParams(vmem_limit_bytes=GRANT if near else None),
        name=name,
    )

    def placed(*args):
        if near:
            args = [
                pltpu.with_memory_space_constraint(arg, pltpu.VMEM) if spec is VMEM else arg
                for spec, arg in zip(in_specs, args, strict=True)
            ]
        return run(*args)

    return placed


def thirds(value):
    high = value.astype(BF16).astype(F32)
    middle = (value - high).astype(BF16).astype(F32)
    return high, middle, value - high - middle


def pack_kernel(right_ref, reg_ref, rows_ref, cols_ref, counts_ref, curv_ref, out_ref):
    sources = curv_ref.shape[0]
    base = STRIP * sources
    for s in range(sources):
        flipped = curv_ref[s].astype(F32).T
        for k in range(COLS):
            strip = flipped[STRIP * k : STRIP * k + STRIP, :].astype(BF16)
            out_ref[k, STRIP * s : STRIP * s + STRIP, :] = strip
    right = right_ref[...].T
    packed = jnp.concatenate([right[16 * j : 16 * j + 16, :] for j in range(4)], axis=1)
    cols = cols_ref[...]
    place = ((cols // 2) * BLKS + rows_ref[...]) * 2 + cols % 2
    place = jnp.where(counts_ref[...] > 0, place, -1).astype(F32)
    lines = [*thirds(reg_ref[...]), place]
    lines.append(jnp.zeros((8 - len(lines), PIECE), F32))
    notes = jnp.concatenate(lines, axis=0)
    notes = jnp.concatenate([notes, jnp.zeros((8, LANE - PIECE), F32)], axis=1)
    tiles = [tile.astype(BF16) for tile in (*thirds(packed), notes)]
    for k in range(COLS):
        for i, tile in enumerate(tiles):
            out_ref[k, base + 16 * i : base + 16 * i + tile.shape[0], :] = tile


def pixel_rows(fields):
    return [jnp.concatenate([fields[b].T, fields[2 + b].T], axis=1) for b in range(2)]


def own_kernel(place_ref, got_ref, own_ref, out_ref, tall_ref):
    base = got_ref.shape[1] - NOTES
    place = place_ref[0]
    strips = []
    for b in range(BLKS):
        parts = [
            got_ref[BLKS * b + place // 4, base + 16 * i : base + 16 * i + 16, :].astype(F32)
            for i in range(3)
        ]
        tall_ref[b] = (parts[0] + parts[1] + parts[2]).T
        start = STRIP * (place % 4)
        pieces = [
            tall_ref[b, pl.ds(pl.multiple_of(PIECE * j + start, STRIP), STRIP), :] for j in range(4)
        ]
        strips.append(jnp.concatenate(pieces, axis=1))
    for b in range(2):
        tile = jnp.concatenate([strips[b], strips[2 + b]], axis=1)
        own_ref[STRIP * b : STRIP * b + STRIP, :] = tile
        for r in range(out_ref.shape[0]):
            out_ref[r, STRIP * b : STRIP * b + STRIP, :] = tile


def unpack_kernel(place_ref, got_ref, res_ref, reg_ref, own_reg_ref, tall_ref):
    base = got_ref.shape[1] - NOTES
    packed, notes = [], []
    for k in range(COLS):
        parts = [got_ref[k, base + 16 * i : base + 16 * i + 16, :].astype(F32) for i in range(3)]
        packed.append(parts[0] + parts[1] + parts[2])
        note = got_ref[k, base + 48 : base + NOTES, :].astype(F32)
        notes.append(note[0:1] + note[1:2] + note[2:3])
    group = lax.broadcasted_iota(jnp.int32, (16, LANE), 1) // PIECE
    fields, regs = [], []
    for b in range(BLKS):
        pieces = []
        for j in range(4):
            piece = jnp.zeros((16, LANE), F32)
            for m in range(4):
                shift = (PIECE * (m - j)) % LANE
                part = packed[4 * b + m]
                part = pltpu.roll(part, shift, 1) if shift else part
                piece = jnp.where(group == m, part, piece)
            pieces.append(piece)
        fields.append(jnp.concatenate(pieces, axis=0))
        reg = jnp.zeros((8, LANE), F32)
        for m in range(4):
            part = jnp.broadcast_to(notes[4 * b + m], (8, LANE))
            part = pltpu.roll(part, PIECE * m, 1) if m else part
            reg = jnp.where(group[0:8] == m, part, reg)
        regs.append(jnp.broadcast_to(reg[0:1], (SMP, LANE)))
        res_ref[b] = fields[b]
        reg_ref[b] = reg
    start = pl.multiple_of(place_ref[0] * STRIP, STRIP)
    for b, tall in enumerate(pixel_rows(regs)):
        tall_ref[b] = tall
        own_reg_ref[STRIP * b : STRIP * b + STRIP, :] = tall_ref[b, pl.ds(start, STRIP), :]


def dense_kernel(place_ref, got_ref, high_ref, low_ref, sum_ref):
    sources = place_ref.shape[1]
    sum_ref[...] = jnp.zeros_like(sum_ref)
    for s in range(sources):
        for k in range(COLS):
            place = place_ref[k, s]
            strip = got_ref[k, STRIP * s : STRIP * s + STRIP, :].astype(F32)
            strip = jnp.where(place >= 0, strip, 0.0)
            spot = jnp.maximum(place, 0)
            plane = spot // 2
            rows = pl.ds(pl.multiple_of(OWN * s + STRIP * (spot % 2), STRIP), STRIP)
            sum_ref[plane, rows, :] = sum_ref[plane, rows, :] + strip
    for plane in range(2 * BLKS):
        total = sum_ref[plane]
        high = total.astype(BF16)
        high_ref[plane] = high
        low_ref[plane] = (total - high.astype(F32)).astype(BF16)


def flat(field_ref):
    return jnp.concatenate([field_ref[b] for b in range(BLKS)], axis=1)


def product_kernel(first, last, *refs):
    spread_ref, high_ref, low_ref, res_ref, reg_ref = refs[:5]
    if first:
        (out_ref,) = refs[5:]
    else:
        img_ref, dir_ref, out_ref = refs[5:]
    pixels = OWN * spread_ref.shape[0]
    spread = spread_ref[...].reshape(pixels, LANE)
    inputs = jnp.concatenate(
        [spread[LANE * i : LANE * i + LANE, :].T for i in range(pixels // LANE)], axis=1
    )
    top = inputs.astype(BF16)
    low = (inputs - top.astype(F32)).astype(BF16)
    coupled = []
    for b in range(BLKS):
        acc = jnp.zeros((SMP, LANE), F32)
        for half in range(2):
            cut = slice(SMP * half, SMP * half + SMP)
            plane = BLKS * half + b
            left = top[cut] if first else jnp.concatenate([top[cut], low[cut]], axis=0)
            main = lax.dot_general(left, high_ref[plane], NN, preferred_element_type=F32)
            acc += main if first else main[0:SMP] + main[SMP:]
            acc += lax.dot_general(top[cut], low_ref[plane], NN, preferred_element_type=F32)
        coupled.append(acc)
    share = 1.0 / COLS
    res = flat(res_ref)
    part = jnp.concatenate(
        [coupled[b] + reg_ref[b, 0:1, :] * res_ref[b] * share for b in range(BLKS)], axis=1
    )
    pair = exact_dot(res, jnp.concatenate([part, res * share], axis=0), NT)
    if first:
        mixed = jnp.zeros((SMP, SMP), F32)
    else:
        left = jnp.concatenate([res, part], axis=1)
        right = jnp.concatenate([flat(img_ref) * share, flat(dir_ref)], axis=1)
        mixed = exact_dot(left, right, NT)
    other = jnp.concatenate([mixed, jnp.zeros((SMP, LANE - SMP), F32)], axis=1)
    tall = [field.T for field in coupled] if last else pixel_rows(coupled)
    for k in range(COLS):
        if last:
            m = PIECE * (k % 4)
            near, far = tall[k // 4][m : m + 16], tall[k // 4][m + 16 : m + 32]
            out_ref[k, 0:OWN, :] = jnp.concatenate([near, far], axis=1)
        else:
            for b in range(2):
                strip = tall[b][STRIP * k : STRIP * k + STRIP]
                out_ref[k, STRIP * b : STRIP * b + STRIP, :] = strip
        source = pair if k < 8 else other
        n = k % 8
        out_ref[k, OWN : OWN + 8, :] = source[8 * n : 8 * n + 8, :]


def col_sum_kernel(last, got_ref, own_ref, own_reg_ref, out_ref, piece_ref):
    total = got_ref[0]
    for k in range(1, COLS):
        total = total + got_ref[k]
    coupled = total[0:OWN, :]
    piece_ref[...] = coupled
    gram = total[OWN : OWN + 8, :]
    full = coupled + own_reg_ref[...] * own_ref[...]
    for r in range(out_ref.shape[0]):
        if last:
            out_ref[r] = gram
        else:
            out_ref[r, 0:OWN, :] = full
            out_ref[r, OWN : OWN + 8, :] = gram


def row_sum_kernel(last, got_ref, *refs):
    top = got_ref.shape[1] - 8
    total = got_ref[0, top:, :]
    for r in range(1, got_ref.shape[0]):
        total = total + got_ref[r, top:, :]
    if last:
        (out_ref,) = refs
    else:
        piece_ref, out_ref = refs
        piece = piece_ref[...]
    for k in range(COLS):
        if last:
            out_ref[k] = total
        else:
            out_ref[k, 0:OWN, :] = piece
            out_ref[k, OWN : OWN + 8, :] = total


def solve_systems(systems, width):
    row_id = lax.broadcasted_iota(jnp.int32, (8, LANE), 0)
    work = []
    for matrix, rhs in systems:
        wide = jnp.concatenate([matrix, rhs], axis=1)
        work.append([wide[8 * t : 8 * t + 8, :] for t in range(8)])
    for j in range(0, SMP, width):
        top, low = divmod(j, 8)
        for tiles in work:
            columns = [
                [
                    jnp.broadcast_to(tile[:, j + i : j + i + 1], (8, LANE))
                    for i in range(width)
                ]
                for tile in tiles
            ]
            rows = [tiles[top][low + i : low + i + 1, :] for i in range(width)]
            block = [
                [columns[top][c][low + r : low + r + 1, :] for c in range(width)]
                for r in range(width)
            ]
            recip, lower = [], {}
            for a in range(width):
                recip.append(1.0 / block[a][a])
                for r in range(a + 1, width):
                    lower[r, a] = block[r][a] * recip[a]
                    rows[r] = rows[r] - lower[r, a] * rows[a]
                    for c in range(a + 1, width):
                        block[r][c] = block[r][c] - lower[r, a] * block[a][c]
            for a in reversed(range(width)):
                rows[a] = rows[a] * recip[a]
                for r in range(a + 1, width):
                    rows[a] = rows[a] - lower[r, a] * rows[r]
            for t in range(8):
                tile = tiles[t]
                for i in range(width):
                    tile = tile - columns[t][i] * rows[i]
                if t == top:
                    for i in range(width):
                        tile = jnp.where(row_id == low + i, rows[i], tile)
                tiles[t] = tile
    return [pltpu.roll(jnp.concatenate(tiles, axis=0), SMP, 1)[:, 0:SMP] for tiles in work]


def both_halves(matrix):
    zero = jnp.zeros((SMP, SMP), F32)
    upper = jnp.concatenate([matrix, zero], axis=1)
    lower = jnp.concatenate([zero, matrix], axis=1)
    return jnp.concatenate([upper, lower], axis=0)


def solve_kernel(first, last, *refs):
    refs = list(refs)
    col_ref, row_ref, got_ref, res_ref, reg_ref = refs[:5]
    refs = refs[5:]
    mine = col_ref[0] // 4
    if not first:
        dir_ref, img_ref, sol_ref, lead_ref = refs[:4]
        refs = refs[4:]
    if last:
        piece_ref, out_sol_ref, out_res_ref = refs
    else:
        spread_ref, fresh_ref = refs[:2]
        refs = refs[2:]
        if not first:
            spread_img_ref = refs.pop(0)
        new_res_ref, new_dir_ref, new_img_ref, new_sol_ref = refs[:4]
        new_lead_ref, new_spread_ref, new_spread_img_ref, own_ref = refs[4:]
    base = got_ref.shape[1] - 8
    pair = jnp.concatenate([got_ref[k, base:, :] for k in range(8)], axis=0)
    gram = pltpu.roll(pair, SMP, 1)[:, 0:SMP]
    curv = pair[:, 0:SMP]
    if not first:
        mixed = jnp.concatenate([got_ref[k, base:, :] for k in range(8, 16)], axis=0)
        mixed = mixed[:, 0:SMP]
        both = exact_dot(gram, lead_ref[...], NN)
        beta_t = both[:, 0:SMP]
        curv = curv + exact_dot(mixed + pltpu.roll(both, SMP, 1)[:, 0:SMP], beta_t, NT)
    curv = 0.5 * (curv + curv.T)
    if last:
        (alpha,) = solve_systems([(curv, gram)], 8)
    else:
        square = (SMP, SMP)
        same = lax.broadcasted_iota(jnp.int32, square, 0) == lax.broadcasted_iota(
            jnp.int32, square, 1
        )
        alpha, inverse = solve_systems([(curv, gram), (gram, same.astype(F32))], 8)
        new_lead_ref[...] = jnp.concatenate([inverse, exact_dot(inverse, curv, NN)], axis=1)
        sources = spread_ref.shape[0]
        pixels = OWN * sources
        spread_img = fresh_ref[:, 0:OWN, :].reshape(pixels, LANE)
        if not first:
            old = spread_img_ref[...].reshape(pixels, LANE)
            spread_img = spread_img + close_dot(old, both_halves(beta_t.T))
        spread = spread_ref[...].reshape(pixels, LANE)
        spread = spread - close_dot(spread_img, both_halves(alpha))
        new_spread_ref[...] = spread.reshape(sources, OWN, LANE)
        new_spread_img_ref[...] = spread_img.reshape(sources, OWN, LANE)
        own_ref[...] = new_spread_ref[row_ref[0]]
    if last:
        shift = (LANE - PIECE * (col_ref[0] % 4)) % LANE

        def cut(rows):
            return pltpu.roll(rows, shift, 1)[:, 0:PIECE].T

        res = cut(res_ref[mine])
        reg = cut(jnp.broadcast_to(reg_ref[mine][0:1, :], (SMP, LANE)))
        piece = piece_ref[...]
        halves = [piece[:, 0:SMP], pltpu.roll(piece, SMP, 1)[:, 0:SMP]]
        image = jnp.concatenate(halves, axis=0) + reg * res
        image = image + exact_dot(cut(img_ref[mine]), beta_t, NT)
        direction = res + exact_dot(cut(dir_ref[mine]), beta_t, NT)
        out_sol_ref[...] = cut(sol_ref[...]) + exact_dot(direction, alpha, NN)
        out_res_ref[...] = res - exact_dot(image, alpha, NN)
        return
    alpha_t = alpha.T
    wide = [
        jnp.concatenate(
            [got_ref[k, STRIP * b : STRIP * b + STRIP, :] for k in range(COLS)], axis=0
        ).T
        for b in range(2)
    ]
    res = flat(res_ref)
    direction = res
    image = jnp.concatenate(
        [
            wide[b % 2][SMP * (b // 2) : SMP * (b // 2) + SMP, :] + reg_ref[b, 0:1, :] * res_ref[b]
            for b in range(BLKS)
        ],
        axis=1,
    )
    if not first:
        image = image + exact_dot(beta_t, flat(img_ref), NN)
        direction = direction + exact_dot(beta_t, flat(dir_ref), NN)
    new_res = res - exact_dot(alpha_t, image, NN)
    for b in range(BLKS):
        part = slice(LANE * b, LANE * b + LANE)
        new_res_ref[b] = new_res[:, part]
        new_img_ref[b] = image[:, part]
        new_dir_ref[b] = direction[:, part]
    new_sol = exact_dot(alpha_t, new_dir_ref[mine], NN)
    new_sol_ref[...] = new_sol if first else sol_ref[...] + new_sol


def body(right_side, regular, curvature, block_rows, block_cols, block_counts):
    sources = block_rows.shape[1]
    pixels = OWN * sources
    curv = curvature.reshape(sources, LANE, LANE)
    tables = [table.reshape(1, sources) for table in (block_rows, block_cols, block_counts)]
    field = ((BLKS, SMP, LANE), F32)
    own_share = ((OWN, LANE), F32)
    spread_share = ((sources, OWN, LANE), F32)
    msg = ((COLS, OWN + 8, LANE), F32)
    start = ((COLS, STRIP * sources + NOTES, LANE), BF16)
    dense = ((2 * BLKS, pixels, LANE), BF16)

    (packed,) = call(pack_kernel, [VMEM] * 6, [start], [], "pack", near=False)(
        right_side.T, regular.reshape(1, PIECE), *tables, curv
    )
    col_here = lax.axis_index(COL).astype(jnp.int32).reshape(1)
    row_here = lax.axis_index(ROW).astype(jnp.int32).reshape(1)
    packed, col_here, row_here = lax.optimization_barrier((packed, col_here, row_here))
    packed = swap(packed, COL)
    own, out = call(
        own_kernel,
        [SMEM, VMEM],
        [own_share, spread_share],
        [pltpu.VMEM((BLKS, LANE, 16), F32)],
        "own",
    )(col_here, packed)
    res, reg, own_reg = call(
        unpack_kernel,
        [SMEM, VMEM],
        [field, ((BLKS, 8, LANE), F32), own_share],
        [pltpu.VMEM((2, LANE, LANE), F32)],
        "unpack",
    )(col_here, packed)
    spread = swap(out, ROW)
    places = packed[:, STRIP * sources + 51, 0:sources].astype(jnp.int32)
    high, low = call(
        dense_kernel,
        [SMEM, VMEM],
        [dense, dense],
        [pltpu.VMEM(dense[0], F32)],
        "dense",
    )(places, packed)
    state, spread_img = [], []
    for step in range(ITERS):
        first, last = step == 0, step == ITERS - 1
        before = [] if first else [state[1], state[0]]
        (part,) = call(
            functools.partial(product_kernel, first, last),
            [VMEM] * (5 + len(before)),
            [msg],
            [],
            f"product_{step}",
        )(spread, high, low, res, reg, *before)
        out, piece = call(
            functools.partial(col_sum_kernel, last),
            [VMEM] * 3,
            [((sources, 8 if last else OWN + 8, LANE), F32), own_share],
            [],
            f"col_sum_{step}",
        )(swap(part, COL), own, own_reg)
        fresh = swap(out, ROW)
        pieces = [] if last else [piece]
        (whole,) = call(
            functools.partial(row_sum_kernel, last),
            [VMEM] * (1 + len(pieces)),
            [((COLS, 8, LANE), F32) if last else msg],
            [],
            f"row_sum_{step}",
        )(fresh, *pieces)
        got = swap(whole, COL)
        solve = functools.partial(solve_kernel, first, last)
        if last:
            share = ((PIECE, SMP), F32)
            shares = call(
                solve,
                [SMEM] * 2 + [VMEM] * (4 + len(state)),
                [share, share],
                [],
                f"solve_{step}",
                jax.ShapeDtypeStruct,
            )(col_here, row_here, got, res, reg, *state, piece)
            return tuple(part.T for part in shares)
        inputs = [got, res, reg, *state, spread, fresh, *spread_img]
        outs = [field] * 3 + [((SMP, LANE), F32)] * 2 + [spread_share] * 2 + [own_share]
        res, *state, spread, img, own = call(
            solve, [SMEM] * 2 + [VMEM] * len(inputs), outs, [], f"solve_{step}"
        )(col_here, row_here, *inputs)
        spread_img = [img]


def solution(mesh):
    finer = Mesh(mesh.devices.reshape(8, 4, 8, 2), ROW_COL)
    placed = (
        P(None, ROW_COL),
        P(ROW_COL),
        P(ROW, None, COL, None, None),
        P(ROW, None, COL),
        P(ROW, None, COL),
        P(ROW, None, COL),
    )
    return jax.shard_map(
        body,
        mesh=finer,
        in_specs=placed,
        out_specs=(P(None, ROW_COL), P(None, ROW_COL)),
        check_vma=False,
    )
```

```python
import functools

import jax
import jax.numpy as jnp
from jax import lax
from jax.experimental import pallas as pl
from jax.experimental.pallas import tpu as pltpu
from jax.sharding import Mesh
from jax.sharding import PartitionSpec as P

ITERS = 3
COL = ("col_0", "col_1")
ROW = ("row_0", "row_1")
ROW_COL = ROW + COL
F32 = jnp.float32
BF16 = jnp.bfloat16
SMP = 64
LANE = 128
BLKS = 4
COLS = 16
PIECE = 32
STRIP = 8
OWN = 2 * STRIP
GRANT = 16 * 2**20
NOTES = 56
BATCHES = 4
NT = (((1,), (1,)), ((), ()))
NN = (((1,), (0,)), ((), ()))
VMEM = pl.BlockSpec(memory_space=pltpu.VMEM)
SMEM = pl.BlockSpec(memory_space=pltpu.SMEM)


def exact_dot(left, right, dims):
    return lax.dot_general(
        left, right, dims, precision=lax.Precision.HIGHEST, preferred_element_type=F32
    )


def close_dot(left, right):
    heads = [side.astype(BF16) for side in (left, right)]
    tails = [
        (side - head.astype(F32)).astype(BF16)
        for side, head in zip((left, right), heads, strict=True)
    ]

    def dot(a, b):
        return lax.dot_general(a, b, NN, preferred_element_type=F32)

    return dot(heads[0], heads[1]) + (dot(tails[0], heads[1]) + dot(heads[0], tails[1]))


def swap(msg, axes):
    return lax.all_to_all(msg, axes, 0, 0, tiled=True)


def call(kernel, in_specs, outs, scratch, name, make=pltpu.VMEM, near=True):
    run = pl.pallas_call(
        kernel,
        in_specs=in_specs,
        out_specs=[VMEM] * len(outs),
        out_shape=[make(s, d) for s, d in outs],
        scratch_shapes=scratch,
        compiler_params=pltpu.CompilerParams(vmem_limit_bytes=GRANT if near else None),
        name=name,
    )

    def placed(*args):
        if near:
            args = [
                pltpu.with_memory_space_constraint(arg, pltpu.VMEM) if spec is VMEM else arg
                for spec, arg in zip(in_specs, args, strict=True)
            ]
        return run(*args)

    return placed


def thirds(value):
    high = value.astype(BF16).astype(F32)
    middle = (value - high).astype(BF16).astype(F32)
    return high, middle, value - high - middle


def pack_share(right_ref, reg_ref, rows_ref, cols_ref, counts_ref, out_ref, base):
    right = right_ref[...].T
    packed = jnp.concatenate([right[16 * j : 16 * j + 16, :] for j in range(4)], axis=1)
    cols = cols_ref[...]
    place = ((cols // 2) * BLKS + rows_ref[...]) * 2 + cols % 2
    place = jnp.where(counts_ref[...] > 0, place, -1).astype(F32)
    lines = [*thirds(reg_ref[...]), place]
    lines.append(jnp.zeros((8 - len(lines), PIECE), F32))
    notes = jnp.concatenate(lines, axis=0)
    notes = jnp.concatenate([notes, jnp.zeros((8, LANE - PIECE), F32)], axis=1)
    tiles = [tile.astype(BF16) for tile in (*thirds(packed), notes)]
    for k in range(COLS):
        for i, tile in enumerate(tiles):
            out_ref[k, base + 16 * i : base + 16 * i + tile.shape[0], :] = tile


def pack_kernel(
    right_ref, reg_ref, rows_ref, cols_ref, counts_ref, far_ref, out_ref, curv_ref, done_ref
):
    sources = curv_ref.shape[0]
    base = STRIP * sources
    batch = sources // BATCHES
    loads = []
    for i in range(BATCHES):
        part = pl.ds(batch * i, batch)
        loads.append(pltpu.make_async_copy(far_ref.at[part], curv_ref.at[part], done_ref.at[i]))
        loads[i].start()
    pack_share(right_ref, reg_ref, rows_ref, cols_ref, counts_ref, out_ref, base)
    for s in range(sources):
        if s % batch == 0:
            loads[s // batch].wait()
        flipped = curv_ref[s].astype(F32).T
        for k in range(COLS):
            strip = flipped[STRIP * k : STRIP * k + STRIP, :].astype(BF16)
            out_ref[k, STRIP * s : STRIP * s + STRIP, :] = strip


def pixel_rows(fields):
    return [jnp.concatenate([fields[b].T, fields[2 + b].T], axis=1) for b in range(2)]


def own_kernel(place_ref, got_ref, own_ref, out_ref, tall_ref):
    base = got_ref.shape[1] - NOTES
    place = place_ref[0]
    strips = []
    for b in range(BLKS):
        parts = [
            got_ref[BLKS * b + place // 4, base + 16 * i : base + 16 * i + 16, :].astype(F32)
            for i in range(3)
        ]
        tall_ref[b] = (parts[0] + parts[1] + parts[2]).T
        start = STRIP * (place % 4)
        pieces = [
            tall_ref[b, pl.ds(pl.multiple_of(PIECE * j + start, STRIP), STRIP), :] for j in range(4)
        ]
        strips.append(jnp.concatenate(pieces, axis=1))
    for b in range(2):
        tile = jnp.concatenate([strips[b], strips[2 + b]], axis=1)
        own_ref[STRIP * b : STRIP * b + STRIP, :] = tile
        for r in range(out_ref.shape[0]):
            out_ref[r, STRIP * b : STRIP * b + STRIP, :] = tile


def unpack_kernel(place_ref, got_ref, res_ref, reg_ref, own_reg_ref, tall_ref):
    base = got_ref.shape[1] - NOTES
    packed, notes = [], []
    for k in range(COLS):
        parts = [got_ref[k, base + 16 * i : base + 16 * i + 16, :].astype(F32) for i in range(3)]
        packed.append(parts[0] + parts[1] + parts[2])
        note = got_ref[k, base + 48 : base + NOTES, :].astype(F32)
        notes.append(note[0:1] + note[1:2] + note[2:3])
    group = lax.broadcasted_iota(jnp.int32, (16, LANE), 1) // PIECE
    fields, regs = [], []
    for b in range(BLKS):
        pieces = []
        for j in range(4):
            piece = jnp.zeros((16, LANE), F32)
            for m in range(4):
                shift = (PIECE * (m - j)) % LANE
                part = packed[4 * b + m]
                part = pltpu.roll(part, shift, 1) if shift else part
                piece = jnp.where(group == m, part, piece)
            pieces.append(piece)
        fields.append(jnp.concatenate(pieces, axis=0))
        reg = jnp.zeros((8, LANE), F32)
        for m in range(4):
            part = jnp.broadcast_to(notes[4 * b + m], (8, LANE))
            part = pltpu.roll(part, PIECE * m, 1) if m else part
            reg = jnp.where(group[0:8] == m, part, reg)
        regs.append(jnp.broadcast_to(reg[0:1], (SMP, LANE)))
        res_ref[b] = fields[b]
        reg_ref[b] = reg
    start = pl.multiple_of(place_ref[0] * STRIP, STRIP)
    for b, tall in enumerate(pixel_rows(regs)):
        tall_ref[b] = tall
        own_reg_ref[STRIP * b : STRIP * b + STRIP, :] = tall_ref[b, pl.ds(start, STRIP), :]


def dense_kernel(place_ref, got_ref, high_ref, low_ref, sum_ref):
    sources = place_ref.shape[1]
    sum_ref[...] = jnp.zeros_like(sum_ref)
    for s in range(sources):
        for k in range(COLS):
            place = place_ref[k, s]
            strip = got_ref[k, STRIP * s : STRIP * s + STRIP, :].astype(F32)
            strip = jnp.where(place >= 0, strip, 0.0)
            spot = jnp.maximum(place, 0)
            plane = spot // 2
            rows = pl.ds(pl.multiple_of(OWN * s + STRIP * (spot % 2), STRIP), STRIP)
            sum_ref[plane, rows, :] = sum_ref[plane, rows, :] + strip
    for plane in range(2 * BLKS):
        total = sum_ref[plane]
        high = total.astype(BF16)
        high_ref[plane] = high
        low_ref[plane] = (total - high.astype(F32)).astype(BF16)


def flat(field_ref):
    return jnp.concatenate([field_ref[b] for b in range(BLKS)], axis=1)


def product_kernel(first, last, *refs):
    spread_ref, high_ref, low_ref, res_ref, reg_ref = refs[:5]
    if first:
        (out_ref,) = refs[5:]
    else:
        img_ref, dir_ref, out_ref = refs[5:]
    pixels = OWN * spread_ref.shape[0]
    spread = spread_ref[...].reshape(pixels, LANE)
    inputs = jnp.concatenate(
        [spread[LANE * i : LANE * i + LANE, :].T for i in range(pixels // LANE)], axis=1
    )
    top = inputs.astype(BF16)
    low = (inputs - top.astype(F32)).astype(BF16)
    coupled = []
    for b in range(BLKS):
        acc = jnp.zeros((SMP, LANE), F32)
        for half in range(2):
            cut = slice(SMP * half, SMP * half + SMP)
            plane = BLKS * half + b
            left = top[cut] if first else jnp.concatenate([top[cut], low[cut]], axis=0)
            main = lax.dot_general(left, high_ref[plane], NN, preferred_element_type=F32)
            acc += main if first else main[0:SMP] + main[SMP:]
            acc += lax.dot_general(top[cut], low_ref[plane], NN, preferred_element_type=F32)
        coupled.append(acc)
    share = 1.0 / COLS
    res = flat(res_ref)
    part = jnp.concatenate(
        [coupled[b] + reg_ref[b, 0:1, :] * res_ref[b] * share for b in range(BLKS)], axis=1
    )
    pair = exact_dot(res, jnp.concatenate([part, res * share], axis=0), NT)
    if first:
        mixed = jnp.zeros((SMP, SMP), F32)
    else:
        left = jnp.concatenate([res, part], axis=1)
        right = jnp.concatenate([flat(img_ref) * share, flat(dir_ref)], axis=1)
        mixed = exact_dot(left, right, NT)
    other = jnp.concatenate([mixed, jnp.zeros((SMP, LANE - SMP), F32)], axis=1)
    tall = [field.T for field in coupled] if last else pixel_rows(coupled)
    for k in range(COLS):
        if last:
            m = PIECE * (k % 4)
            near, far = tall[k // 4][m : m + 16], tall[k // 4][m + 16 : m + 32]
            out_ref[k, 0:OWN, :] = jnp.concatenate([near, far], axis=1)
        else:
            for b in range(2):
                strip = tall[b][STRIP * k : STRIP * k + STRIP]
                out_ref[k, STRIP * b : STRIP * b + STRIP, :] = strip
        source = pair if k < 8 else other
        n = k % 8
        out_ref[k, OWN : OWN + 8, :] = source[8 * n : 8 * n + 8, :]


def col_sum_kernel(last, got_ref, own_ref, own_reg_ref, out_ref, piece_ref):
    total = got_ref[0]
    for k in range(1, COLS):
        total = total + got_ref[k]
    coupled = total[0:OWN, :]
    piece_ref[...] = coupled
    gram = total[OWN : OWN + 8, :]
    full = coupled + own_reg_ref[...] * own_ref[...]
    for r in range(out_ref.shape[0]):
        if last:
            out_ref[r] = gram
        else:
            out_ref[r, 0:OWN, :] = full
            out_ref[r, OWN : OWN + 8, :] = gram


def row_sum_kernel(last, got_ref, *refs):
    top = got_ref.shape[1] - 8
    total = got_ref[0, top:, :]
    for r in range(1, got_ref.shape[0]):
        total = total + got_ref[r, top:, :]
    if last:
        (out_ref,) = refs
    else:
        piece_ref, out_ref = refs
        piece = piece_ref[...]
    for k in range(COLS):
        if last:
            out_ref[k] = total
        else:
            out_ref[k, 0:OWN, :] = piece
            out_ref[k, OWN : OWN + 8, :] = total


def solve_systems(systems, width):
    row_id = lax.broadcasted_iota(jnp.int32, (8, LANE), 0)
    work = []
    for matrix, rhs in systems:
        wide = jnp.concatenate([matrix, rhs], axis=1)
        work.append([wide[8 * t : 8 * t + 8, :] for t in range(8)])
    for j in range(0, SMP, width):
        top, low = divmod(j, 8)
        for tiles in work:
            columns = [
                [
                    jnp.broadcast_to(tile[:, j + i : j + i + 1], (8, LANE))
                    for i in range(width)
                ]
                for tile in tiles
            ]
            rows = [tiles[top][low + i : low + i + 1, :] for i in range(width)]
            block = [
                [columns[top][c][low + r : low + r + 1, :] for c in range(width)]
                for r in range(width)
            ]
            recip, lower = [], {}
            for a in range(width):
                recip.append(1.0 / block[a][a])
                for r in range(a + 1, width):
                    lower[r, a] = block[r][a] * recip[a]
                    rows[r] = rows[r] - lower[r, a] * rows[a]
                    for c in range(a + 1, width):
                        block[r][c] = block[r][c] - lower[r, a] * block[a][c]
            for a in reversed(range(width)):
                rows[a] = rows[a] * recip[a]
                for r in range(a + 1, width):
                    rows[a] = rows[a] - lower[r, a] * rows[r]
            for t in range(8):
                tile = tiles[t]
                for i in range(width):
                    tile = tile - columns[t][i] * rows[i]
                if t == top:
                    for i in range(width):
                        tile = jnp.where(row_id == low + i, rows[i], tile)
                tiles[t] = tile
    return [pltpu.roll(jnp.concatenate(tiles, axis=0), SMP, 1)[:, 0:SMP] for tiles in work]


def both_halves(matrix):
    zero = jnp.zeros((SMP, SMP), F32)
    upper = jnp.concatenate([matrix, zero], axis=1)
    lower = jnp.concatenate([zero, matrix], axis=1)
    return jnp.concatenate([upper, lower], axis=0)


def solve_kernel(first, last, *refs):
    refs = list(refs)
    col_ref, row_ref, got_ref, res_ref, reg_ref = refs[:5]
    refs = refs[5:]
    mine = col_ref[0] // 4
    if not first:
        dir_ref, img_ref, sol_ref, inv_ref, curv_ref = refs[:5]
        refs = refs[5:]
    if last:
        piece_ref, out_sol_ref, out_res_ref = refs
    else:
        spread_ref, fresh_ref = refs[:2]
        refs = refs[2:]
        if not first:
            spread_img_ref = refs.pop(0)
        new_res_ref, new_dir_ref, new_img_ref, new_sol_ref = refs[:4]
        new_inv_ref, new_curv_ref, new_spread_ref, new_spread_img_ref, own_ref = refs[4:]
    base = got_ref.shape[1] - 8
    pair = jnp.concatenate([got_ref[k, base:, :] for k in range(8)], axis=0)
    gram = pltpu.roll(pair, SMP, 1)[:, 0:SMP]
    curv = pair[:, 0:SMP]
    if not first:
        mixed = jnp.concatenate([got_ref[k, base:, :] for k in range(8, 16)], axis=0)
        mixed = mixed[:, 0:SMP]
        beta_t = exact_dot(gram, inv_ref[...], NN)
        curv = curv + exact_dot(mixed + exact_dot(beta_t, curv_ref[...], NN), beta_t, NT)
    curv = 0.5 * (curv + curv.T)
    if last:
        (alpha,) = solve_systems([(curv, gram)], 8)
    else:
        square = (SMP, SMP)
        same = lax.broadcasted_iota(jnp.int32, square, 0) == lax.broadcasted_iota(
            jnp.int32, square, 1
        )
        alpha, inverse = solve_systems([(curv, gram), (gram, same.astype(F32))], 8)
        new_inv_ref[...] = inverse
        new_curv_ref[...] = curv
        sources = spread_ref.shape[0]
        pixels = OWN * sources
        spread_img = fresh_ref[:, 0:OWN, :].reshape(pixels, LANE)
        if not first:
            old = spread_img_ref[...].reshape(pixels, LANE)
            spread_img = spread_img + close_dot(old, both_halves(beta_t.T))
        spread = spread_ref[...].reshape(pixels, LANE)
        spread = spread - close_dot(spread_img, both_halves(alpha))
        new_spread_ref[...] = spread.reshape(sources, OWN, LANE)
        new_spread_img_ref[...] = spread_img.reshape(sources, OWN, LANE)
        own_ref[...] = new_spread_ref[row_ref[0]]
    if last:
        shift = (LANE - PIECE * (col_ref[0] % 4)) % LANE

        def cut(rows):
            return pltpu.roll(rows, shift, 1)[:, 0:PIECE].T

        res = cut(res_ref[mine])
        reg = cut(jnp.broadcast_to(reg_ref[mine][0:1, :], (SMP, LANE)))
        piece = piece_ref[...]
        halves = [piece[:, 0:SMP], pltpu.roll(piece, SMP, 1)[:, 0:SMP]]
        image = jnp.concatenate(halves, axis=0) + reg * res
        image = image + exact_dot(cut(img_ref[mine]), beta_t, NT)
        direction = res + exact_dot(cut(dir_ref[mine]), beta_t, NT)
        out_sol_ref[...] = cut(sol_ref[...]) + exact_dot(direction, alpha, NN)
        out_res_ref[...] = res - exact_dot(image, alpha, NN)
        return
    alpha_t = alpha.T
    wide = [
        jnp.concatenate(
            [got_ref[k, STRIP * b : STRIP * b + STRIP, :] for k in range(COLS)], axis=0
        ).T
        for b in range(2)
    ]
    res = flat(res_ref)
    direction = res
    image = jnp.concatenate(
        [
            wide[b % 2][SMP * (b // 2) : SMP * (b // 2) + SMP, :] + reg_ref[b, 0:1, :] * res_ref[b]
            for b in range(BLKS)
        ],
        axis=1,
    )
    if not first:
        image = image + exact_dot(beta_t, flat(img_ref), NN)
        direction = direction + exact_dot(beta_t, flat(dir_ref), NN)
    new_res = res - exact_dot(alpha_t, image, NN)
    for b in range(BLKS):
        part = slice(LANE * b, LANE * b + LANE)
        new_res_ref[b] = new_res[:, part]
        new_img_ref[b] = image[:, part]
        new_dir_ref[b] = direction[:, part]
    new_sol = exact_dot(alpha_t, new_dir_ref[mine], NN)
    new_sol_ref[...] = new_sol if first else sol_ref[...] + new_sol


def body(right_side, regular, curvature, block_rows, block_cols, block_counts):
    sources = block_rows.shape[1]
    pixels = OWN * sources
    curv = curvature.reshape(sources, LANE, LANE)
    tables = [table.reshape(1, sources) for table in (block_rows, block_cols, block_counts)]
    field = ((BLKS, SMP, LANE), F32)
    own_share = ((OWN, LANE), F32)
    spread_share = ((sources, OWN, LANE), F32)
    msg = ((COLS, OWN + 8, LANE), F32)
    start = ((COLS, STRIP * sources + NOTES, LANE), BF16)
    dense = ((2 * BLKS, pixels, LANE), BF16)

    loaded = [pltpu.VMEM((sources, LANE, LANE), BF16), pltpu.SemaphoreType.DMA((BATCHES,))]
    far = pl.BlockSpec(memory_space=pltpu.HBM)
    (packed,) = call(pack_kernel, [VMEM] * 5 + [far], [start], loaded, "pack", near=False)(
        right_side.T, regular.reshape(1, PIECE), *tables, curv
    )
    col_here = lax.axis_index(COL).astype(jnp.int32).reshape(1)
    row_here = lax.axis_index(ROW).astype(jnp.int32).reshape(1)
    packed, col_here, row_here = lax.optimization_barrier((packed, col_here, row_here))
    packed = swap(packed, COL)
    own, out = call(
        own_kernel,
        [SMEM, VMEM],
        [own_share, spread_share],
        [pltpu.VMEM((BLKS, LANE, 16), F32)],
        "own",
    )(col_here, packed)
    res, reg, own_reg = call(
        unpack_kernel,
        [SMEM, VMEM],
        [field, ((BLKS, 8, LANE), F32), own_share],
        [pltpu.VMEM((2, LANE, LANE), F32)],
        "unpack",
    )(col_here, packed)
    spread = swap(out, ROW)
    places = packed[:, STRIP * sources + 51, 0:sources].astype(jnp.int32)
    high, low = call(
        dense_kernel,
        [SMEM, VMEM],
        [dense, dense],
        [pltpu.VMEM(dense[0], F32)],
        "dense",
    )(places, packed)
    state, spread_img = [], []
    for step in range(ITERS):
        first, last = step == 0, step == ITERS - 1
        before = [] if first else [state[1], state[0]]
        (part,) = call(
            functools.partial(product_kernel, first, last),
            [VMEM] * (5 + len(before)),
            [msg],
            [],
            f"product_{step}",
        )(spread, high, low, res, reg, *before)
        out, piece = call(
            functools.partial(col_sum_kernel, last),
            [VMEM] * 3,
            [((sources, 8 if last else OWN + 8, LANE), F32), own_share],
            [],
            f"col_sum_{step}",
        )(swap(part, COL), own, own_reg)
        fresh = swap(out, ROW)
        pieces = [] if last else [piece]
        (whole,) = call(
            functools.partial(row_sum_kernel, last),
            [VMEM] * (1 + len(pieces)),
            [((COLS, 8, LANE), F32) if last else msg],
            [],
            f"row_sum_{step}",
        )(fresh, *pieces)
        got = swap(whole, COL)
        solve = functools.partial(solve_kernel, first, last)
        if last:
            share = ((PIECE, SMP), F32)
            shares = call(
                solve,
                [SMEM] * 2 + [VMEM] * (4 + len(state)),
                [share, share],
                [],
                f"solve_{step}",
                jax.ShapeDtypeStruct,
            )(col_here, row_here, got, res, reg, *state, piece)
            return tuple(part.T for part in shares)
        inputs = [got, res, reg, *state, spread, fresh, *spread_img]
        outs = [field] * 3 + [((SMP, LANE), F32)] + [((SMP, SMP), F32)] * 2 + [spread_share] * 2 + [own_share]
        res, *state, spread, img, own = call(
            solve, [SMEM] * 2 + [VMEM] * len(inputs), outs, [], f"solve_{step}"
        )(col_here, row_here, *inputs)
        spread_img = [img]


def solution(mesh):
    finer = Mesh(mesh.devices.reshape(8, 4, 8, 2), ROW_COL)
    placed = (
        P(None, ROW_COL),
        P(ROW_COL),
        P(ROW, None, COL, None, None),
        P(ROW, None, COL),
        P(ROW, None, COL),
        P(ROW, None, COL),
    )
    return jax.shard_map(
        body,
        mesh=finer,
        in_specs=placed,
        out_specs=(P(None, ROW_COL), P(None, ROW_COL)),
        check_vma=False,
    )
```

```python
import functools

import jax
import jax.numpy as jnp
from jax import lax
from jax.experimental import pallas as pl
from jax.experimental.pallas import tpu as pltpu
from jax.sharding import Mesh
from jax.sharding import PartitionSpec as P

ITERS = 3
COL = ("col_0", "col_1")
ROW = ("row_0", "row_1")
ROW_COL = ROW + COL
F32 = jnp.float32
BF16 = jnp.bfloat16
SMP = 64
LANE = 128
BLKS = 4
COLS = 16
PIECE = 32
STRIP = 8
OWN = 2 * STRIP
GRANT = 16 * 2**20
NOTES = 56
NT = (((1,), (1,)), ((), ()))
NN = (((1,), (0,)), ((), ()))
VMEM = pl.BlockSpec(memory_space=pltpu.VMEM)
SMEM = pl.BlockSpec(memory_space=pltpu.SMEM)


def exact_dot(left, right, dims):
    return lax.dot_general(
        left, right, dims, precision=lax.Precision.HIGHEST, preferred_element_type=F32
    )


def close_dot(left, right):
    heads = [side.astype(BF16) for side in (left, right)]
    tails = [
        (side - head.astype(F32)).astype(BF16)
        for side, head in zip((left, right), heads, strict=True)
    ]

    def dot(a, b):
        return lax.dot_general(a, b, NN, preferred_element_type=F32)

    return dot(heads[0], heads[1]) + (dot(tails[0], heads[1]) + dot(heads[0], tails[1]))


def swap(msg, axes):
    return lax.all_to_all(msg, axes, 0, 0, tiled=True)


def call(kernel, in_specs, outs, scratch, name, make=pltpu.VMEM, near=True):
    run = pl.pallas_call(
        kernel,
        in_specs=in_specs,
        out_specs=[VMEM] * len(outs),
        out_shape=[make(s, d) for s, d in outs],
        scratch_shapes=scratch,
        compiler_params=pltpu.CompilerParams(vmem_limit_bytes=GRANT if near else None),
        name=name,
    )

    def placed(*args):
        if near:
            args = [
                pltpu.with_memory_space_constraint(arg, pltpu.VMEM) if spec is VMEM else arg
                for spec, arg in zip(in_specs, args, strict=True)
            ]
        return run(*args)

    return placed


def thirds(value):
    high = value.astype(BF16).astype(F32)
    middle = (value - high).astype(BF16).astype(F32)
    return high, middle, value - high - middle


def pack_kernel(right_ref, reg_ref, rows_ref, cols_ref, counts_ref, curv_ref, out_ref):
    sources = curv_ref.shape[0]
    base = STRIP * sources
    for s in range(sources):
        flipped = curv_ref[s].astype(F32).T
        for k in range(COLS):
            strip = flipped[STRIP * k : STRIP * k + STRIP, :].astype(BF16)
            out_ref[k, STRIP * s : STRIP * s + STRIP, :] = strip
    right = right_ref[...].T
    packed = jnp.concatenate([right[16 * j : 16 * j + 16, :] for j in range(4)], axis=1)
    cols = cols_ref[...]
    place = ((cols // 2) * BLKS + rows_ref[...]) * 2 + cols % 2
    place = jnp.where(counts_ref[...] > 0, place, -1).astype(F32)
    lines = [*thirds(reg_ref[...]), place]
    lines.append(jnp.zeros((8 - len(lines), PIECE), F32))
    notes = jnp.concatenate(lines, axis=0)
    notes = jnp.concatenate([notes, jnp.zeros((8, LANE - PIECE), F32)], axis=1)
    tiles = [tile.astype(BF16) for tile in (*thirds(packed), notes)]
    for k in range(COLS):
        for i, tile in enumerate(tiles):
            out_ref[k, base + 16 * i : base + 16 * i + tile.shape[0], :] = tile


def pixel_rows(fields):
    return [jnp.concatenate([fields[b].T, fields[2 + b].T], axis=1) for b in range(2)]


def own_kernel(place_ref, got_ref, own_ref, out_ref, tall_ref):
    base = got_ref.shape[1] - NOTES
    place = place_ref[0]
    strips = []
    for b in range(BLKS):
        parts = [
            got_ref[BLKS * b + place // 4, base + 16 * i : base + 16 * i + 16, :].astype(F32)
            for i in range(3)
        ]
        tall_ref[b] = (parts[0] + parts[1] + parts[2]).T
        start = STRIP * (place % 4)
        pieces = [
            tall_ref[b, pl.ds(pl.multiple_of(PIECE * j + start, STRIP), STRIP), :] for j in range(4)
        ]
        strips.append(jnp.concatenate(pieces, axis=1))
    for b in range(2):
        tile = jnp.concatenate([strips[b], strips[2 + b]], axis=1)
        own_ref[STRIP * b : STRIP * b + STRIP, :] = tile
        for r in range(out_ref.shape[0]):
            out_ref[r, STRIP * b : STRIP * b + STRIP, :] = tile


def unpack_kernel(place_ref, got_ref, res_ref, reg_ref, own_reg_ref, tall_ref):
    base = got_ref.shape[1] - NOTES
    packed, notes = [], []
    for k in range(COLS):
        parts = [got_ref[k, base + 16 * i : base + 16 * i + 16, :].astype(F32) for i in range(3)]
        packed.append(parts[0] + parts[1] + parts[2])
        note = got_ref[k, base + 48 : base + NOTES, :].astype(F32)
        notes.append(note[0:1] + note[1:2] + note[2:3])
    group = lax.broadcasted_iota(jnp.int32, (16, LANE), 1) // PIECE
    fields, regs = [], []
    for b in range(BLKS):
        pieces = []
        for j in range(4):
            piece = jnp.zeros((16, LANE), F32)
            for m in range(4):
                shift = (PIECE * (m - j)) % LANE
                part = packed[4 * b + m]
                part = pltpu.roll(part, shift, 1) if shift else part
                piece = jnp.where(group == m, part, piece)
            pieces.append(piece)
        fields.append(jnp.concatenate(pieces, axis=0))
        reg = jnp.zeros((8, LANE), F32)
        for m in range(4):
            part = jnp.broadcast_to(notes[4 * b + m], (8, LANE))
            part = pltpu.roll(part, PIECE * m, 1) if m else part
            reg = jnp.where(group[0:8] == m, part, reg)
        regs.append(jnp.broadcast_to(reg[0:1], (SMP, LANE)))
        res_ref[b] = fields[b]
        reg_ref[b] = reg
    start = pl.multiple_of(place_ref[0] * STRIP, STRIP)
    for b, tall in enumerate(pixel_rows(regs)):
        tall_ref[b] = tall
        own_reg_ref[STRIP * b : STRIP * b + STRIP, :] = tall_ref[b, pl.ds(start, STRIP), :]


def dense_kernel(place_ref, got_ref, high_ref, low_ref, sum_ref):
    sources = place_ref.shape[1]
    sum_ref[...] = jnp.zeros_like(sum_ref)
    for s in range(sources):
        for k in range(COLS):
            place = place_ref[k, s]
            strip = got_ref[k, STRIP * s : STRIP * s + STRIP, :].astype(F32)
            strip = jnp.where(place >= 0, strip, 0.0)
            spot = jnp.maximum(place, 0)
            plane = spot // 2
            rows = pl.ds(pl.multiple_of(OWN * s + STRIP * (spot % 2), STRIP), STRIP)
            sum_ref[plane, rows, :] = sum_ref[plane, rows, :] + strip
    for plane in range(2 * BLKS):
        total = sum_ref[plane]
        high = total.astype(BF16)
        high_ref[plane] = high
        low_ref[plane] = (total - high.astype(F32)).astype(BF16)


def flat(field_ref):
    return jnp.concatenate([field_ref[b] for b in range(BLKS)], axis=1)


def product_kernel(first, last, *refs):
    spread_ref, high_ref, low_ref, res_ref, reg_ref = refs[:5]
    if first:
        (out_ref,) = refs[5:]
    else:
        img_ref, dir_ref, out_ref = refs[5:]
    pixels = OWN * spread_ref.shape[0]
    spread = spread_ref[...].reshape(pixels, LANE)
    inputs = jnp.concatenate(
        [spread[LANE * i : LANE * i + LANE, :].T for i in range(pixels // LANE)], axis=1
    )
    top = inputs.astype(BF16)
    low = (inputs - top.astype(F32)).astype(BF16)
    coupled = []
    for b in range(BLKS):
        acc = jnp.zeros((SMP, LANE), F32)
        for half in range(2):
            cut = slice(SMP * half, SMP * half + SMP)
            plane = BLKS * half + b
            left = top[cut] if first else jnp.concatenate([top[cut], low[cut]], axis=0)
            main = lax.dot_general(left, high_ref[plane], NN, preferred_element_type=F32)
            acc += main if first else main[0:SMP] + main[SMP:]
            acc += lax.dot_general(top[cut], low_ref[plane], NN, preferred_element_type=F32)
        coupled.append(acc)
    share = 1.0 / COLS
    res = flat(res_ref)
    part = jnp.concatenate(
        [coupled[b] + reg_ref[b, 0:1, :] * res_ref[b] * share for b in range(BLKS)], axis=1
    )
    pair = exact_dot(res, jnp.concatenate([part, res * share], axis=0), NT)
    if first:
        mixed = jnp.zeros((SMP, SMP), F32)
    else:
        left = jnp.concatenate([res, part], axis=1)
        right = jnp.concatenate([flat(img_ref) * share, flat(dir_ref)], axis=1)
        mixed = exact_dot(left, right, NT)
    other = jnp.concatenate([mixed, jnp.zeros((SMP, LANE - SMP), F32)], axis=1)
    tall = [field.T for field in coupled] if last else pixel_rows(coupled)
    for k in range(COLS):
        if last:
            m = PIECE * (k % 4)
            near, far = tall[k // 4][m : m + 16], tall[k // 4][m + 16 : m + 32]
            out_ref[k, 0:OWN, :] = jnp.concatenate([near, far], axis=1)
        else:
            for b in range(2):
                strip = tall[b][STRIP * k : STRIP * k + STRIP]
                out_ref[k, STRIP * b : STRIP * b + STRIP, :] = strip
        source = pair if k < 8 else other
        n = k % 8
        out_ref[k, OWN : OWN + 8, :] = source[8 * n : 8 * n + 8, :]


def col_sum_kernel(last, got_ref, own_ref, own_reg_ref, out_ref, piece_ref):
    total = got_ref[0]
    for k in range(1, COLS):
        total = total + got_ref[k]
    coupled = total[0:OWN, :]
    piece_ref[...] = coupled
    gram = total[OWN : OWN + 8, :]
    full = coupled + own_reg_ref[...] * own_ref[...]
    for r in range(out_ref.shape[0]):
        if last:
            out_ref[r] = gram
        else:
            out_ref[r, 0:OWN, :] = full
            out_ref[r, OWN : OWN + 8, :] = gram


def row_sum_kernel(last, got_ref, *refs):
    top = got_ref.shape[1] - 8
    total = got_ref[0, top:, :]
    for r in range(1, got_ref.shape[0]):
        total = total + got_ref[r, top:, :]
    if last:
        (out_ref,) = refs
    else:
        piece_ref, out_ref = refs
        piece = piece_ref[...]
    for k in range(COLS):
        if last:
            out_ref[k] = total
        else:
            out_ref[k, 0:OWN, :] = piece
            out_ref[k, OWN : OWN + 8, :] = total


def solve_systems(systems, width):
    row_id = lax.broadcasted_iota(jnp.int32, (8, LANE), 0)
    work = []
    for matrix, rhs in systems:
        wide = jnp.concatenate([matrix, rhs], axis=1)
        work.append([wide[8 * t : 8 * t + 8, :] for t in range(8)])
    for j in range(0, SMP, width):
        top, low = divmod(j, 8)
        for tiles in work:
            columns = [
                [
                    jnp.broadcast_to(tile[:, j + i : j + i + 1], (8, LANE))
                    for i in range(width)
                ]
                for tile in tiles
            ]
            rows = [tiles[top][low + i : low + i + 1, :] for i in range(width)]
            block = [
                [columns[top][c][low + r : low + r + 1, :] for c in range(width)]
                for r in range(width)
            ]
            recip, lower = [], {}
            for a in range(width):
                recip.append(1.0 / block[a][a])
                for r in range(a + 1, width):
                    lower[r, a] = block[r][a] * recip[a]
                    rows[r] = rows[r] - lower[r, a] * rows[a]
                    for c in range(a + 1, width):
                        block[r][c] = block[r][c] - lower[r, a] * block[a][c]
            for a in reversed(range(width)):
                rows[a] = rows[a] * recip[a]
                for r in range(a + 1, width):
                    rows[a] = rows[a] - lower[r, a] * rows[r]
            for t in range(8):
                tile = tiles[t]
                for i in range(width):
                    tile = tile - columns[t][i] * rows[i]
                if t == top:
                    for i in range(width):
                        tile = jnp.where(row_id == low + i, rows[i], tile)
                tiles[t] = tile
    return [pltpu.roll(jnp.concatenate(tiles, axis=0), SMP, 1)[:, 0:SMP] for tiles in work]


def both_halves(matrix):
    zero = jnp.zeros((SMP, SMP), F32)
    upper = jnp.concatenate([matrix, zero], axis=1)
    lower = jnp.concatenate([zero, matrix], axis=1)
    return jnp.concatenate([upper, lower], axis=0)


def solve_kernel(first, last, *refs):
    refs = list(refs)
    col_ref, row_ref, got_ref, res_ref, reg_ref = refs[:5]
    refs = refs[5:]
    mine = col_ref[0] // 4
    if not first:
        dir_ref, img_ref, sol_ref, inv_ref, curv_ref = refs[:5]
        refs = refs[5:]
    if last:
        piece_ref, out_sol_ref, out_res_ref = refs
    else:
        spread_ref, fresh_ref = refs[:2]
        refs = refs[2:]
        if not first:
            spread_img_ref = refs.pop(0)
        new_res_ref, new_dir_ref, new_img_ref, new_sol_ref = refs[:4]
        new_inv_ref, new_curv_ref, new_spread_ref, new_spread_img_ref, own_ref = refs[4:]
    base = got_ref.shape[1] - 8
    pair = jnp.concatenate([got_ref[k, base:, :] for k in range(8)], axis=0)
    gram = pltpu.roll(pair, SMP, 1)[:, 0:SMP]
    curv = pair[:, 0:SMP]
    if not first:
        mixed = jnp.concatenate([got_ref[k, base:, :] for k in range(8, 16)], axis=0)
        mixed = mixed[:, 0:SMP]
        beta_t = exact_dot(gram, inv_ref[...], NN)
        curv = curv + exact_dot(mixed + exact_dot(beta_t, curv_ref[...], NN), beta_t, NT)
    curv = 0.5 * (curv + curv.T)
    if last:
        (alpha,) = solve_systems([(curv, gram)], 8)
    else:
        square = (SMP, SMP)
        same = lax.broadcasted_iota(jnp.int32, square, 0) == lax.broadcasted_iota(
            jnp.int32, square, 1
        )
        alpha, inverse = solve_systems([(curv, gram), (gram, same.astype(F32))], 8)
        new_inv_ref[...] = inverse
        new_curv_ref[...] = curv
        sources = spread_ref.shape[0]
        pixels = OWN * sources
        spread_img = fresh_ref[:, 0:OWN, :].reshape(pixels, LANE)
        if not first:
            old = spread_img_ref[...].reshape(pixels, LANE)
            spread_img = spread_img + close_dot(old, both_halves(beta_t.T))
        spread = spread_ref[...].reshape(pixels, LANE)
        spread = spread - close_dot(spread_img, both_halves(alpha))
        new_spread_ref[...] = spread.reshape(sources, OWN, LANE)
        new_spread_img_ref[...] = spread_img.reshape(sources, OWN, LANE)
        own_ref[...] = new_spread_ref[row_ref[0]]
    if last:
        shift = (LANE - PIECE * (col_ref[0] % 4)) % LANE

        def cut(rows):
            return pltpu.roll(rows, shift, 1)[:, 0:PIECE].T

        res = cut(res_ref[mine])
        reg = cut(jnp.broadcast_to(reg_ref[mine][0:1, :], (SMP, LANE)))
        piece = piece_ref[...]
        halves = [piece[:, 0:SMP], pltpu.roll(piece, SMP, 1)[:, 0:SMP]]
        image = jnp.concatenate(halves, axis=0) + reg * res
        image = image + exact_dot(cut(img_ref[mine]), beta_t, NT)
        direction = res + exact_dot(cut(dir_ref[mine]), beta_t, NT)
        out_sol_ref[...] = cut(sol_ref[...]) + exact_dot(direction, alpha, NN)
        out_res_ref[...] = res - exact_dot(image, alpha, NN)
        return
    alpha_t = alpha.T
    wide = [
        jnp.concatenate(
            [got_ref[k, STRIP * b : STRIP * b + STRIP, :] for k in range(COLS)], axis=0
        ).T
        for b in range(2)
    ]
    res = flat(res_ref)
    direction = res
    image = jnp.concatenate(
        [
            wide[b % 2][SMP * (b // 2) : SMP * (b // 2) + SMP, :] + reg_ref[b, 0:1, :] * res_ref[b]
            for b in range(BLKS)
        ],
        axis=1,
    )
    if not first:
        image = image + exact_dot(beta_t, flat(img_ref), NN)
        direction = direction + exact_dot(beta_t, flat(dir_ref), NN)
    new_res = res - exact_dot(alpha_t, image, NN)
    for b in range(BLKS):
        part = slice(LANE * b, LANE * b + LANE)
        new_res_ref[b] = new_res[:, part]
        new_img_ref[b] = image[:, part]
        new_dir_ref[b] = direction[:, part]
    new_sol = exact_dot(alpha_t, new_dir_ref[mine], NN)
    new_sol_ref[...] = new_sol if first else sol_ref[...] + new_sol


def body(right_side, regular, curvature, block_rows, block_cols, block_counts):
    sources = block_rows.shape[1]
    pixels = OWN * sources
    curv = curvature.reshape(sources, LANE, LANE)
    tables = [table.reshape(1, sources) for table in (block_rows, block_cols, block_counts)]
    field = ((BLKS, SMP, LANE), F32)
    own_share = ((OWN, LANE), F32)
    spread_share = ((sources, OWN, LANE), F32)
    msg = ((COLS, OWN + 8, LANE), F32)
    start = ((COLS, STRIP * sources + NOTES, LANE), BF16)
    dense = ((2 * BLKS, pixels, LANE), BF16)

    (packed,) = call(pack_kernel, [VMEM] * 6, [start], [], "pack", near=False)(
        right_side.T, regular.reshape(1, PIECE), *tables, curv
    )
    col_here = lax.axis_index(COL).astype(jnp.int32).reshape(1)
    row_here = lax.axis_index(ROW).astype(jnp.int32).reshape(1)
    packed, col_here, row_here = lax.optimization_barrier((packed, col_here, row_here))
    packed = swap(packed, COL)
    own, out = call(
        own_kernel,
        [SMEM, VMEM],
        [own_share, spread_share],
        [pltpu.VMEM((BLKS, LANE, 16), F32)],
        "own",
    )(col_here, packed)
    res, reg, own_reg = call(
        unpack_kernel,
        [SMEM, VMEM],
        [field, ((BLKS, 8, LANE), F32), own_share],
        [pltpu.VMEM((2, LANE, LANE), F32)],
        "unpack",
    )(col_here, packed)
    spread = swap(out, ROW)
    places = packed[:, STRIP * sources + 51, 0:sources].astype(jnp.int32)
    high, low = call(
        dense_kernel,
        [SMEM, VMEM],
        [dense, dense],
        [pltpu.VMEM(dense[0], F32)],
        "dense",
    )(places, packed)
    state, spread_img = [], []
    for step in range(ITERS):
        first, last = step == 0, step == ITERS - 1
        before = [] if first else [state[1], state[0]]
        (part,) = call(
            functools.partial(product_kernel, first, last),
            [VMEM] * (5 + len(before)),
            [msg],
            [],
            f"product_{step}",
        )(spread, high, low, res, reg, *before)
        out, piece = call(
            functools.partial(col_sum_kernel, last),
            [VMEM] * 3,
            [((sources, 8 if last else OWN + 8, LANE), F32), own_share],
            [],
            f"col_sum_{step}",
        )(swap(part, COL), own, own_reg)
        fresh = swap(out, ROW)
        pieces = [] if last else [piece]
        (whole,) = call(
            functools.partial(row_sum_kernel, last),
            [VMEM] * (1 + len(pieces)),
            [((COLS, 8, LANE), F32) if last else msg],
            [],
            f"row_sum_{step}",
        )(fresh, *pieces)
        got = swap(whole, COL)
        solve = functools.partial(solve_kernel, first, last)
        if last:
            share = ((PIECE, SMP), F32)
            shares = call(
                solve,
                [SMEM] * 2 + [VMEM] * (4 + len(state)),
                [share, share],
                [],
                f"solve_{step}",
                jax.ShapeDtypeStruct,
            )(col_here, row_here, got, res, reg, *state, piece)
            return tuple(part.T for part in shares)
        inputs = [got, res, reg, *state, spread, fresh, *spread_img]
        outs = [field] * 3 + [((SMP, LANE), F32)] + [((SMP, SMP), F32)] * 2 + [spread_share] * 2 + [own_share]
        res, *state, spread, img, own = call(
            solve, [SMEM] * 2 + [VMEM] * len(inputs), outs, [], f"solve_{step}"
        )(col_here, row_here, *inputs)
        spread_img = [img]


def solution(mesh):
    finer = Mesh(mesh.devices.reshape(8, 4, 8, 2), ROW_COL)
    placed = (
        P(None, ROW_COL),
        P(ROW_COL),
        P(ROW, None, COL, None, None),
        P(ROW, None, COL),
        P(ROW, None, COL),
        P(ROW, None, COL),
    )
    return jax.shard_map(
        body,
        mesh=finer,
        in_specs=placed,
        out_specs=(P(None, ROW_COL), P(None, ROW_COL)),
        check_vma=False,
    )
```
